32 devices in a mesh: dp: 16 (over z, y, x), rep: 2 (over core).
Axes of the slice: x: 2, y: 2, z: 4, core: 2. Of those that a mesh axis runs over, the one named last changes fastest.
Arguments:
- tokens: bfloat16 [2, 16384, 768], P(None, ('dp', 'rep')), may hold values from -6 to 6
- doc_lengths: int32 [2, 32, 6], P(None, ('dp', 'rep')), may hold values from 1 to 256, 512 in all within a row
- cotangent: bfloat16 [2, 16384, 768], P(None, ('dp', 'rep')), may hold values from -6 to 6
- attn_gain: bfloat16 [768], P('dp'), may hold values from 0.5 to 1.5
- attn_shift: bfloat16 [768], P('dp'), may hold values from -1 to 1
- qkv_weight: bfloat16 [768, 2304], P('dp'), may hold values from -0.21875 to 0.21875
- qkv_bias: bfloat16 [2304], P('dp'), may hold values from -1 to 1
- out_weight: bfloat16 [768, 768], P('dp'), may hold values from -0.625 to 0.625
- out_bias: bfloat16 [768], P('dp'), may hold values from -1 to 1
- mlp_gain: bfloat16 [768], P('dp'), may hold values from 0.5 to 1.5
- mlp_shift: bfloat16 [768], P('dp'), may hold values from -1 to 1
- fc_weight: bfloat16 [768, 3072], P('dp'), may hold values from -0.21875 to 0.21875
- fc_bias: bfloat16 [3072], P('dp'), may hold values from -1 to 1
- proj_weight: bfloat16 [3072, 768], P('dp'), may hold values from -0.15625 to 0.15625
- proj_bias: bfloat16 [768], P('dp'), may hold values from -1 to 1
Outputs:
- activations: bfloat16 [2, 16384, 768], P(None, ('dp', 'rep'))
- input_grad: bfloat16 [2, 16384, 768], P(None, ('dp', 'rep'))
- grad_attn_gain: float32 [768], P('dp')
- grad_attn_shift: float32 [768], P('dp')
- grad_qkv_weight: float32 [768, 2304], P('dp')
- grad_qkv_bias: float32 [2304], P('dp')
- grad_out_weight: float32 [768, 768], P('dp')
- grad_out_bias: float32 [768], P('dp')
- grad_mlp_gain: float32 [768], P('dp')
- grad_mlp_shift: float32 [768], P('dp')
- grad_fc_weight: float32 [768, 3072], P('dp')
- grad_fc_bias: float32 [3072], P('dp')
- grad_proj_weight: float32 [3072, 768], P('dp')
- grad_proj_bias: float32 [768], P('dp')
The draws below stay inside these ranges and needn't reach their ends.
Inputs may be any that keep to these rules, and one draw needn't show every extreme that they name: `doc_lengths`: each row of 6 lengths sums to 512, and its largest is 256.
All inputs are finite; a program needn't handle non-finite values.
Results may differ from the reference program's by a relative error of at most 0.015.
Values may be sent and summed in bfloat16 or wider, within the bound.
No kernel may reach another device: no remote copies, remote signals or barrier semaphores. Data moves between devices by JAX's collectives and lax.ppermute only.
A program may use at most 320 MiB of HBM per device.

```python
import math
import jax
import jax.numpy as jnp
import numpy as np
from jax import lax

D = 768
H = 12
HD = 64
FF = 3072
TOK_MB = 512
MICRO = 2
USES = 2
DOCS = 6
LONGEST = 256
ROWS = 16384
N_DP = 16
N_REP = 2


def spiked(array, own_key, source, target, blocks, factor):
    owner, partner = [(jnp.arange(array.shape[dim]) // (array.shape[dim] // blocks)).reshape([-1 if axis == dim else 1 for axis in range(array.ndim)]) for dim in (source, target)]
    chosen = jax.random.permutation(own_key, blocks)[partner]
    strong = (owner == chosen) | (owner == (partner + blocks // 2) % blocks)
    return jnp.where(strong, factor * array, array)


def block_levels(own_key, shape, pieces, low, high):
    loudness = 1.0
    for position, shards_of in pieces:
        steps = jax.random.uniform(jax.random.fold_in(jax.random.fold_in(own_key, 6), position), (shards_of,), jnp.float32, low / len(pieces), high / len(pieces))
        loudness = loudness * jnp.repeat(jnp.exp(steps), shape[position] // shards_of).reshape((-1,) + (1,) * (len(shape) - 1 - position))
    return loudness


def profile(count, total, most, skew):
    portions = [(1 << 20) // math.isqrt(standing ** skew) + 1 for standing in range(2, count + 1)]
    surplus, given = total - most - (count - 1), [1] * (count - 1)
    while surplus > 0:
        free = [i for i in range(count - 1) if given[i] < most]
        whole, remaining = sum([portions[i] for i in free]), surplus
        for i in free:
            more = min(most - given[i], max(1, remaining * portions[i] // whole), surplus)
            given[i] = given[i] + more
            surplus = surplus - more
    return np.array([most] + given)


def ragged_sizes(key, number_of, total, most, slope):
    if number_of == 2:
        one = jax.random.randint(key, (), max(1, total - most), min(most, total - 1) + 1)
        return jnp.stack([one, total - one])
    lengths = jnp.asarray(profile(number_of, total, most, slope), jnp.int32)
    pairs = (number_of - 1) // 2
    donor, sink = lengths[1:1 + 2 * pairs:2], lengths[2:2 + 2 * pairs:2]
    margin = jnp.minimum(donor - 1, most - sink)
    passed = jax.random.randint(jax.random.fold_in(key, 1), (pairs,), 0, 1 << 20) % (margin + 1)
    lengths = lengths.at[1:1 + 2 * pairs:2].set(donor - passed).at[2:2 + 2 * pairs:2].set(sink + passed)
    return lengths[jax.random.permutation(jax.random.fold_in(key, 2), number_of)]


def centred(stream_key, dims, deviation, reach, cuts=(), kind=jnp.bfloat16):
    factor_of = block_levels(stream_key, dims, cuts, -0.22, 0.18) if cuts else 1.0
    drawn = jax.random.normal(stream_key, dims, jnp.float32) * deviation * factor_of
    return jnp.minimum(jnp.maximum(drawn, -reach), reach).astype(kind)


def bell_draw_with(stream_key, dims, scale, limit, shards, heavy, kind=jnp.bfloat16):
    values = scale * jax.random.normal(stream_key, dims, jnp.float32)
    if shards:
        values = values * block_levels(stream_key, dims, shards, -0.22, 0.18)
    return jnp.clip(spiked(values, jax.random.fold_in(stream_key, 3), *heavy), -limit, limit).astype(kind)


def setup_inputs(seed: int = 0) -> dict:
    key_of = jax.random.split(jax.random.key(seed), 16)
    return {
        "tokens": centred(key_of[0], (MICRO, ROWS, D), 1.0, 6.0, ((1, 32),)),
        "doc_lengths": jax.vmap(lambda own: ragged_sizes(own, DOCS, TOK_MB, LONGEST, 2))(jax.random.split(key_of[1], MICRO * (N_DP * N_REP))).reshape((MICRO, N_DP * N_REP, DOCS)).astype(jnp.int32),
        "cotangent": bell_draw_with(key_of[2], (MICRO, ROWS, D), 1.0, 6.0, ((1, 32),), (1, 2, 32, 2.75)),
        "attn_gain": jnp.clip(1.0 + 0.1 * jax.random.normal(key_of[3], (D,), jnp.float32), 0.5, 1.5).astype(jnp.bfloat16),
        "attn_shift": centred(key_of[4], (D,), 0.2, 1.0, ((0, 16),)),
        "qkv_weight": centred(key_of[5], (D, 3 * D), D ** -0.5, 0.21875, ((0, 16),)),
        "qkv_bias": centred(key_of[6], (3 * D,), 0.2, 1.0, ((0, 16),)),
        "out_weight": centred(key_of[7], (D, D), (D // 8) ** -0.5, 0.625, ((0, 16),)),
        "out_bias": centred(key_of[8], (D,), 0.2, 1.0, ((0, 16),)),
        "mlp_gain": jnp.clip(1.0 + 0.1 * jax.random.normal(key_of[9], (D,), jnp.float32), 0.5, 1.5).astype(jnp.bfloat16),
        "mlp_shift": centred(key_of[10], (D,), 0.2, 1.0, ((0, 16),)),
        "fc_weight": centred(key_of[11], (D, FF), D ** -0.5, 0.21875, ((0, 16),)),
        "fc_bias": centred(key_of[12], (FF,), 0.2, 1.0, ((0, 16),)),
        "proj_weight": centred(key_of[13], (FF, D), (FF // 2) ** -0.5, 0.15625, ((0, 16),)),
        "proj_bias": centred(key_of[14], (D,), 0.2, 1.0, ((0, 16),)),
    }


@jax.custom_vjp
def low(v):
    return lax.optimization_barrier(v.astype(jnp.bfloat16)).astype(jnp.float32)

@jax.custom_vjp
def low_back(v):
    return v

def low_keep(v):
    return (low(v), None)

def low_pass(kept, grad):
    return (grad,)

def back_keep(v):
    return (v, None)

def back_low(kept, grad):
    return (low(grad),)
low.defvjp(low_keep, low_pass)
low_back.defvjp(back_keep, back_low)
eps_norm = 1e-05
highest = lax.Precision.HIGHEST

def matmul(left, right):
    return jnp.dot(left, right, precision=highest)

def layer_norm(values, gain, shift):
    center = values - lax.optimization_barrier(jnp.mean(values, axis=-1, keepdims=True))
    spread = lax.optimization_barrier(jnp.mean(center * center, axis=-1, keepdims=True))
    return center * lax.rsqrt(spread + eps_norm) * gain + shift

def segment_ids(lengths_row, count):
    ends = jnp.cumsum(lengths_row.astype(jnp.int32)).astype(jnp.int32)
    places = jnp.arange(count, dtype=jnp.int32)
    return lax.optimization_barrier(jnp.sum((places[:, None] >= ends[None, :]).astype(jnp.int32), axis=1)).astype(jnp.int32)

def attend_row(packed):
    query, keys, values, segs = packed
    count = query.shape[0]
    places = jnp.arange(count, dtype=jnp.int32)
    allowed = (segs[:, None] == segs[None, :]) & (places[None, :] <= places[:, None])
    scores = low_back(jnp.einsum('qhd,khd->hqk', query, keys, precision=highest) * 0.125)
    scores = jnp.where(allowed[None], scores, -1e+30)
    top = lax.optimization_barrier(jnp.max(scores, axis=-1, keepdims=True))
    expo = jnp.exp(scores - top)
    probs = low(expo / lax.optimization_barrier(jnp.sum(expo, axis=-1, keepdims=True)))
    return jnp.einsum('hqk,khd->qhd', probs, values, precision=highest)

def block(states, segs, weights):
    attn_gain, attn_shift, qkv_weight, qkv_bias, out_weight, out_bias, mlp_gain, mlp_shift, fc_weight, fc_bias, proj_weight, proj_bias = weights
    rows, count, width = states.shape
    flat = states.reshape(rows * count, width)
    normed_a = low(layer_norm(flat, attn_gain, attn_shift))
    mixed = low(low_back(matmul(normed_a, qkv_weight) + qkv_bias))
    heads = mixed.reshape(rows, count, 3, H, HD)
    attended = lax.map(jax.checkpoint(attend_row), (heads[:, :, 0], heads[:, :, 1], heads[:, :, 2], segs))
    attended = low(low_back(attended.reshape(rows * count, width)))
    hidden = flat + low_back(matmul(attended, out_weight) + out_bias)
    normed_m = low(layer_norm(hidden, mlp_gain, mlp_shift))
    expanded = low_back(matmul(normed_m, fc_weight) + fc_bias)
    activated = low(jax.nn.gelu(expanded, approximate=True))
    result = hidden + low_back(matmul(activated, proj_weight) + proj_bias)
    return result.reshape(rows, count, width)

def reference(tokens, doc_lengths, cotangent, attn_gain, attn_shift, qkv_weight, qkv_bias, out_weight, out_bias, mlp_gain, mlp_shift, fc_weight, fc_bias, proj_weight, proj_bias):
    rows_all = MICRO * N_DP * N_REP
    pack = math.gcd(rows_all, max(1, 4096 // TOK_MB))
    packs = rows_all // pack
    weights = (attn_gain.astype(jnp.float32), attn_shift.astype(jnp.float32), qkv_weight.astype(jnp.float32), qkv_bias.astype(jnp.float32), out_weight.astype(jnp.float32), out_bias.astype(jnp.float32), mlp_gain.astype(jnp.float32), mlp_shift.astype(jnp.float32), fc_weight.astype(jnp.float32), fc_bias.astype(jnp.float32), proj_weight.astype(jnp.float32), proj_bias.astype(jnp.float32))
    states = tokens.astype(jnp.float32).reshape(packs, pack, TOK_MB, D)
    grads_in = cotangent.astype(jnp.float32).reshape(packs, pack, TOK_MB, D)
    lengths_all = doc_lengths.reshape(rows_all, DOCS)
    segs = jax.vmap(lambda row: segment_ids(row, TOK_MB))(lengths_all).reshape(packs, pack, TOK_MB)

    def forward(states_pack, segs_pack, weight_set):
        current = states_pack
        for use in range(USES):
            current = block(current, segs_pack, weight_set)
        return current

    def step(carry, packed):
        states_pack, segs_pack, grad_pack = packed
        result, pull = jax.vjp(lambda state_arg, weight_arg: forward(state_arg, segs_pack, weight_arg), states_pack, weights)
        d_states, d_weights = pull(grad_pack)
        carry = jax.tree.map(jnp.add, carry, d_weights)
        return (carry, (result, d_states))
    zero = tuple((jnp.zeros_like(weight) for weight in weights))
    totals, (results, backs) = lax.scan(step, zero, (states, segs, grads_in))
    shape = tokens.shape
    return (results.reshape(shape).astype(jnp.bfloat16), backs.reshape(shape).astype(jnp.bfloat16), totals[0], totals[1], totals[2], totals[3], totals[4], totals[5], totals[6], totals[7], totals[8], totals[9], totals[10], totals[11])
```

```python
import functools

import jax
import jax.numpy as jnp
from jax import lax
from jax.experimental import pallas as pl
from jax.experimental.pallas import tpu as pltpu
from jax.sharding import PartitionSpec as P

H = 12
HD = 64
USES = 2
BOTH = ("dp", "rep")


eps_norm = 1e-05


def layer_norm(values, gain, shift):
    center = values - jnp.mean(values, axis=-1, keepdims=True)
    spread = jnp.mean(center * center, axis=-1, keepdims=True)
    return center * lax.rsqrt(spread + eps_norm) * gain + shift


def segment_ids(lengths_row, count):
    ends = jnp.cumsum(lengths_row)
    places = jnp.arange(count, dtype=jnp.int32)
    return jnp.sum((places[:, None] >= ends[None, :]).astype(jnp.int32), axis=1)


def outer_sum(left, right):
    return lax.dot_general(
        left, right, (((0,), (0,)), ((), ())), preferred_element_type=jnp.float32
    )


def times_transpose(left, right):
    return lax.dot_general(
        left, right, (((1,), (1,)), ((), ())), preferred_element_type=jnp.float32
    )


def swap(value, bits):
    return lax.ppermute(value, BOTH, [(i, i ^ bits) for i in range(32)])


CORE, X, Y, Z1, Z2, Z3 = (1, 2, 4, 8, 16, 24)


def place_kernel(me_ref, *refs):
    sources, (target, sems) = (refs[:16], refs[16:])
    me = me_ref[0]
    copies = []
    for slot, source in enumerate(sources):
        core, rest = (slot // 8, slot % 8)
        for inner in range(2):
            z_rel = (rest // 4) * 2 + inner
            rel = z_rel * 8 + (rest % 4) * 2 + core
            copies.append(
                pltpu.make_async_copy(
                    source.at[inner], target.at[rel ^ me], sems.at[2 * slot + inner]
                )
            )
    for copy in copies:
        copy.start()
    for copy in copies:
        copy.wait()


def place(me, sources, rows, width):
    placed = pl.pallas_call(
        place_kernel,
        out_shape=jax.ShapeDtypeStruct((32, rows, width), jnp.bfloat16),
        in_specs=[pl.BlockSpec(memory_space=pltpu.SMEM)]
        + [pl.BlockSpec(memory_space=pl.ANY)] * 16,
        out_specs=pl.BlockSpec(memory_space=pltpu.VMEM),
        scratch_shapes=[pltpu.SemaphoreType.DMA((32,))],
    )(me, *sources)
    return placed.reshape(32 * rows, width)


def gather_rows(piece, me):
    rows, width = piece.shape
    piece = piece[None]
    first, second, third = (swap(piece, Z1), swap(piece, Z2), swap(piece, Z3))
    near = jnp.concatenate([piece, first])
    far = jnp.concatenate([second, third])
    near_y, near_x = (swap(near, Y), swap(near, X))
    far_x, far_y = (swap(far, X), swap(far, Y))
    near_xy = swap(near_y, X)
    far_xy = swap(far_x, Y)
    mine = [near, near_x, near_y, near_xy, far, far_x, far_y, far_xy]
    theirs = [swap(part, CORE) for part in mine]
    return place(me, mine + theirs, rows, width)


def pick(array, axis, index):
    return lax.dynamic_index_in_dim(array, index, axis, keepdims=False)


def low(value):
    return value.astype(jnp.bfloat16)


def wide(value):
    return value.astype(jnp.float32)


def reduce_rows(grad, spot):
    z_pair, z_low, y, x, core = spot
    rows, width = (grad.shape[0] // 32, grad.shape[1])
    parts = grad.reshape(2, 2, 2, 2, 2, rows, width)
    got = swap(pick(parts, 4, 1 - core), CORE)
    mine = pick(parts, 4, core)
    near, near_got = (pick(mine, 0, z_pair), pick(got, 0, z_pair))
    far, far_got = (pick(mine, 0, 1 - z_pair), pick(got, 0, 1 - z_pair))

    def add(left, right):
        return low(wide(left) + wide(right))

    near_sent = swap(add(pick(near, 2, 1 - x), pick(near_got, 2, 1 - x)), X)
    far_sent = swap(add(pick(far, 1, 1 - y), pick(far_got, 1, 1 - y)), Y)

    def add3(left, middle, right):
        return low(wide(left) + wide(middle) + wide(right))

    near_x, near_x_got = (pick(near, 2, x), pick(near_got, 2, x))
    far_y, far_y_got = (pick(far, 1, y), pick(far_got, 1, y))
    near_next = swap(
        add3(pick(near_x, 1, 1 - y), pick(near_x_got, 1, 1 - y), pick(near_sent, 1, 1 - y)), Y
    )
    far_next = swap(
        add3(pick(far_y, 1, 1 - x), pick(far_y_got, 1, 1 - x), pick(far_sent, 1, 1 - x)), X
    )

    def add4(a, b, c, d):
        return wide(a) + wide(b) + wide(c) + wide(d)

    near_last = (pick(near_x, 1, y), pick(near_x_got, 1, y), pick(near_sent, 1, y), near_next)
    far_last = (pick(far_y, 1, x), pick(far_y_got, 1, x), pick(far_sent, 1, x), far_next)

    def row(parts4, index):
        return add4(*[pick(part, 0, index) for part in parts4])

    one = swap(low(row(near_last, 1 - z_low)), Z1)
    two = swap(low(row(far_last, z_low)), Z2)
    three = swap(low(row(far_last, 1 - z_low)), Z3)
    return row(near_last, z_low) + wide(one) + wide(two) + wide(three)


def both_halves(half, core):
    other = swap(half, CORE)
    return jnp.where(
        core == 0, jnp.concatenate([half, other]), jnp.concatenate([other, half])
    )


def gather_small(pieces, spot):
    z_pair, z_low, y, x, core = spot
    sizes = [piece.shape[0] for piece in pieces]
    packed = jnp.concatenate(pieces)
    packed = jnp.pad(packed, (0, 1024 - packed.shape[0])).reshape(8, 128)
    group = jnp.stack([packed, swap(packed, Z1), swap(packed, Z2), swap(packed, Z3)])
    group = jnp.stack([group, swap(group, X)])
    group = jnp.stack([group, swap(group, Y)])
    group = group.reshape(2, 2, 2, 2, 1024)
    for axis, bit in enumerate((y, x, z_pair, z_low)):
        group = jnp.where(bit == 1, jnp.flip(group, axis), group)
    group = jnp.transpose(group, (2, 3, 0, 1, 4)).reshape(16, 1024)
    vectors, start = ([], 0)
    for size in sizes:
        vectors.append(group[:, start : start + size].reshape(-1))
        start += size
    return vectors


def reduce_small(vectors, dp):
    sizes = [vector.shape[0] // 16 for vector in vectors]
    packed = jnp.concatenate([vector.reshape(16, -1) for vector in vectors], axis=1)
    packed = jnp.pad(packed, ((0, 0), (0, 640 - packed.shape[1])))
    for bits in (CORE, X, Y, Z1, Z2):
        packed = packed + swap(packed, bits)
    own = pick(packed, 0, dp)
    parts, start = ([], 0)
    for size in sizes:
        parts.append(own[start : start + size])
        start += size
    return parts


def gather_all(weights, spot, me):
    gain_a, shift_a, qkv, qbias, out, obias, gain_m, shift_m, fc, fbias, proj, pbias = weights
    core = spot[4]

    def half(weight):
        rows = weight.shape[0] // 2
        return lax.dynamic_slice_in_dim(weight, core * rows, rows, 0)

    small = gather_small([gain_a, shift_a, qbias, obias, gain_m, shift_m, fbias, pbias], spot)
    first = gather_rows(jnp.concatenate([half(qkv), half(out)], axis=1), me)
    whole_fc = gather_rows(half(fc), me)
    whole_proj = gather_rows(half(proj), me)
    width = qkv.shape[1]
    gain_a, shift_a, qbias, obias, gain_m, shift_m, fbias, pbias = small
    return (
        gain_a,
        shift_a,
        first[:, :width],
        qbias,
        first[:, width:],
        obias,
        gain_m,
        shift_m,
        whole_fc,
        fbias,
        whole_proj,
        pbias,
    )


def reduce_all(grads, spot, dp):
    core = spot[4]
    matrices = {}
    for index in (10, 8, 4, 2):
        matrices[index] = both_halves(reduce_rows(low(grads[index]), spot), core)
    order = (0, 1, 3, 5, 6, 7, 9, 11)
    small = reduce_small([grads[index] for index in order], dp)
    result = list(grads)
    for index, part in zip(order, small):
        result[index] = part
    for index, part in matrices.items():
        result[index] = part
    return tuple(result)


def block_scores(query, keys, segs, start, length):
    count = keys.shape[0]
    query_pos = start + jnp.arange(length, dtype=jnp.int32)
    key_pos = jnp.arange(count, dtype=jnp.int32)
    allowed = (segs[:, None] == segs[None, :]) & (key_pos[None, :] <= query_pos[:, None])
    scores = jnp.einsum("qhd,khd->hqk", query, keys, preferred_element_type=jnp.float32) * 0.125
    return jnp.where(allowed[None], scores, -1e30)


def attend_forward(query, keys, values, segs):
    count = query.shape[0]
    scores = block_scores(query, keys, segs, 0, count)
    top = jnp.max(scores, axis=-1, keepdims=True)
    expo = jnp.exp(scores - top)
    total = jnp.sum(expo, axis=-1, keepdims=True)
    probs = (expo / total).astype(jnp.bfloat16)
    result = jnp.einsum("hqk,khd->qhd", probs, values, preferred_element_type=jnp.float32)
    return (result.astype(jnp.bfloat16).reshape(count, H * HD), (top + jnp.log(total))[..., 0])


def attend_backward(query, keys, values, segs, logsum, grad_att):
    count = query.shape[0]
    scores = block_scores(query, keys, segs, 0, count)
    probs = jnp.exp(scores - logsum[..., None])
    grad_values = jnp.einsum(
        "hqk,qhd->khd", probs.astype(jnp.bfloat16), grad_att, preferred_element_type=jnp.float32
    )
    grad_probs = jnp.einsum("qhd,khd->hqk", grad_att, values, preferred_element_type=jnp.float32)
    grad_scores = probs * (grad_probs - jnp.sum(probs * grad_probs, axis=-1, keepdims=True))
    score_low = grad_scores.astype(jnp.bfloat16)
    grad_query = (
        jnp.einsum("hqk,khd->qhd", score_low, keys, preferred_element_type=jnp.float32) * 0.125
    )
    grad_keys = (
        jnp.einsum("hqk,qhd->khd", score_low, query, preferred_element_type=jnp.float32) * 0.125
    )
    return jnp.stack([grad_query, grad_keys, grad_values], axis=1).reshape(count, 3 * H * HD)


def layer_forward(inputs, weights, segs):
    tokens = segs[0].shape[0]
    normed_a = low(layer_norm(inputs, wide(weights[0]), wide(weights[1])))
    mixed = low(
        jnp.dot(normed_a, weights[2], preferred_element_type=jnp.float32) + wide(weights[3])
    )
    attended, logsum = ([], [])
    for index, seg in enumerate(segs):
        heads = mixed[index * tokens : (index + 1) * tokens].reshape(tokens, 3, H, HD)
        one, log_one = attend_forward(heads[:, 0], heads[:, 1], heads[:, 2], seg)
        attended.append(one)
        logsum.append(log_one)
    attended = jnp.concatenate(attended)
    hidden = inputs + (
        jnp.dot(attended, weights[4], preferred_element_type=jnp.float32) + wide(weights[5])
    )
    normed_m = low(layer_norm(hidden, wide(weights[6]), wide(weights[7])))
    expanded = jnp.dot(normed_m, weights[8], preferred_element_type=jnp.float32) + wide(weights[9])
    activated = low(jax.nn.gelu(expanded, approximate=True))
    result = hidden + (
        jnp.dot(activated, weights[10], preferred_element_type=jnp.float32) + wide(weights[11])
    )
    return (
        result,
        (inputs, normed_a, mixed, logsum, attended, hidden, normed_m, expanded, activated),
    )


def layer_backward(grad, weights, saved, segs):
    inputs, normed_a, mixed, logsum, attended, hidden, normed_m, expanded, activated = saved
    tokens = segs[0].shape[0]
    grad_low = low(grad)
    grad_proj = outer_sum(activated, grad_low)
    grad_pbias = jnp.sum(wide(grad_low), axis=0)
    grad_act = times_transpose(grad_low, weights[10])
    unused, gelu_back = jax.vjp(lambda point: jax.nn.gelu(point, approximate=True), expanded)
    grad_exp = low(gelu_back(grad_act)[0])
    grad_fc = outer_sum(normed_m, grad_exp)
    grad_fbias = jnp.sum(wide(grad_exp), axis=0)
    grad_normm = times_transpose(grad_exp, weights[8])
    unused, norm_back = jax.vjp(layer_norm, hidden, wide(weights[6]), wide(weights[7]))
    grad_norm, grad_mgain, grad_mshift = norm_back(grad_normm)
    grad_hidden = grad + grad_norm
    hidden_low = low(grad_hidden)
    grad_out = outer_sum(attended, hidden_low)
    grad_obias = jnp.sum(wide(hidden_low), axis=0)
    grad_att = low(times_transpose(hidden_low, weights[4]))
    grad_mixed = []
    for index, seg in enumerate(segs):
        rows = slice(index * tokens, (index + 1) * tokens)
        heads = mixed[rows].reshape(tokens, 3, H, HD)
        grad_mixed.append(
            attend_backward(
                heads[:, 0],
                heads[:, 1],
                heads[:, 2],
                seg,
                logsum[index],
                grad_att[rows].reshape(tokens, H, HD),
            )
        )
    grad_mixed = low(jnp.concatenate(grad_mixed))
    grad_qkv = outer_sum(normed_a, grad_mixed)
    grad_qbias = jnp.sum(wide(grad_mixed), axis=0)
    grad_norma = times_transpose(grad_mixed, weights[2])
    unused, first_back = jax.vjp(layer_norm, inputs, wide(weights[0]), wide(weights[1]))
    grad_inputs, grad_again, grad_ashift = first_back(grad_norma)
    grads = (
        grad_again,
        grad_ashift,
        grad_qkv,
        grad_qbias,
        grad_out,
        grad_obias,
        grad_mgain,
        grad_mshift,
        grad_fc,
        grad_fbias,
        grad_proj,
        grad_pbias,
    )
    return (grad_hidden + grad_inputs, grads)


def shards(custom, tokens, doc_lengths, cotangent, *weights):
    micro, count, width = tokens.shape
    dp, core = (lax.axis_index("dp"), lax.axis_index("rep"))
    spot = (dp // 8, dp // 4 % 2, dp // 2 % 2, dp % 2, core)
    me = (dp * 2 + core).astype(jnp.int32).reshape(1)
    if custom:
        whole = gather_all(weights, spot, me)
    else:
        whole = tuple(lax.all_gather(weight, "dp", axis=0, tiled=True) for weight in weights)
    segs = [segment_ids(doc_lengths[index, 0], count) for index in range(micro)]
    current = wide(tokens.reshape(micro * count, width))
    kept = []
    for use in range(USES):
        current, saved = layer_forward(current, whole, segs)
        kept.append(saved)
    grad = wide(cotangent.reshape(micro * count, width))
    summed = None
    for use in range(USES - 1, -1, -1):
        grad, grads = layer_backward(grad, whole, kept[use], segs)
        summed = grads if summed is None else jax.tree.map(jnp.add, summed, grads)
    if custom:
        final = reduce_all(summed, spot, dp)
    else:
        final = tuple(
            wide(
                lax.psum(
                    low(lax.psum_scatter(value, "dp", scatter_dimension=0, tiled=True)), "rep"
                )
            )
            for value in summed
        )
    return (low(current).reshape(tokens.shape), low(grad).reshape(tokens.shape), *final)


def solution(mesh):
    custom = mesh.shape["dp"] == 16 and mesh.shape["rep"] == 2
    placed = tuple(
        P("dp", None) if index in (2, 4, 8, 10) else P("dp") for index in range(12)
    )
    rows = P(None, BOTH, None)
    return jax.shard_map(
        functools.partial(shards, custom),
        mesh=mesh,
        in_specs=(rows, rows, rows, *placed),
        out_specs=(rows, rows, *placed),
        check_vma=False,
    )
```

```python
import functools
import math

import jax
import jax.numpy as jnp
from jax import lax
from jax.experimental import pallas as pl
from jax.experimental.pallas import tpu as pltpu
from jax.sharding import PartitionSpec as P

H = 12
HD = 64
USES = 2
LONGEST = 256
BOTH = ("dp", "rep")


NORM_EPS = 1e-05
BLOCK = 128
FEATURES = H * HD
VMEM_LIMIT = 60 << 20


def dot(left, right):
    return jnp.dot(left, right, preferred_element_type=jnp.float32)


def norm_parts(values):
    center = values - jnp.mean(values, axis=-1, keepdims=True)
    spread = jnp.mean(center * center, axis=-1, keepdims=True)
    scale = lax.rsqrt(spread + NORM_EPS)
    return (center * scale, scale)


def norm_back(normed, scale, gain, grad):
    inner = grad * gain
    first = jnp.mean(inner, axis=-1, keepdims=True)
    second = jnp.mean(inner * normed, axis=-1, keepdims=True)
    return (inner - first - normed * second) * scale


def segment_of(places, lengths, docs):
    end = jnp.int32(0)
    segment = jnp.zeros(places.shape, jnp.int32)
    for doc in range(docs):
        end = end + lengths[doc]
        segment = segment + (places >= end).astype(jnp.int32)
    return segment


def allowed_bias(count, lengths, docs, query_axis):
    query_shape = (count, 1) if query_axis == 0 else (1, count)
    key_shape = (1, count) if query_axis == 0 else (count, 1)
    query = lax.broadcasted_iota(jnp.int32, query_shape, query_axis)
    key = lax.broadcasted_iota(jnp.int32, key_shape, 1 - query_axis)
    same = segment_of(query, lengths, docs) == segment_of(key, lengths, docs)
    return jnp.where(same & (key <= query), 0.0, -1e30).astype(jnp.float32)


def head_split(pair):
    left = lax.broadcasted_iota(jnp.int32, pair.shape, 1) < HD
    zero = jnp.zeros_like(pair)
    return jnp.concatenate([jnp.where(left, pair, zero), jnp.where(left, zero, pair)], axis=0)


def head_join(stacked):
    count = stacked.shape[0] // 2
    left = lax.broadcasted_iota(jnp.int32, (count, 2 * HD), 1) < HD
    return jnp.where(left, stacked[:count], stacked[count:])


def attention_forward_kernel(
    docs,
    back,
    lengths_ref,
    state_ref,
    gain_ref,
    shift_ref,
    weight_ref,
    qbias_ref,
    obias_ref,
    gain2_ref,
    shift2_ref,
    normed_ref,
    mixed_ref,
    att_ref,
    lse_ref,
    hidden_ref,
    normed2_ref,
    bias_ref,
    lse_cols,
):
    micro = pl.program_id(0)
    state = state_ref[...].astype(jnp.float32)
    count = state.shape[0]
    normed = (norm_parts(state)[0] * gain_ref[...] + shift_ref[...]).astype(jnp.bfloat16)
    normed_ref[...] = normed
    for part in range(3):
        columns = slice(part * FEATURES, (part + 1) * FEATURES)
        mixed_ref[:, columns] = (dot(normed, weight_ref[part]) + qbias_ref[:, columns]).astype(
            jnp.bfloat16
        )
    bias_ref[...] = allowed_bias(count, [lengths_ref[micro, d] for d in range(docs)], docs, 0)
    lse_cols[...] = jnp.zeros_like(lse_cols)

    def one_pair(pair, carry):
        lanes = pl.multiple_of(pair * 2 * HD, 2 * HD)
        for block in range(count // BLOCK):
            rows = slice(block * BLOCK, (block + 1) * BLOCK)
            low_key = max(0, block - back) * BLOCK
            keys = slice(low_key, (block + 1) * BLOCK)
            query = head_split(mixed_ref[rows, pl.ds(lanes, 2 * HD)])
            key = mixed_ref[keys, pl.ds(FEATURES + lanes, 2 * HD)]
            value = mixed_ref[keys, pl.ds(2 * FEATURES + lanes, 2 * HD)]
            scores = lax.dot_general(
                query, key, (((1,), (1,)), ((), ())), preferred_element_type=jnp.float32
            )
            bias = bias_ref[rows, keys]
            scores = scores * 0.125 + jnp.concatenate([bias, bias], axis=0)
            top = jnp.max(scores, axis=-1, keepdims=True)
            expo = jnp.exp(scores - top)
            total = jnp.sum(expo, axis=-1, keepdims=True)
            result = dot(expo.astype(jnp.bfloat16), value) / total
            att_ref[rows, pl.ds(lanes, 2 * HD)] = head_join(result).astype(jnp.bfloat16)
            lse = top + jnp.log(total)
            lane = lax.broadcasted_iota(jnp.int32, (BLOCK, 128), 1)
            lse_cols[rows, :] += jnp.where(lane == 2 * pair, lse[:BLOCK], 0.0) + jnp.where(
                lane == 2 * pair + 1, lse[BLOCK:], 0.0
            )
        return carry

    lax.fori_loop(0, H // 2, one_pair, 0)
    lse = jnp.transpose(lse_cols[...])
    for index in range(H):
        lse_ref[index] = lse[index : index + 1]
    hidden = state + (dot(att_ref[...], weight_ref[3]) + obias_ref[...])
    hidden_ref[...] = hidden
    normed2_ref[...] = (norm_parts(hidden)[0] * gain2_ref[...] + shift2_ref[...]).astype(
        jnp.bfloat16
    )


def whole(array):
    dims = len(array.shape)
    return pl.BlockSpec(array.shape, lambda *unused: (0,) * dims, pipeline_mode=pl.Buffered(1))


SMEM = pl.BlockSpec(memory_space=pltpu.SMEM)


def rows_of(count, width):
    return pl.BlockSpec((count, width), lambda i: (i, 0))


def params():
    return pltpu.CompilerParams(vmem_limit_bytes=VMEM_LIMIT)


def cost(flops, transcendentals, *arrays):
    size = sum(math.prod(a.shape) * a.dtype.itemsize for a in arrays)
    return pl.CostEstimate(
        flops=int(flops), transcendentals=int(transcendentals), bytes_accessed=int(size)
    )


def attention_forward(lengths, state, count, back, gain, shift, weight, qbias, obias, gain2, shift2):
    rows = state.shape[0]
    micro, docs = lengths.shape
    width = FEATURES
    shape = jax.ShapeDtypeStruct
    outs = (
        shape((rows, width), jnp.bfloat16),
        shape((rows, 3 * width), jnp.bfloat16),
        shape((rows, width), jnp.bfloat16),
        shape((micro * H, 1, count), jnp.float32),
        shape((rows, width), jnp.float32),
        shape((rows, width), jnp.bfloat16),
    )
    weights = (gain, shift, weight, qbias, obias, gain2, shift2)
    return pl.pallas_call(
        functools.partial(attention_forward_kernel, docs, back),
        grid=(micro,),
        out_shape=outs,
        in_specs=[SMEM, rows_of(count, width)] + [whole(w) for w in weights],
        out_specs=(
            rows_of(count, width),
            rows_of(count, 3 * width),
            rows_of(count, width),
            pl.BlockSpec((H, 1, count), lambda i: (i, 0, 0)),
            rows_of(count, width),
            rows_of(count, width),
        ),
        scratch_shapes=[
            pltpu.VMEM((count, count), jnp.float32),
            pltpu.VMEM((count, 128), jnp.float32),
        ],
        compiler_params=params(),
        cost_estimate=cost(
            8 * rows * width * width + 4 * rows * count * width, rows * count * H, state, *weights, *outs
        ),
        name="attention_forward",
    )(lengths, state, *weights)


GELU_C = 0.7978845608028654
GELU_K = 0.044715 * GELU_C


def gelu_gate(value):
    square = value * value
    gate = 0.5 * jnp.tanh(value * (GELU_C + GELU_K * square)) + 0.5
    return (gate, square)


def mlp_forward_kernel(
    last, hidden_ref, normed_ref, fc_ref, fbias_ref, proj_ref, pbias_ref, expanded_ref, *rest
):
    final_ref, state_ref = rest if last else (None, rest[0])
    step = pl.program_id(0)
    chunk = 256

    @pl.when(step == 0)
    def _():
        state_ref[...] = hidden_ref[...] + pbias_ref[...]

    for start in range(0, normed_ref.shape[0], chunk):
        rows = slice(start, start + chunk)
        expanded = dot(normed_ref[rows, :], square_of(fc_ref)) + fbias_ref[...]
        expanded_ref[rows, :] = expanded.astype(expanded_ref.dtype)
        gate, unused = gelu_gate(expanded)
        activated = (expanded * gate).astype(jnp.bfloat16)
        state_ref[rows, :] += dot(activated, square_of(proj_ref))

    if last:

        @pl.when(step == pl.num_programs(0) - 1)
        def _():
            final_ref[...] = state_ref[...].astype(jnp.bfloat16)


def square_of(ref):
    return ref[...].reshape(FEATURES, FEATURES)


FC_BLOCK = pl.BlockSpec((16, 1, 1, 48, FEATURES), lambda i: (0, i // 2, i % 2, 0, 0))
PROJ_BLOCK = pl.BlockSpec((4, 2, 2, 48, FEATURES), lambda i: (i, 0, 1, 0, 0))


def mlp_forward(hidden, normed, mlp, fbias, pbias, last):
    rows, width = hidden.shape
    block = width
    hidden_units = 4 * block
    shape = jax.ShapeDtypeStruct
    outs = (
        shape((rows, hidden_units), jnp.bfloat16),
        shape((rows, width), jnp.bfloat16 if last else jnp.float32),
    )
    specs = (
        pl.BlockSpec((rows, block), lambda i: (0, i)),
        pl.BlockSpec((rows, width), lambda i: (0, 0)),
    )
    return pl.pallas_call(
        functools.partial(mlp_forward_kernel, last),
        grid=(hidden_units // block,),
        out_shape=outs,
        in_specs=[
            whole(hidden),
            whole(normed),
            FC_BLOCK,
            pl.BlockSpec((1, block), lambda i: (0, i)),
            PROJ_BLOCK,
            whole(pbias),
        ],
        out_specs=specs,
        scratch_shapes=[pltpu.VMEM((rows, width), jnp.float32)] if last else [],
        compiler_params=params(),
        cost_estimate=cost(
            4 * rows * width * hidden_units, rows * hidden_units, hidden, normed, mlp, *outs
        ),
        name="mlp_forward",
    )(hidden, normed, mlp, fbias, mlp, pbias)


def transposed_dot(left, right):
    return lax.dot_general(
        left, right, (((0,), (0,)), ((), ())), preferred_element_type=jnp.float32
    )


def dot_transposed(left, right):
    return lax.dot_general(
        left, right, (((1,), (1,)), ((), ())), preferred_element_type=jnp.float32
    )


def transposed_dot(left, right):
    return lax.dot_general(
        left, right, (((0,), (0,)), ((), ())), preferred_element_type=jnp.float32
    )


def dot_transposed(left, right):
    return lax.dot_general(
        left, right, (((1,), (1,)), ((), ())), preferred_element_type=jnp.float32
    )


def store_halves(core, value, mine_ref, theirs_ref, earlier):
    half = value.shape[1] // 2
    left, right = (value[:, :half], value[:, half:])
    mine = jnp.where(core == 0, left, right)
    theirs = jnp.where(core == 0, right, left)
    if earlier is not None:
        mine = mine + earlier[0][0].astype(jnp.float32)
        theirs = theirs + earlier[1][0].astype(jnp.float32)
    mine_ref[0] = mine.astype(mine_ref.dtype)
    theirs_ref[0] = theirs.astype(theirs_ref.dtype)


def mlp_backward_kernel(
    more,
    core_ref,
    grad_ref,
    hidden_ref,
    normed_ref,
    expanded_ref,
    fc_ref,
    proj_ref,
    gain_ref,
    *rest,
):
    earlier = rest[:8] if more else (None,) * 8
    if more:
        rest = rest[8:]
    (
        dhid_ref,
        fc_mine,
        fc_theirs,
        proj_mine,
        proj_theirs,
        dfbias_ref,
        dpbias_ref,
        dgain_ref,
        dshift_ref,
        low_ref,
        normed_t,
        acc_ref,
        act_ref,
        ge_ref,
    ) = rest
    step = pl.program_id(0)
    core = core_ref[0]
    rows = grad_ref.shape[0]
    chunk = 256

    @pl.when(step == 0)
    def _():
        low_grad = grad_ref[...].astype(jnp.bfloat16)
        low_ref[...] = low_grad
        dpbias = jnp.sum(low_grad.astype(jnp.float32), axis=0, keepdims=True)
        dpbias_ref[...] = dpbias + earlier[5][...] if more else dpbias
        normed_t[...] = jnp.transpose(normed_ref[...])
        acc_ref[...] = jnp.zeros_like(acc_ref)

    bias_sum = jnp.zeros(dfbias_ref.shape[1:], jnp.float32)
    for start in range(0, rows, chunk):
        part = slice(start, start + chunk)
        grad_act = dot_transposed(low_ref[part, :], square_of(proj_ref))
        value = expanded_ref[part, :].astype(jnp.float32)
        gate, square = gelu_gate(value)
        act = value * gate
        slope = gate + act * (1.0 - gate) * (2 * GELU_C + 6 * GELU_K * square)
        act_ref[part, :] = act.astype(jnp.bfloat16)
        grad_exp = (grad_act * slope).astype(jnp.bfloat16)
        ge_ref[part, :] = grad_exp
        bias_sum = bias_sum + jnp.sum(grad_exp.astype(jnp.float32), axis=0, keepdims=True)
        acc_ref[part, :] += dot_transposed(grad_exp, square_of(fc_ref))
    dfbias_ref[0] = bias_sum + earlier[4][0] if more else bias_sum
    dproj = transposed_dot(act_ref[...], low_ref[...])
    store_halves(core, dproj, proj_mine, proj_theirs, earlier[2:4] if more else None)
    dfc = dot(normed_t[...], ge_ref[...])
    store_halves(core, dfc, fc_mine, fc_theirs, earlier[:2] if more else None)

    @pl.when(step == pl.num_programs(0) - 1)
    def _():
        normed, scale = norm_parts(hidden_ref[...])
        grad_norm = acc_ref[...]
        dgain = jnp.sum(grad_norm * normed, axis=0, keepdims=True)
        dshift = jnp.sum(grad_norm, axis=0, keepdims=True)
        dgain_ref[...] = dgain + earlier[6][...] if more else dgain
        dshift_ref[...] = dshift + earlier[7][...] if more else dshift
        dhid_ref[...] = grad_ref[...].astype(jnp.float32) + norm_back(
            normed, scale, gain_ref[...], grad_norm
        )


def mlp_backward(core, grad, hidden, normed, expanded, mlp, gain, earlier=None):
    rows, width = hidden.shape
    blocks, block = (4, width)
    shape = jax.ShapeDtypeStruct
    half = shape((blocks, width, width // 2), jnp.bfloat16)
    row = shape((1, width), jnp.float32)
    outs = (
        shape((rows, width), jnp.float32),
        half,
        half,
        half,
        half,
        shape((blocks, 1, block), jnp.float32),
        row,
        row,
        row,
    )
    halves = pl.BlockSpec((1, width, width // 2), lambda i: (i, 0, 0))
    bias = pl.BlockSpec((1, 1, block), lambda i: (i, 0, 0))
    vector = pl.BlockSpec((1, width), lambda i: (0, 0))
    inputs = [grad, hidden, normed, expanded, mlp, mlp, gain]
    specs = [
        whole(grad),
        whole(hidden),
        whole(normed),
        pl.BlockSpec((rows, block), lambda i: (0, i)),
        FC_BLOCK,
        PROJ_BLOCK,
        whole(gain),
    ]
    summed = [halves, halves, halves, halves, bias, vector, vector, vector]
    if earlier is not None:
        inputs += list(earlier)
        specs += summed
    return pl.pallas_call(
        functools.partial(mlp_backward_kernel, earlier is not None),
        grid=(blocks,),
        out_shape=outs,
        in_specs=[SMEM] + specs,
        out_specs=[pl.BlockSpec((rows, width), lambda i: (0, 0))] + summed,
        scratch_shapes=[
            pltpu.VMEM((rows, width), jnp.bfloat16),
            pltpu.VMEM((width, rows), jnp.bfloat16),
            pltpu.VMEM((rows, width), jnp.float32),
            pltpu.VMEM((rows, block), jnp.bfloat16),
            pltpu.VMEM((rows, block), jnp.bfloat16),
        ],
        compiler_params=params(),
        cost_estimate=cost(8 * rows * width * blocks * block, rows * blocks * block, *inputs, *outs),
        name="mlp_backward",
    )(core, *inputs)


def attention_backward_kernel(
    docs,
    back,
    micro,
    lengths_ref,
    dhid_ref,
    att_ref,
    mixed_ref,
    lse_ref,
    out_ref,
    gmix_ref,
    datt_ref,
    bias_ref,
    delta_ref,
    dq_ref,
):
    count = dhid_ref.shape[0]
    low_grad = dhid_ref[...].astype(jnp.bfloat16)
    datt = dot_transposed(low_grad, out_ref[0]).astype(jnp.bfloat16)
    datt_ref[...] = datt
    product = datt.astype(jnp.float32) * att_ref[...].astype(jnp.float32)
    high = product.astype(jnp.bfloat16)
    rest_low = (product - high.astype(jnp.float32)).astype(jnp.bfloat16)
    feature = lax.broadcasted_iota(jnp.int32, (16, FEATURES), 1)
    head = lax.broadcasted_iota(jnp.int32, (16, FEATURES), 0)
    chosen = ((feature >= head * HD) & (feature < (head + 1) * HD)).astype(jnp.bfloat16)
    delta = dot_transposed(chosen, high) + dot_transposed(chosen, rest_low)
    for index in range(H):
        delta_ref[index] = delta[index : index + 1]
    bias_ref[...] = allowed_bias(count, [lengths_ref[micro, d] for d in range(docs)], docs, 1)

    def one_pair(pair, carry):
        lanes = pl.multiple_of(pair * 2 * HD, 2 * HD)
        dq_ref[...] = jnp.zeros_like(dq_ref)
        for block in range(count // BLOCK):
            keys = slice(block * BLOCK, (block + 1) * BLOCK)
            rows = slice(block * BLOCK, min(count, (block + 1 + back) * BLOCK))
            key = head_split(mixed_ref[keys, pl.ds(FEATURES + lanes, 2 * HD)])
            value = head_split(mixed_ref[keys, pl.ds(2 * FEATURES + lanes, 2 * HD)])
            query = mixed_ref[rows, pl.ds(lanes, 2 * HD)]
            datt_pair = datt_ref[rows, pl.ds(lanes, 2 * HD)]
            scores = dot_transposed(key, query)
            dprobs = dot_transposed(value, datt_pair)
            bias = bias_ref[keys, rows]
            probs_low, dscores_low = ([], [])
            for half in range(2):
                part = slice(half * BLOCK, (half + 1) * BLOCK)
                lse = lse_ref[2 * pair + half, :, rows]
                delta = delta_ref[2 * pair + half, :, rows]
                probs = jnp.exp((scores[part] * 0.125 + bias) - lse)
                dscores = probs * (dprobs[part] - delta)
                probs_low.append(probs.astype(jnp.bfloat16))
                dscores_low.append(dscores.astype(jnp.bfloat16))
            probs_low = jnp.concatenate(probs_low, axis=0)
            dscores_low = jnp.concatenate(dscores_low, axis=0)
            dvalue = head_join(dot(probs_low, datt_pair))
            dkey = head_join(dot(dscores_low, query)) * 0.125
            dq_ref[rows, :] += transposed_dot(dscores_low, key)
            gmix_ref[keys, pl.ds(FEATURES + lanes, 2 * HD)] = dkey.astype(jnp.bfloat16)
            gmix_ref[keys, pl.ds(2 * FEATURES + lanes, 2 * HD)] = dvalue.astype(jnp.bfloat16)
        gmix_ref[:, pl.ds(lanes, 2 * HD)] = (dq_ref[...] * 0.125).astype(jnp.bfloat16)
        return carry

    lax.fori_loop(0, H // 2, one_pair, 0)


def attention_backward(micro, lengths, dhid, count, back, att, mixed, lse, weight):
    width = dhid.shape[1]
    docs = lengths.shape[1]
    outs = jax.ShapeDtypeStruct((count, 3 * width), jnp.bfloat16)
    inputs = [dhid, att, mixed, lse, weight]
    return pl.pallas_call(
        functools.partial(attention_backward_kernel, docs, back, micro),
        grid=(1,),
        out_shape=outs,
        in_specs=[
            SMEM,
            pl.BlockSpec((count, width), lambda i: (micro, 0)),
            pl.BlockSpec((count, width), lambda i: (micro, 0)),
            pl.BlockSpec((count, 3 * width), lambda i: (micro, 0)),
            pl.BlockSpec((H, 1, count), lambda i: (micro, 0, 0)),
            pl.BlockSpec((1, width, width), lambda i: (3, 0, 0)),
        ],
        out_specs=pl.BlockSpec((count, 3 * width), lambda i: (0, 0)),
        scratch_shapes=[
            pltpu.VMEM((count, width), jnp.bfloat16),
            pltpu.VMEM((count, count), jnp.float32),
            pltpu.VMEM((H, 1, count), jnp.float32),
            pltpu.VMEM((count, 2 * HD), jnp.float32),
        ],
        compiler_params=params(),
        cost_estimate=cost(
            2 * count * width * width + 10 * count * count * width, count * count * H, outs, outs
        ),
        name="attention_backward",
    )(lengths, *inputs)


def attention_terms_kernel(more, micro, core_ref, normed_ref, att_ref, dhid_ref, *rest):
    gmix_refs, rest = (rest[:micro], rest[micro:])
    earlier = rest[:3] if more else (None,) * 3
    if more:
        rest = rest[3:]
    mine_ref, theirs_ref, dbias_ref, left_t, right_ref = rest
    step = pl.program_id(0)
    core = core_ref[0]

    @pl.when(step == 0)
    def _():
        left_t[...] = jnp.transpose(normed_ref[...])

    @pl.when(step < 3)
    def _():
        for index, gmix_ref in enumerate(gmix_refs):
            count = gmix_ref.shape[0]
            right_ref[index * count : (index + 1) * count] = gmix_ref[...]

    @pl.when(step == 3)
    def _():
        left_t[...] = jnp.transpose(att_ref[...])
        right_ref[...] = dhid_ref[...].astype(jnp.bfloat16)

    right = right_ref[...]
    dbias = jnp.sum(right.astype(jnp.float32), axis=0, keepdims=True)
    dbias_ref[0] = dbias + earlier[2][0] if more else dbias
    store_halves(
        core, dot(left_t[...], right), mine_ref, theirs_ref, earlier[:2] if more else None
    )


def attention_terms(core, normed, att, gmix, dhid, earlier=None):
    rows, width = dhid.shape
    shape = jax.ShapeDtypeStruct
    outs = (
        shape((4, width, width // 2), jnp.bfloat16),
        shape((4, width, width // 2), jnp.bfloat16),
        shape((4, 1, width), jnp.float32),
    )
    halves = pl.BlockSpec((1, width, width // 2), lambda i: (i, 0, 0))
    summed = [halves, halves, pl.BlockSpec((1, 1, width), lambda i: (i, 0, 0))]
    inputs = [normed, att, dhid, *gmix]
    specs = [whole(normed), whole(att), whole(dhid)] + [
        pl.BlockSpec((part.shape[0], width), lambda i: (0, jnp.minimum(i, 2))) for part in gmix
    ]
    if earlier is not None:
        inputs += list(earlier)
        specs += summed
    return pl.pallas_call(
        functools.partial(attention_terms_kernel, earlier is not None, len(gmix)),
        grid=(4,),
        out_shape=outs,
        in_specs=[SMEM] + specs,
        out_specs=summed,
        scratch_shapes=[
            pltpu.VMEM((width, rows), jnp.bfloat16),
            pltpu.VMEM((rows, width), jnp.bfloat16),
        ],
        compiler_params=params(),
        cost_estimate=cost(8 * rows * width * width, 0, *inputs, *outs),
        name="attention_terms",
    )(core, *inputs)


def attention_input_kernel(more, micro, dhid_ref, state_ref, weight_ref, gain_ref, *rest):
    gmix_refs, rest = (rest[:micro], rest[micro:])
    earlier = rest[:2] if more else None
    if more:
        rest = rest[2:]
    grad_ref, dgain_ref, dshift_ref, gmix_ref = rest
    step = pl.program_id(0)
    each = pl.num_programs(0) // micro
    for index, part_ref in enumerate(gmix_refs):

        @pl.when(step // each == index)
        def _(part_ref=part_ref):
            gmix_ref[...] = part_ref[...]

    grad_norm = dot_transposed(gmix_ref[:, :FEATURES], weight_ref[0])
    for part in range(1, 3):
        grad_norm = grad_norm + dot_transposed(
            gmix_ref[:, part * FEATURES : (part + 1) * FEATURES], weight_ref[part]
        )
    normed, scale = norm_parts(state_ref[...].astype(jnp.float32))
    dgain = jnp.sum(grad_norm * normed, axis=0, keepdims=True)
    dshift = jnp.sum(grad_norm, axis=0, keepdims=True)

    @pl.when(step == 0)
    def _():
        dgain_ref[...] = dgain + earlier[0][...] if more else dgain
        dshift_ref[...] = dshift + earlier[1][...] if more else dshift

    @pl.when(step > 0)
    def _():
        dgain_ref[...] += dgain
        dshift_ref[...] += dshift

    grad = dhid_ref[...] + norm_back(normed, scale, gain_ref[...], grad_norm)
    grad_ref[...] = grad.astype(grad_ref.dtype)


def attention_input(dhid, state, gmix, weight, gain, kind, earlier=None, chunk=256):
    rows, width = dhid.shape
    shape = jax.ShapeDtypeStruct
    vector = pl.BlockSpec((1, width), lambda i: (0, 0))
    outs = (shape((rows, width), kind), shape((1, width), jnp.float32), shape((1, width), jnp.float32))
    inputs = [dhid, state, weight, gain, *gmix]
    each = rows // chunk // len(gmix)
    specs = [
        rows_of(chunk, width),
        rows_of(chunk, width),
        pl.BlockSpec((3, width, width), lambda i: (0, 0, 0), pipeline_mode=pl.Buffered(1)),
        whole(gain),
    ]
    for index in range(len(gmix)):
        specs.append(
            pl.BlockSpec(
                (chunk, 3 * width),
                lambda i, index=index: (jnp.clip(i - index * each, 0, each - 1), 0),
            )
        )
    if earlier is not None:
        inputs += list(earlier)
        specs += [vector, vector]
    return pl.pallas_call(
        functools.partial(attention_input_kernel, earlier is not None, len(gmix)),
        grid=(rows // chunk,),
        out_shape=outs,
        in_specs=specs,
        out_specs=[rows_of(chunk, width), vector, vector],
        scratch_shapes=[pltpu.VMEM((chunk, 3 * width), jnp.bfloat16)],
        compiler_params=params(),
        cost_estimate=cost(6 * rows * width * width, 0, *inputs, *outs),
        name="attention_input",
    )(*inputs)


def place_small_kernel(sizes, me_ref, small_ref, *outs):
    dp = me_ref[0] // 2
    slot = lax.broadcasted_iota(jnp.int32, (16, 1), 0)
    owner = ((slot % 4) * 4 + (slot // 8) * 2 + slot // 4 % 2) ^ dp
    for index, (size, out_ref) in enumerate(zip(sizes, outs)):
        width = 16 * size
        lane = lax.broadcasted_iota(jnp.int32, (256, width), 0)
        column = lax.broadcasted_iota(jnp.int32, (256, width), 1)
        spread = (column % size == lane).astype(jnp.bfloat16)
        rows = jnp.concatenate([small_ref[d, index : index + 1] for d in range(16)], axis=0)
        spread_rows = dot(rows, spread)
        column = lax.broadcasted_iota(jnp.int32, (1, width), 1)
        out_ref[...] = jnp.sum(
            jnp.where(column // size == owner, spread_rows, 0.0), axis=0, keepdims=True
        )


def place_small(me, small, sizes):
    return pl.pallas_call(
        functools.partial(place_small_kernel, sizes),
        out_shape=[jax.ShapeDtypeStruct((1, 16 * size), jnp.float32) for size in sizes],
        in_specs=[SMEM, pl.BlockSpec(memory_space=pltpu.VMEM)],
        out_specs=[pl.BlockSpec(memory_space=pltpu.VMEM)] * len(sizes),
        name="place_small",
    )(me, small)


def swap(value, bits):
    return lax.ppermute(value, BOTH, [(i, i ^ bits) for i in range(32)])


CORE, X, Y, Z1, Z2, Z3 = (1, 2, 4, 8, 16, 24)


def place_kernel(slots, me_ref, *refs):
    sources, (out, sems) = (refs[: len(slots)], refs[len(slots) :])
    me = me_ref[0]
    copies = []
    for source, rels in zip(sources, slots):
        for inner, rel in enumerate(rels):
            copies.append(
                pltpu.make_async_copy(
                    source.at[inner], out.at[:, rel ^ me], sems.at[len(copies)]
                )
            )
    for copy in copies:
        copy.start()
    for copy in copies:
        copy.wait()


def place(me, sources, slots):
    placed = pl.pallas_call(
        functools.partial(place_kernel, slots),
        out_shape=jax.ShapeDtypeStruct((4, 32, 24, FEATURES), jnp.bfloat16),
        in_specs=[SMEM] + [pl.BlockSpec(memory_space=pl.ANY)] * len(sources),
        out_specs=pl.BlockSpec(memory_space=pltpu.VMEM),
        scratch_shapes=[pltpu.SemaphoreType.DMA((32,))],
        name="place",
    )(me, *sources)
    return placed.reshape(4, FEATURES, FEATURES)


def after(values, *others):
    return lax.optimization_barrier((values, others))[0]


def gather_first(piece, me):
    base = (0, Z1, Z2, Z3)
    pieces = lax.optimization_barrier(
        (piece, swap(piece, Z1), swap(piece, Z2), swap(piece, Z3))
    )
    four = jnp.concatenate(pieces)
    four_x, four_y = (swap(four, X), swap(four, Y))
    four_core = swap(four, CORE)
    four_x, four_y, four_core = lax.optimization_barrier((four_x, four_y, four_core))
    near_xy, far_xy = (swap(four_y[:2], X), swap(four_x[2:], Y))
    x_core, y_core = (swap(four_x, CORE), swap(four_y, CORE))
    near_xy, far_xy, x_core, y_core = lax.optimization_barrier((near_xy, far_xy, x_core, y_core))
    parts = [four, four_x, four_y, near_xy, far_xy]
    parts += [four_core, x_core, y_core, swap(near_xy, CORE), swap(far_xy, CORE)]
    slots = [base] + [tuple(rel ^ bits for rel in base) for bits in (X, Y)]
    slots += [(X ^ Y, X ^ Y ^ Z1), (X ^ Y ^ Z2, X ^ Y ^ Z3)]
    slots += [tuple(rel ^ CORE for rel in rels) for rels in slots]
    return (place(me, parts, slots), pieces[1], four_x)


def pick(array, axis, index):
    return lax.dynamic_index_in_dim(array, index, axis, keepdims=False)


def low(value):
    return value.astype(jnp.bfloat16)


def wide(value):
    return value.astype(jnp.float32)


def add(*terms):
    total = wide(terms[0])
    for term in terms[1:]:
        total = total + wide(term)
    return total


class Reduction:
    def __init__(self, spot, views, theirs):
        self.z_pair, self.z_low, self.y, self.x, self.core = spot
        self.views = [[self.by_device(view)] for view in views]
        for terms, part in zip(self.views, theirs):
            terms.append(self.by_device(swap(part[0], CORE), part[1]))

    @staticmethod
    def by_device(view, change=None):
        view = view if change is None else change(view)
        return view.reshape(2, 2, 2, 2, *view.shape[1:])

    def sums(self, pieces, extra=None):
        total = jnp.concatenate([add(*terms) for terms in pieces], axis=-2)
        return total if extra is None else total + wide(extra)

    def chosen(self, pieces, axis, index):
        return [[pick(term, axis, index) for term in terms] for terms in pieces]

    def first(self):
        near = self.chosen(self.views, 0, self.z_pair)
        far = self.chosen(self.views, 0, 1 - self.z_pair)
        near_sent = low(self.sums(self.chosen(near, 2, 1 - self.x)))
        far_sent = low(self.sums(self.chosen(far, 1, 1 - self.y)))
        self.near = self.chosen(near, 2, self.x)
        self.far = self.chosen(far, 1, self.y)
        self.near_in, self.far_in = (swap(near_sent, X), swap(far_sent, Y))
        return (near_sent, far_sent)

    def second(self):
        near, far = (self.near, self.far)
        near_sent = low(
            self.sums(self.chosen(near, 1, 1 - self.y), pick(self.near_in, 1, 1 - self.y))
        )
        far_sent = low(
            self.sums(self.chosen(far, 1, 1 - self.x), pick(self.far_in, 1, 1 - self.x))
        )
        near = self.sums(self.chosen(near, 1, self.y), pick(self.near_in, 1, self.y))
        far = self.sums(self.chosen(far, 1, self.x), pick(self.far_in, 1, self.x))
        self.near, self.far = (low(near), low(far))
        self.near_in, self.far_in = (swap(near_sent, Y), swap(far_sent, X))
        return (near_sent, far_sent)

    def third(self):
        near, far = ((self.near, self.near_in), (self.far, self.far_in))

        def summed(pair, index):
            return add(*[pick(term, 0, index) for term in pair])

        sent = low(jnp.stack([summed(near, 1 - self.z_low), summed(far, 1 - self.z_low)]))
        self.kept = (summed(near, self.z_low), summed(far, self.z_low))
        self.back = swap(sent, Z1)
        return sent

    def last(self):
        far = low(self.kept[1] + wide(self.back[1]))
        half = self.kept[0] + wide(self.back[0]) + wide(swap(far, Z2))
        other = swap(half, CORE)
        core = self.core
        return jnp.where(core == 0, jnp.stack([half, other], -2), jnp.stack([other, half], -2))


def blocks_first(array):
    view = array.reshape(4, 16, 48, array.shape[2])
    return jnp.transpose(view, (1, 0, 2, 3)).reshape(16, 192, array.shape[2])


def rows_first(array):
    return array.reshape(16, 192, array.shape[2])


def reduce_small(small, dp):
    small = jnp.concatenate([part.reshape(-1, FEATURES) for part in small])
    for bits in (CORE, X, Y, Z1, Z2):
        small = small + swap(small, bits)

    def own(start, rows):
        vector = small[start : start + rows].reshape(-1)
        size = vector.shape[0] // 16
        return lax.dynamic_slice_in_dim(vector, dp * size, size)

    return [own(0, 1), own(1, 1), own(2, 3), own(5, 1), own(6, 1), own(7, 1), own(8, 4), own(12, 1)]


def gather_small(pieces, me):
    sizes = tuple(piece.shape[0] for piece in pieces)
    small = jnp.stack([jnp.pad(piece, (0, 256 - piece.shape[0])) for piece in pieces])[None]
    for bits in (Z1, Z2, X, Y):
        small = jnp.concatenate([small, swap(small, bits)])
    return place_small(me, small, sizes)


def gather_all(weights, spot, me):
    gain_a, shift_a, qkv, qbias, out, obias, gain_m, shift_m, fc, fbias, proj, pbias = weights
    core = spot[4]

    def half(weight):
        part = lax.dynamic_slice_in_dim(weight, core * 24, 24, 0)
        return jnp.transpose(part.reshape(24, -1, FEATURES), (1, 0, 2))

    columns = lax.dynamic_slice_in_dim(fc, core * 2 * FEATURES, 2 * FEATURES, 1)
    columns = jnp.transpose(columns.reshape(48, 2, FEATURES), (1, 0, 2))
    across = lax.dynamic_slice_in_dim(proj, core * 96, 96, 0).reshape(2, 48, FEATURES)
    mlp = lax.all_gather(jnp.concatenate([columns, across]), BOTH)
    mlp = mlp.reshape(16, 2, 4, 48, FEATURES)
    first, early, later = gather_first(jnp.concatenate([half(qkv), half(out)])[None], me)
    vectors = [gain_a, shift_a, qbias, obias, gain_m, shift_m, fbias, pbias]
    return (first, mlp, *gather_small(after(vectors, early), me))


def gather_plain(weights):
    whole_ones = [lax.all_gather(weight, "dp", axis=0, tiled=True) for weight in weights]
    gain_a, shift_a, qkv, qbias, out, obias, gain_m, shift_m, fc, fbias, proj, pbias = whole_ones

    def blocks(weight):
        return jnp.transpose(weight.reshape(FEATURES, -1, FEATURES), (1, 0, 2))

    rows = [
        wide(v).reshape(1, -1)
        for v in (gain_a, shift_a, qbias, obias, gain_m, shift_m, fbias, pbias)
    ]
    first = jnp.concatenate([blocks(qkv), blocks(out)])
    fc = blocks(fc).reshape(2, 2, 16, 48, FEATURES)
    fc = jnp.transpose(fc, (2, 0, 1, 3, 4))
    mlp = jnp.concatenate([fc, proj.reshape(16, 2, 2, 48, FEATURES)], axis=2)
    return (first, mlp, *rows)


def reduce_plain(terms):
    matrices, small = terms

    def joined(pair):
        return wide(jnp.concatenate(pair, axis=2))

    def sides(blocks):
        return jnp.transpose(blocks, (1, 0, 2)).reshape(FEATURES, -1)

    first, fc, proj = [joined(pair) for pair in matrices]
    gain_a, shift_a, bias_a, gain_m, shift_m, fbias, pbias = small
    values = (
        gain_a.reshape(-1), shift_a.reshape(-1), sides(first[:3]), bias_a[:3].reshape(-1), first[3],
        bias_a[3].reshape(-1), gain_m.reshape(-1), shift_m.reshape(-1), sides(fc), fbias.reshape(-1),
        proj.reshape(-1, FEATURES), pbias.reshape(-1),
    )
    return tuple(
        wide(lax.psum(low(lax.psum_scatter(v, "dp", scatter_dimension=0, tiled=True)), "rep"))
        for v in values
    )


def forward(tokens, lengths, count, back, weights):
    weight, mlp, gain_a, shift_a, qbias, obias, gain_m, shift_m, fbias, pbias = weights
    state, kept = (tokens, [])
    for use in range(USES):
        normed_a, mixed, att, lse, hidden, normed_m = attention_forward(
            lengths, state, count, back, gain_a, shift_a, weight, qbias, obias, gain_m, shift_m
        )
        expanded, after_mlp = mlp_forward(hidden, normed_m, mlp, fbias, pbias, use == USES - 1)
        kept.append((state, normed_a, mixed, att, lse, hidden, normed_m, expanded))
        state = after_mlp
    return (state, kept)


def shards(custom, tokens, doc_lengths, cotangent, *weights):
    micro, count, width = tokens.shape
    dp, core = (lax.axis_index("dp"), lax.axis_index("rep"))
    spot = (dp // 8, dp // 4 % 2, dp // 2 % 2, dp % 2, core)
    me = (dp * 2 + core).astype(jnp.int32).reshape(1)
    side = core.astype(jnp.int32).reshape(1) if custom else jnp.zeros((1,), jnp.int32)
    back = -(-(LONGEST - 1) // BLOCK)
    lengths = doc_lengths.reshape(micro, doc_lengths.shape[-1])
    whole_ones = gather_all(weights, spot, me) if custom else gather_plain(weights)
    state, kept = forward(
        tokens.reshape(micro * count, width), lengths, count, back, whole_ones
    )
    weight, mlp, gain_a, gain_m = (whole_ones[0], whole_ones[1], whole_ones[2], whole_ones[6])
    grad, mlp_terms, terms, norm = (cotangent.reshape(micro * count, width), None, None, None)
    for use in range(USES - 1, -1, -1):
        before, normed_a, mixed, att, lse, hidden, normed_m, expanded = kept[use]
        dhid, *mlp_terms = mlp_backward(
            side, grad, hidden, normed_m, expanded, mlp, gain_m, mlp_terms
        )
        sending = custom and use == 0
        if sending:
            fc_mine, fc_theirs, proj_mine, proj_theirs = mlp_terms[:4]
            sums = Reduction(
                spot,
                (blocks_first(fc_mine), rows_first(proj_mine)),
                ((fc_theirs, blocks_first), (proj_theirs, rows_first)),
            )
        gmix = []
        for index in range(micro):
            if sending and index == micro - 1:
                dhid, *unused = after((dhid, gmix), sums.first())
                gmix = list(unused[0])
            gmix.append(
                attention_backward(index, lengths, dhid, count, back, att, mixed, lse, weight)
            )
        terms = attention_terms(side, normed_a, att, gmix, dhid, terms)
        if sending:
            gmix, terms, unused = lax.optimization_barrier((gmix, terms, sums.second()))
            attention_sums = Reduction(
                spot, (blocks_first(terms[0]),), ((terms[1], blocks_first),)
            )
        kind = jnp.float32 if use else jnp.bfloat16
        grad, *norm = attention_input(dhid, before, gmix, weight, gain_a, kind, norm)
    small = (norm[0], norm[1], terms[2], mlp_terms[6], mlp_terms[7], mlp_terms[4], mlp_terms[5])
    if custom:
        sums.third()
        attention_sums.first()
        attention_sums.second()
        attention_sums.third()
        fc, proj = jnp.split(sums.last(), 2)
        first = attention_sums.last()

        def columns(array):
            return jnp.transpose(array.reshape(4, 48, width), (1, 0, 2)).reshape(48, 4 * width)

        first = columns(first)
        gain_a, shift_a, qbias, obias, gain_m, shift_m, fbias, pbias = reduce_small(small, dp)
        final = (
            gain_a, shift_a, first[:, : 3 * width], qbias, first[:, 3 * width :], obias,
            gain_m, shift_m, columns(fc), fbias, proj.reshape(192, width), pbias,
        )
    else:
        matrices = (terms[:2], mlp_terms[:2], mlp_terms[2:4])
        final = reduce_plain((matrices, small))
    return (state.reshape(tokens.shape), grad.reshape(tokens.shape), *final)


def solution(mesh):
    custom = mesh.shape["dp"] == 16 and mesh.shape["rep"] == 2
    placed = tuple(
        P("dp", None) if index in (2, 4, 8, 10) else P("dp") for index in range(12)
    )
    rows = P(None, BOTH, None)
    return jax.shard_map(
        functools.partial(shards, custom),
        mesh=mesh,
        in_specs=(rows, rows, rows, *placed),
        out_specs=(rows, rows, *placed),
        check_vma=False,
    )
```

```python
import functools
import math

import jax
import jax.numpy as jnp
from jax import lax
from jax.experimental import pallas as pl
from jax.experimental.pallas import tpu as pltpu
from jax.sharding import PartitionSpec as P

H = 12
HD = 64
USES = 2
LONGEST = 256
BOTH = ("dp", "rep")


NORM_EPS = 1e-05
BLOCK = 128
FEATURES = H * HD
VMEM_LIMIT = 40 << 20
COST_SCALE = 8


def dot(left, right):
    return jnp.dot(left, right, preferred_element_type=jnp.float32)


def transposed_dot(left, right):
    return lax.dot_general(
        left, right, (((0,), (0,)), ((), ())), preferred_element_type=jnp.float32
    )


def dot_transposed(left, right):
    return lax.dot_general(
        left, right, (((1,), (1,)), ((), ())), preferred_element_type=jnp.float32
    )


def norm_parts(values):
    center = values - jnp.mean(values, axis=-1, keepdims=True)
    spread = jnp.mean(center * center, axis=-1, keepdims=True)
    scale = lax.rsqrt(spread + NORM_EPS)
    return (center * scale, scale)


def norm_back(normed, scale, gain, grad):
    inner = grad * gain
    first = jnp.mean(inner, axis=-1, keepdims=True)
    second = jnp.mean(inner * normed, axis=-1, keepdims=True)
    return (inner - first - normed * second) * scale


def segment_of(places, lengths, docs):
    end = jnp.int32(0)
    segment = jnp.zeros(places.shape, jnp.int32)
    for doc in range(docs):
        end = end + lengths[doc]
        segment = segment + (places >= end).astype(jnp.int32)
    return segment


def allowed_bias(count, lengths, docs, query_axis):
    query_shape = (count, 1) if query_axis == 0 else (1, count)
    key_shape = (1, count) if query_axis == 0 else (count, 1)
    query = lax.broadcasted_iota(jnp.int32, query_shape, query_axis)
    key = lax.broadcasted_iota(jnp.int32, key_shape, 1 - query_axis)
    same = segment_of(query, lengths, docs) == segment_of(key, lengths, docs)
    return jnp.where(same & (key <= query), 0.0, -1e30).astype(jnp.float32)


GROUP = 4
LANES = GROUP * HD


def head_split(array):
    head = lax.broadcasted_iota(jnp.int32, array.shape, 1) // HD
    zero = jnp.zeros_like(array)
    return jnp.concatenate([jnp.where(head == h, array, zero) for h in range(GROUP)], axis=0)


def head_join(stacked):
    count = stacked.shape[0] // GROUP
    head = lax.broadcasted_iota(jnp.int32, (count, LANES), 1) // HD
    joined = stacked[:count]
    for h in range(1, GROUP):
        joined = jnp.where(head == h, stacked[h * count : (h + 1) * count], joined)
    return joined


def attention_forward_kernel(
    docs,
    back,
    lengths_ref,
    state_ref,
    gain_ref,
    shift_ref,
    weight_ref,
    qbias_ref,
    obias_ref,
    gain2_ref,
    shift2_ref,
    normed_ref,
    mixed_ref,
    att_ref,
    lse_ref,
    hidden_ref,
    normed2_ref,
    bias_ref,
    lse_cols,
):
    micro = pl.program_id(0)
    state = state_ref[...].astype(jnp.float32)
    count = state.shape[0]
    normed = (norm_parts(state)[0] * gain_ref[...] + shift_ref[...]).astype(jnp.bfloat16)
    normed_ref[...] = normed
    for part in range(3):
        columns = slice(part * FEATURES, (part + 1) * FEATURES)
        mixed_ref[:, columns] = (dot(normed, weight_ref[part]) + qbias_ref[:, columns]).astype(
            jnp.bfloat16
        )
    bias_ref[...] = allowed_bias(count, [lengths_ref[micro, d] for d in range(docs)], docs, 0)
    lse_cols[...] = jnp.zeros_like(lse_cols)

    def one_group(group, carry):
        lanes = pl.multiple_of(group * LANES, LANES)
        for block in range(count // BLOCK):
            rows = slice(block * BLOCK, (block + 1) * BLOCK)
            low_key = max(0, block - back) * BLOCK
            keys = slice(low_key, (block + 1) * BLOCK)
            query = head_split(mixed_ref[rows, pl.ds(lanes, LANES)])
            key = mixed_ref[keys, pl.ds(FEATURES + lanes, LANES)]
            value = mixed_ref[keys, pl.ds(2 * FEATURES + lanes, LANES)]
            scores = dot_transposed(query, key)
            bias = bias_ref[rows, keys]
            scores = scores * 0.125 + jnp.concatenate([bias] * GROUP, axis=0)
            top = jnp.max(scores, axis=-1, keepdims=True)
            expo = jnp.exp(scores - top)
            total_expo = jnp.sum(expo, axis=-1, keepdims=True)
            result = dot(expo.astype(jnp.bfloat16), value) / total_expo
            att_ref[rows, pl.ds(lanes, LANES)] = head_join(result).astype(jnp.bfloat16)
            lse = top + jnp.log(total_expo)
            lane = lax.broadcasted_iota(jnp.int32, (BLOCK, 128), 1)
            for h in range(GROUP):
                lse_cols[rows, :] += jnp.where(
                    lane == GROUP * group + h, lse[h * BLOCK : (h + 1) * BLOCK], 0.0
                )
        return carry

    lax.fori_loop(0, H // GROUP, one_group, 0, unroll=H // GROUP)
    lse = jnp.transpose(lse_cols[...])
    for index in range(H):
        lse_ref[index] = lse[index : index + 1]
    hidden = state + (dot(att_ref[...], weight_ref[3]) + obias_ref[...])
    hidden_ref[...] = hidden
    normed2_ref[...] = (norm_parts(hidden)[0] * gain2_ref[...] + shift2_ref[...]).astype(
        jnp.bfloat16
    )


def whole(array):
    dims = len(array.shape)
    return pl.BlockSpec(array.shape, lambda *unused: (0,) * dims, pipeline_mode=pl.Buffered(1))


SMEM = pl.BlockSpec(memory_space=pltpu.SMEM)


def in_hbm(arrays):
    return [pltpu.with_memory_space_constraint(array, pltpu.HBM) for array in arrays]


def rows_of(count, width):
    return pl.BlockSpec((count, width), lambda i: (i, 0))


def params(limit=VMEM_LIMIT):
    return pltpu.CompilerParams(vmem_limit_bytes=limit)


def cost(flops, transcendentals, *arrays):
    size = sum(math.prod(a.shape) * a.dtype.itemsize for a in arrays)
    return pl.CostEstimate(
        flops=int(flops) // COST_SCALE,
        transcendentals=int(transcendentals) // COST_SCALE,
        bytes_accessed=int(size) // COST_SCALE,
    )


def attention_forward(lengths, state, count, back, gain, shift, weight, qbias, obias, gain2, shift2):
    rows = state.shape[0]
    micro, docs = lengths.shape
    width = FEATURES
    shape = pltpu.HBM
    outs = (
        shape((rows, width), jnp.bfloat16),
        shape((rows, 3 * width), jnp.bfloat16),
        shape((rows, width), jnp.bfloat16),
        shape((micro * H, 1, count), jnp.float32),
        shape((rows, width), jnp.float32),
        shape((rows, width), jnp.bfloat16),
    )
    weights = (gain, shift, weight, qbias, obias, gain2, shift2)
    return pl.pallas_call(
        functools.partial(attention_forward_kernel, docs, back),
        grid=(micro,),
        out_shape=outs,
        in_specs=[SMEM, rows_of(count, width)] + [whole(w) for w in weights],
        out_specs=(
            rows_of(count, width),
            rows_of(count, 3 * width),
            rows_of(count, width),
            pl.BlockSpec((H, 1, count), lambda i: (i, 0, 0)),
            rows_of(count, width),
            rows_of(count, width),
        ),
        scratch_shapes=[
            pltpu.VMEM((count, count), jnp.float32),
            pltpu.VMEM((count, 128), jnp.float32),
        ],
        compiler_params=params(),
        cost_estimate=cost(
            8 * rows * width * width + 4 * rows * count * width, rows * count * H, state, *weights, *outs
        ),
        name="attention_forward",
    )(lengths, *in_hbm((state, *weights)))


GELU_C = 0.7978845608028654
GELU_K = 0.044715 * GELU_C


def gelu_gate(value):
    square = value * value
    gate = 0.5 * jnp.tanh(value * (GELU_C + GELU_K * square)) + 0.5
    return (gate, square)


def mlp_forward_kernel(
    last, hidden_ref, normed_ref, fc_ref, fbias_ref, proj_ref, pbias_ref, expanded_ref, *rest
):
    final_ref, state_ref = rest if last else (None, rest[0])
    step = pl.program_id(0)
    chunk = 256

    @pl.when(step == 0)
    def _():
        state_ref[...] = hidden_ref[...] + pbias_ref[...]

    for start in range(0, normed_ref.shape[0], chunk):
        rows = slice(start, start + chunk)
        expanded = dot(normed_ref[rows, :], square_of(fc_ref)) + fbias_ref[...]
        expanded_ref[rows, :] = expanded.astype(expanded_ref.dtype)
        gate, unused = gelu_gate(expanded)
        activated = (expanded * gate).astype(jnp.bfloat16)
        state_ref[rows, :] += dot(activated, square_of(proj_ref))

    if last:

        @pl.when(step == pl.num_programs(0) - 1)
        def _():
            final_ref[...] = state_ref[...].astype(jnp.bfloat16)


DEVICE_GROUPS = 16


def square_of(ref):
    return ref[...].reshape(FEATURES, FEATURES)


FC_BLOCK = pl.BlockSpec((16, 1, 1, 48, FEATURES), lambda i: (0, i // 2, i % 2, 0, 0))
PROJ_BLOCK = pl.BlockSpec((4, 2, 2, 48, FEATURES), lambda i: (i, 0, 1, 0, 0))


def mlp_forward(hidden, normed, mlp, fbias, pbias, last):
    rows, width = hidden.shape
    block = width
    hidden_units = 4 * block
    shape = pltpu.HBM
    outs = (
        shape((rows, hidden_units), jnp.bfloat16),
        shape((rows, width), jnp.bfloat16 if last else jnp.float32),
    )
    specs = (
        pl.BlockSpec((rows, block), lambda i: (0, i)),
        pl.BlockSpec((rows, width), lambda i: (0, 0)),
    )
    return pl.pallas_call(
        functools.partial(mlp_forward_kernel, last),
        grid=(hidden_units // block,),
        out_shape=outs,
        in_specs=[
            whole(hidden),
            whole(normed),
            FC_BLOCK,
            pl.BlockSpec((1, block), lambda i: (0, i)),
            PROJ_BLOCK,
            whole(pbias),
        ],
        out_specs=specs,
        scratch_shapes=[pltpu.VMEM((rows, width), jnp.float32)] if last else [],
        compiler_params=params(),
        cost_estimate=cost(
            4 * rows * width * hidden_units, rows * hidden_units, hidden, normed, mlp, *outs
        ),
        name="mlp_forward",
    )(*in_hbm((hidden, normed, mlp, fbias, mlp, pbias)))


def transposed_dot(left, right):
    return lax.dot_general(
        left, right, (((0,), (0,)), ((), ())), preferred_element_type=jnp.float32
    )


def dot_transposed(left, right):
    return lax.dot_general(
        left, right, (((1,), (1,)), ((), ())), preferred_element_type=jnp.float32
    )


def store_halves(core, value, mine_ref, theirs_ref, earlier):
    half = value.shape[1] // 2
    left, right = (value[:, :half], value[:, half:])
    mine = jnp.where(core == 0, left, right)
    theirs = jnp.where(core == 0, right, left)
    shape = mine_ref.shape
    mine, theirs = (mine.reshape(shape), theirs.reshape(shape))
    if earlier is not None:
        mine = mine + earlier[0][...].astype(jnp.float32)
        theirs = theirs + earlier[1][...].astype(jnp.float32)
    mine_ref[...] = mine.astype(mine_ref.dtype)
    theirs_ref[...] = theirs.astype(theirs_ref.dtype)


def mlp_backward_kernel(
    more,
    core_ref,
    grad_ref,
    hidden_ref,
    normed_ref,
    att_ref,
    expanded_ref,
    fc_ref,
    proj_ref,
    gain_ref,
    *rest,
):
    earlier = rest[:11] if more else (None,) * 11
    if more:
        rest = rest[11:]
    (
        dhid_ref,
        fc_mine,
        fc_theirs,
        proj_mine,
        proj_theirs,
        out_mine,
        out_theirs,
        dobias_ref,
        dfbias_ref,
        dpbias_ref,
        dgain_ref,
        dshift_ref,
        low_ref,
        normed_t,
        acc_ref,
        act_ref,
        ge_ref,
    ) = rest
    step = pl.program_id(0)
    core = core_ref[0]
    rows = grad_ref.shape[0]
    chunk = 256

    @pl.when(step == 0)
    def _():
        low_grad = grad_ref[...].astype(jnp.bfloat16)
        low_ref[...] = low_grad
        dpbias = jnp.sum(low_grad.astype(jnp.float32), axis=0, keepdims=True)
        dpbias_ref[...] = dpbias + earlier[8][...] if more else dpbias
        normed_t[...] = jnp.transpose(normed_ref[...])
        acc_ref[...] = jnp.zeros_like(acc_ref)

    bias_sum = jnp.zeros(dfbias_ref.shape[1:], jnp.float32)
    for start in range(0, rows, chunk):
        part = slice(start, start + chunk)
        grad_act = dot_transposed(low_ref[part, :], square_of(proj_ref))
        value = expanded_ref[part, :].astype(jnp.float32)
        gate, square = gelu_gate(value)
        act = value * gate
        slope = gate + act * (1.0 - gate) * (2 * GELU_C + 6 * GELU_K * square)
        act_ref[part, :] = act.astype(jnp.bfloat16)
        grad_exp = (grad_act * slope).astype(jnp.bfloat16)
        ge_ref[part, :] = grad_exp
        bias_sum = bias_sum + jnp.sum(grad_exp.astype(jnp.float32), axis=0, keepdims=True)
        acc_ref[part, :] += dot_transposed(grad_exp, square_of(fc_ref))
    dfbias_ref[0] = bias_sum + earlier[7][0] if more else bias_sum
    dproj = transposed_dot(act_ref[...], low_ref[...])
    store_halves(core, dproj, proj_mine, proj_theirs, earlier[2:4] if more else None)
    dfc = dot(normed_t[...], ge_ref[...])
    store_halves(core, dfc, fc_mine, fc_theirs, earlier[:2] if more else None)

    @pl.when(step == pl.num_programs(0) - 1)
    def _():
        normed, scale = norm_parts(hidden_ref[...])
        grad_norm = acc_ref[...]
        dgain = jnp.sum(grad_norm * normed, axis=0, keepdims=True)
        dshift = jnp.sum(grad_norm, axis=0, keepdims=True)
        dgain_ref[...] = dgain + earlier[9][...] if more else dgain
        dshift_ref[...] = dshift + earlier[10][...] if more else dshift
        dhid = grad_ref[...].astype(jnp.float32) + norm_back(
            normed, scale, gain_ref[...], grad_norm
        )
        dhid_ref[...] = dhid
        low_dhid = dhid.astype(jnp.bfloat16)
        low_ref[...] = low_dhid
        dobias = jnp.sum(low_dhid.astype(jnp.float32), axis=0, keepdims=True)
        dobias_ref[...] = dobias + earlier[6][...] if more else dobias
        dout = transposed_dot(att_ref[...], low_ref[...])
        store_halves(core, dout, out_mine, out_theirs, earlier[4:6] if more else None)


def mlp_backward(core, grad, hidden, normed, att, expanded, mlp, gain, earlier=None):
    rows, width = hidden.shape
    blocks, block = (4, width)
    shape = pltpu.HBM
    groups = DEVICE_GROUPS
    each = width // groups
    fc_half = shape((groups, blocks, each, width // 2), jnp.bfloat16)
    proj_half = shape((blocks * width, width // 2), jnp.bfloat16)
    out_half = shape((groups, each, width // 2), jnp.bfloat16)
    row = shape((1, width), jnp.float32)
    outs = (
        shape((rows, width), jnp.float32),
        fc_half,
        fc_half,
        proj_half,
        proj_half,
        out_half,
        out_half,
        row,
        shape((blocks, 1, block), jnp.float32),
        row,
        row,
        row,
    )
    fc_spec = pl.BlockSpec((groups, None, each, width // 2), lambda i: (0, i, 0, 0))
    proj_spec = pl.BlockSpec((width, width // 2), lambda i: (i, 0))
    out_spec = pl.BlockSpec((groups, each, width // 2), lambda i: (0, 0, 0))
    bias = pl.BlockSpec((1, 1, block), lambda i: (i, 0, 0))
    vector = pl.BlockSpec((1, width), lambda i: (0, 0))
    inputs = [grad, hidden, normed, att, expanded, mlp, mlp, gain]
    specs = [
        whole(grad),
        whole(hidden),
        whole(normed),
        whole(att),
        pl.BlockSpec((rows, block), lambda i: (0, i)),
        FC_BLOCK,
        PROJ_BLOCK,
        whole(gain),
    ]
    summed = [fc_spec, fc_spec, proj_spec, proj_spec, out_spec, out_spec, vector, bias]
    summed += [vector, vector, vector]
    if earlier is not None:
        inputs += list(earlier)
        specs += summed
    return pl.pallas_call(
        functools.partial(mlp_backward_kernel, earlier is not None),
        grid=(blocks,),
        out_shape=outs,
        in_specs=[SMEM] + specs,
        out_specs=[pl.BlockSpec((rows, width), lambda i: (0, 0))] + summed,
        scratch_shapes=[
            pltpu.VMEM((rows, width), jnp.bfloat16),
            pltpu.VMEM((width, rows), jnp.bfloat16),
            pltpu.VMEM((rows, width), jnp.float32),
            pltpu.VMEM((rows, block), jnp.bfloat16),
            pltpu.VMEM((rows, block), jnp.bfloat16),
        ],
        compiler_params=params(50 << 20),
        cost_estimate=cost(8 * rows * width * blocks * block, rows * blocks * block, *inputs, *outs),
        name="mlp_backward",
    )(core, grad, *in_hbm(inputs[1:]))


def attention_backward_kernel(
    docs,
    back,
    micro,
    lengths_ref,
    dhid_ref,
    att_ref,
    mixed_ref,
    lse_ref,
    out_ref,
    gmix_ref,
    datt_ref,
    bias_ref,
    delta_ref,
    dq_ref,
):
    count = dhid_ref.shape[0]
    low_grad = dhid_ref[...].astype(jnp.bfloat16)
    datt = dot_transposed(low_grad, out_ref[0]).astype(jnp.bfloat16)
    datt_ref[...] = datt
    product = datt.astype(jnp.float32) * att_ref[...].astype(jnp.float32)
    high = product.astype(jnp.bfloat16)
    rest_low = (product - high.astype(jnp.float32)).astype(jnp.bfloat16)
    feature = lax.broadcasted_iota(jnp.int32, (16, FEATURES), 1)
    head = lax.broadcasted_iota(jnp.int32, (16, FEATURES), 0)
    chosen = ((feature >= head * HD) & (feature < (head + 1) * HD)).astype(jnp.bfloat16)
    delta = dot_transposed(chosen, high) + dot_transposed(chosen, rest_low)
    for index in range(H):
        delta_ref[index] = delta[index : index + 1]
    bias_ref[...] = allowed_bias(count, [lengths_ref[micro, d] for d in range(docs)], docs, 1)

    def one_group(group, carry):
        lanes = pl.multiple_of(group * LANES, LANES)
        dq_ref[...] = jnp.zeros_like(dq_ref)
        for block in range(count // BLOCK):
            keys = slice(block * BLOCK, (block + 1) * BLOCK)
            rows = slice(block * BLOCK, min(count, (block + 1 + back) * BLOCK))
            key = head_split(mixed_ref[keys, pl.ds(FEATURES + lanes, LANES)])
            value = head_split(mixed_ref[keys, pl.ds(2 * FEATURES + lanes, LANES)])
            query = mixed_ref[rows, pl.ds(lanes, LANES)]
            datt_group = datt_ref[rows, pl.ds(lanes, LANES)]
            scores = dot_transposed(key, query)
            dprobs = dot_transposed(value, datt_group)
            bias = bias_ref[keys, rows]
            probs_low, dscores_low = ([], [])
            for h in range(GROUP):
                part = slice(h * BLOCK, (h + 1) * BLOCK)
                lse = lse_ref[GROUP * group + h, :, rows]
                delta = delta_ref[GROUP * group + h, :, rows]
                probs = jnp.exp((scores[part] * 0.125 + bias) - lse)
                dscores = probs * (dprobs[part] - delta)
                probs_low.append(probs.astype(jnp.bfloat16))
                dscores_low.append(dscores.astype(jnp.bfloat16))
            probs_low = jnp.concatenate(probs_low, axis=0)
            dscores_low = jnp.concatenate(dscores_low, axis=0)
            dvalue = head_join(dot(probs_low, datt_group))
            dkey = head_join(dot(dscores_low, query)) * 0.125
            dq_ref[rows, :] += transposed_dot(dscores_low, key)
            gmix_ref[keys, pl.ds(FEATURES + lanes, LANES)] = dkey.astype(jnp.bfloat16)
            gmix_ref[keys, pl.ds(2 * FEATURES + lanes, LANES)] = dvalue.astype(jnp.bfloat16)
        gmix_ref[:, pl.ds(lanes, LANES)] = (dq_ref[...] * 0.125).astype(jnp.bfloat16)
        return carry

    lax.fori_loop(0, H // GROUP, one_group, 0, unroll=H // GROUP)


def attention_backward(micro, lengths, dhid, count, back, att, mixed, lse, weight, shape):
    width = dhid.shape[1]
    docs = lengths.shape[1]
    outs = shape((count, 3 * width), jnp.bfloat16)
    inputs = [dhid, att, mixed, lse, weight]
    return pl.pallas_call(
        functools.partial(attention_backward_kernel, docs, back, micro),
        grid=(1,),
        out_shape=outs,
        in_specs=[
            SMEM,
            pl.BlockSpec((count, width), lambda i: (micro, 0)),
            pl.BlockSpec((count, width), lambda i: (micro, 0)),
            pl.BlockSpec((count, 3 * width), lambda i: (micro, 0)),
            pl.BlockSpec((H, 1, count), lambda i: (micro, 0, 0)),
            pl.BlockSpec((1, width, width), lambda i: (3, 0, 0)),
        ],
        out_specs=pl.BlockSpec((count, 3 * width), lambda i: (0, 0)),
        scratch_shapes=[
            pltpu.VMEM((count, width), jnp.bfloat16),
            pltpu.VMEM((count, count), jnp.float32),
            pltpu.VMEM((H, 1, count), jnp.float32),
            pltpu.VMEM((count, LANES), jnp.float32),
        ],
        compiler_params=params(),
        cost_estimate=cost(
            2 * count * width * width + 10 * count * count * width, count * count * H, outs, outs
        ),
        name="attention_backward",
    )(lengths, *in_hbm(inputs))


def attention_terms_kernel(more, micro, core_ref, normed_ref, *rest):
    gmix_refs, rest = (rest[:micro], rest[micro:])
    earlier = rest[:3] if more else (None,) * 3
    if more:
        rest = rest[3:]
    mine_ref, theirs_ref, dbias_ref, right_ref = rest
    core = core_ref[0]
    for index, gmix_ref in enumerate(gmix_refs):
        count = gmix_ref.shape[0]
        right_ref[index * count : (index + 1) * count] = gmix_ref[...]
    right = right_ref[...]
    dbias = jnp.sum(right.astype(jnp.float32), axis=0, keepdims=True)
    dbias_ref[0] = dbias + earlier[2][0] if more else dbias
    terms = transposed_dot(normed_ref[...], right)
    store_halves(core, terms, mine_ref, theirs_ref, earlier[:2] if more else None)


def attention_terms(core, normed, gmix, earlier=None):
    rows, width = normed.shape
    groups = DEVICE_GROUPS
    each = width // groups
    shape = pltpu.HBM
    half = shape((groups, 3, each, width // 2), jnp.bfloat16)
    outs = (half, half, shape((3, 1, width), jnp.float32))
    halves = pl.BlockSpec((groups, None, each, width // 2), lambda i: (0, i, 0, 0))
    summed = [halves, halves, pl.BlockSpec((1, 1, width), lambda i: (i, 0, 0))]
    inputs = [normed, *gmix]
    specs = [whole(normed)] + [
        pl.BlockSpec((part.shape[0], width), lambda i: (0, i)) for part in gmix
    ]
    if earlier is not None:
        inputs += list(earlier)
        specs += summed
    return pl.pallas_call(
        functools.partial(attention_terms_kernel, earlier is not None, len(gmix)),
        grid=(3,),
        out_shape=outs,
        in_specs=[SMEM] + specs,
        out_specs=summed,
        scratch_shapes=[pltpu.VMEM((rows, width), jnp.bfloat16)],
        compiler_params=params(),
        cost_estimate=cost(6 * rows * width * width, 0, *inputs, *outs),
        name="attention_terms",
    )(core, *in_hbm(inputs[:1]), *gmix, *in_hbm(inputs[1 + len(gmix) :]))


def attention_input_kernel(more, micro, dhid_ref, state_ref, weight_ref, gain_ref, *rest):
    gmix_refs, rest = (rest[:micro], rest[micro:])
    earlier = rest[:2] if more else None
    if more:
        rest = rest[2:]
    grad_ref, dgain_ref, dshift_ref, gmix_ref = rest
    step = pl.program_id(0)
    each = pl.num_programs(0) // micro
    for index, part_ref in enumerate(gmix_refs):

        @pl.when(step // each == index)
        def _(part_ref=part_ref):
            gmix_ref[...] = part_ref[...]

    grad_norm = dot_transposed(gmix_ref[:, :FEATURES], weight_ref[0])
    for part in range(1, 3):
        grad_norm = grad_norm + dot_transposed(
            gmix_ref[:, part * FEATURES : (part + 1) * FEATURES], weight_ref[part]
        )
    normed, scale = norm_parts(state_ref[...].astype(jnp.float32))
    dgain = jnp.sum(grad_norm * normed, axis=0, keepdims=True)
    dshift = jnp.sum(grad_norm, axis=0, keepdims=True)

    @pl.when(step == 0)
    def _():
        dgain_ref[...] = dgain + earlier[0][...] if more else dgain
        dshift_ref[...] = dshift + earlier[1][...] if more else dshift

    @pl.when(step > 0)
    def _():
        dgain_ref[...] += dgain
        dshift_ref[...] += dshift

    grad = dhid_ref[...] + norm_back(normed, scale, gain_ref[...], grad_norm)
    grad_ref[...] = grad.astype(grad_ref.dtype)


def attention_input(dhid, state, gmix, weight, gain, kind, earlier=None, chunk=256):
    rows, width = dhid.shape
    shape = jax.ShapeDtypeStruct
    vector = pl.BlockSpec((1, width), lambda i: (0, 0))
    outs = (shape((rows, width), kind), shape((1, width), jnp.float32), shape((1, width), jnp.float32))
    inputs = [dhid, state, weight, gain, *gmix]
    each = rows // chunk // len(gmix)
    specs = [
        rows_of(chunk, width),
        rows_of(chunk, width),
        pl.BlockSpec((3, width, width), lambda i: (0, 0, 0), pipeline_mode=pl.Buffered(1)),
        whole(gain),
    ]
    for index in range(len(gmix)):
        specs.append(
            pl.BlockSpec(
                (chunk, 3 * width),
                lambda i, index=index: (jnp.clip(i - index * each, 0, each - 1), 0),
            )
        )
    if earlier is not None:
        inputs += list(earlier)
        specs += [vector, vector]
    return pl.pallas_call(
        functools.partial(attention_input_kernel, earlier is not None, len(gmix)),
        grid=(rows // chunk,),
        out_shape=outs,
        in_specs=specs,
        out_specs=[rows_of(chunk, width), vector, vector],
        scratch_shapes=[pltpu.VMEM((chunk, 3 * width), jnp.bfloat16)],
        compiler_params=params(),
        cost_estimate=cost(6 * rows * width * width, 0, *inputs, *outs),
        name="attention_input",
    )(*in_hbm(inputs[:4]), *gmix, *in_hbm(inputs[4 + len(gmix) :]))


def place_small_kernel(sizes, me_ref, small_ref, *outs):
    dp = me_ref[0] // 2
    slot = lax.broadcasted_iota(jnp.int32, (16, 1), 0)
    owner = ((slot % 4) * 4 + (slot // 8) * 2 + slot // 4 % 2) ^ dp
    for index, (size, out_ref) in enumerate(zip(sizes, outs)):
        width = 16 * size
        lane = lax.broadcasted_iota(jnp.int32, (256, width), 0)
        column = lax.broadcasted_iota(jnp.int32, (256, width), 1)
        spread = (column % size == lane).astype(jnp.bfloat16)
        rows = jnp.concatenate([small_ref[d, index : index + 1] for d in range(16)], axis=0)
        spread_rows = dot(rows, spread)
        column = lax.broadcasted_iota(jnp.int32, (1, width), 1)
        out_ref[...] = jnp.sum(
            jnp.where(column // size == owner, spread_rows, 0.0), axis=0, keepdims=True
        )


def place_small(me, small, sizes):
    return pl.pallas_call(
        functools.partial(place_small_kernel, sizes),
        out_shape=[jax.ShapeDtypeStruct((1, 16 * size), jnp.float32) for size in sizes],
        in_specs=[SMEM, pl.BlockSpec(memory_space=pltpu.VMEM)],
        out_specs=[pl.BlockSpec(memory_space=pltpu.VMEM)] * len(sizes),
        name="place_small",
    )(me, small)


def swap(value, bits):
    return lax.ppermute(value, BOTH, [(i, i ^ bits) for i in range(32)])


CORE, X, Y, Z1, Z2, Z3 = (1, 2, 4, 8, 16, 24)


def place_kernel(slots, me_ref, *refs):
    sources, (out, sems) = (refs[: len(slots)], refs[len(slots) :])
    me = me_ref[0]
    copies = []
    for source, rels in zip(sources, slots):
        for inner, rel in enumerate(rels):
            copies.append(
                pltpu.make_async_copy(
                    source.at[inner], out.at[:, rel ^ me], sems.at[len(copies)]
                )
            )
    for copy in copies:
        copy.start()
    for copy in copies:
        copy.wait()


def place(me, sources, slots):
    placed = pl.pallas_call(
        functools.partial(place_kernel, slots),
        out_shape=jax.ShapeDtypeStruct((4, 32, 24, FEATURES), jnp.bfloat16),
        in_specs=[SMEM] + [pl.BlockSpec(memory_space=pl.ANY)] * len(sources),
        out_specs=pl.BlockSpec(memory_space=pltpu.VMEM),
        scratch_shapes=[pltpu.SemaphoreType.DMA((32,))],
        name="place",
    )(me, *sources)
    return placed.reshape(4, FEATURES, FEATURES)


def after(values, *others):
    return lax.optimization_barrier((values, others))[0]


def gather_first(piece, small, me):
    base = (0, Z1, Z2, Z3)
    pieces = lax.optimization_barrier(
        [piece] + [swap(piece, bits) for bits in base[1:]]
        + [small] + [swap(small, bits) for bits in base[1:]]
    )
    four, small = (jnp.concatenate(pieces[:4]), jnp.concatenate(pieces[4:]))
    four_x, four_y, four_core, small_x, small_y = lax.optimization_barrier(
        (swap(four, X), swap(four, Y), swap(four, CORE), swap(small, X), swap(small, Y))
    )
    near_xy, far_xy, x_core, y_core, small_xy = lax.optimization_barrier(
        (
            swap(four_y[:2], X), swap(four_x[2:], Y), swap(four_x, CORE), swap(four_y, CORE),
            swap(small_y, X),
        )
    )
    parts = [four, four_x, four_y, near_xy, far_xy]
    parts += [four_core, x_core, y_core, swap(near_xy, CORE), swap(far_xy, CORE)]
    slots = [base] + [tuple(rel ^ bits for rel in base) for bits in (X, Y)]
    slots += [(X ^ Y, X ^ Y ^ Z1), (X ^ Y ^ Z2, X ^ Y ^ Z3)]
    slots += [tuple(rel ^ CORE for rel in rels) for rels in slots]
    return (place(me, parts, slots), jnp.concatenate([small, small_x, small_y, small_xy]))


def pick(array, axis, index):
    return lax.dynamic_index_in_dim(array, index, axis, keepdims=False)


def low(value):
    return value.astype(jnp.bfloat16)


def wide(value):
    return value.astype(jnp.float32)


def add(*terms):
    total = wide(terms[0])
    for term in terms[1:]:
        total = total + wide(term)
    return total


def device_at(z_pair, z_low, y, x):
    return z_pair * 8 + z_low * 4 + y * 2 + x


def total(*terms):
    result = terms[0].astype(jnp.float32)
    for term in terms[1:]:
        result = result + term.astype(jnp.float32)
    return result


def first_sums_kernel(views, spot_ref, *refs):
    mine, got = (refs[:views], refs[views : 2 * views])
    near_sent, far_sent, near_kept, far_kept = refs[2 * views :]
    z_pair, y, x = (spot_ref[0], spot_ref[2], spot_ref[3])
    for low_z in range(2):
        for other in range(2):
            for out, device in (
                (near_sent, device_at(z_pair, low_z, other, 1 - x)),
                (far_sent, device_at(1 - z_pair, low_z, 1 - y, other)),
                (near_kept, device_at(z_pair, low_z, other, x)),
                (far_kept, device_at(1 - z_pair, low_z, y, other)),
            ):
                start = 0
                for left, right in zip(mine, got):
                    count = left.shape[1]
                    out[low_z, other, start : start + count] = total(
                        left[device], right[device]
                    ).astype(jnp.bfloat16)
                    start += count


def second_sums_kernel(spot_ref, near, far, near_in, far_in, *outs):
    near_sent, far_sent, near_kept, far_kept = outs
    y, x = (spot_ref[2], spot_ref[3])
    for low_z in range(2):
        for out, kept, got, index in (
            (near_sent, near, near_in, 1 - y),
            (far_sent, far, far_in, 1 - x),
            (near_kept, near, near_in, y),
            (far_kept, far, far_in, x),
        ):
            out[low_z] = total(kept[low_z, index], got[low_z, index]).astype(jnp.bfloat16)


def third_sums_kernel(spot_ref, near, far, near_in, far_in, sent, kept):
    low_z = spot_ref[1]
    sent[0] = total(near[1 - low_z], near_in[1 - low_z]).astype(jnp.bfloat16)
    sent[1] = total(far[1 - low_z], far_in[1 - low_z]).astype(jnp.bfloat16)
    kept[0] = total(near[low_z], near_in[low_z])
    kept[1] = total(far[low_z], far_in[low_z])


def assemble_kernel(layouts, core_ref, half_ref, other_ref, *outs):
    core = core_ref[0]
    half, other = (half_ref[...], other_ref[...])
    left = jnp.where(core == 0, half, other)
    right = jnp.where(core == 0, other, half)
    start, wide_half = (0, half.shape[1])
    for (blocks, rows), out in zip(layouts, outs):
        for block in range(blocks):
            part = slice(start, start + rows)
            column = 2 * block * wide_half
            out[:, column : column + wide_half] = left[part]
            out[:, column + wide_half : column + 2 * wide_half] = right[part]
            start += rows


def in_vmem(kernel, name, outs, *args):
    vmem = pl.BlockSpec(memory_space=pltpu.VMEM)
    return pl.pallas_call(
        kernel,
        out_shape=outs,
        in_specs=[SMEM] + [vmem] * (len(args) - 1),
        out_specs=[vmem] * len(outs),
        compiler_params=params(),
        cost_estimate=cost(0, 0, *args, *outs),
        name=name,
    )(*args)


class Reduction:
    def __init__(self, spot, mine, theirs):
        self.spot = spot
        self.mine = list(mine)
        self.got = [swap(part, CORE) for part in theirs]
        self.count = sum(part.shape[1] for part in self.mine)
        self.width = self.mine[0].shape[2]

    def like(self, *lead, kind=jnp.bfloat16):
        return jax.ShapeDtypeStruct((*lead, self.count, self.width), kind)

    def first(self):
        near_sent, far_sent, *self.kept = in_vmem(
            functools.partial(first_sums_kernel, len(self.mine)),
            "first_sums",
            [self.like(2, 2)] * 4,
            self.spot,
            *self.mine,
            *self.got,
        )
        self.got = [swap(near_sent, X), swap(far_sent, Y)]
        return self.kept

    def second(self):
        near_sent, far_sent, *self.kept = in_vmem(
            second_sums_kernel, "second_sums", [self.like(2)] * 4, self.spot, *self.kept, *self.got
        )
        self.got = [swap(near_sent, Y), swap(far_sent, X)]
        return self.kept

    def third(self):
        sent, kept = in_vmem(
            third_sums_kernel,
            "third_sums",
            [self.like(2), self.like(2, kind=jnp.float32)],
            self.spot,
            *self.kept,
            *self.got,
        )
        self.kept, self.got = ([kept], [swap(sent, Z1)])
        return self.kept

    def fourth(self):
        (kept,), (got,) = (self.kept, self.got)
        far = low(kept[1] + wide(got[1]))
        self.kept, self.got = ([kept, got], [swap(far, Z2)])

    def fifth(self):
        (kept, got), (far,) = (self.kept, self.got)
        half = kept[0] + wide(got[0]) + wide(far)
        self.kept, self.got = ([half], [swap(half, CORE)])

    def whole(self, core, layouts):
        outs = [
            jax.ShapeDtypeStruct((rows, 2 * self.width * blocks), jnp.float32)
            for blocks, rows in layouts
        ]
        return in_vmem(
            functools.partial(assemble_kernel, layouts), "assemble", outs, core, *self.kept, *self.got
        )


def own_small(small, dp):
    def own(start, rows):
        vector = small[start : start + rows].reshape(-1)
        size = vector.shape[0] // 16
        return lax.dynamic_slice_in_dim(vector, dp * size, size)

    return [own(0, 1), own(1, 1), own(2, 3), own(5, 1), own(6, 1), own(7, 1), own(8, 4), own(12, 1)]


def gather_all(weights, spot, me):
    gain_a, shift_a, qkv, qbias, out, obias, gain_m, shift_m, fc, fbias, proj, pbias = weights
    core = spot[4]

    def half(weight):
        part = lax.dynamic_slice_in_dim(weight, core * 24, 24, 0)
        return jnp.transpose(part.reshape(24, -1, FEATURES), (1, 0, 2))

    columns = lax.dynamic_slice_in_dim(fc, core * 2 * FEATURES, 2 * FEATURES, 1)
    columns = jnp.transpose(columns.reshape(48, 2, FEATURES), (1, 0, 2))
    across = lax.dynamic_slice_in_dim(proj, core * 96, 96, 0).reshape(2, 48, FEATURES)
    mlp = lax.all_gather(jnp.concatenate([columns, across]), BOTH)
    mlp = mlp.reshape(16, 2, 4, 48, FEATURES)
    vectors = [gain_a, shift_a, qbias, obias, gain_m, shift_m, fbias, pbias]
    sizes = tuple(vector.shape[0] for vector in vectors)
    small = jnp.stack([jnp.pad(v, (0, 256 - size)) for v, size in zip(vectors, sizes)])
    first, small = gather_first(jnp.concatenate([half(qkv), half(out)])[None], small[None], me)
    return (first, mlp, *place_small(me, small, sizes))


def gather_plain(weights):
    whole_ones = [lax.all_gather(weight, "dp", axis=0, tiled=True) for weight in weights]
    gain_a, shift_a, qkv, qbias, out, obias, gain_m, shift_m, fc, fbias, proj, pbias = whole_ones

    def blocks(weight):
        return jnp.transpose(weight.reshape(FEATURES, -1, FEATURES), (1, 0, 2))

    rows = [
        wide(v).reshape(1, -1)
        for v in (gain_a, shift_a, qbias, obias, gain_m, shift_m, fbias, pbias)
    ]
    first = jnp.concatenate([blocks(qkv), blocks(out)])
    fc = blocks(fc).reshape(2, 2, 16, 48, FEATURES)
    fc = jnp.transpose(fc, (2, 0, 1, 3, 4))
    mlp = jnp.concatenate([fc, proj.reshape(16, 2, 2, 48, FEATURES)], axis=2)
    return (first, mlp, *rows)


def reduce_plain(matrices, small):
    def joined(left, right):
        both = jnp.concatenate([left, right], axis=-1)
        if both.ndim == 4:
            both = jnp.transpose(both, (0, 2, 1, 3)).reshape(FEATURES, -1)
        return both.reshape(-1, both.shape[-1])

    qkv, out, fc, proj = [joined(*pair) for pair in matrices]
    gain_a, shift_a, qbias, obias, gain_m, shift_m, fbias, pbias = [v.reshape(-1) for v in small]
    values = (
        gain_a, shift_a, qkv, qbias, out, obias, gain_m, shift_m, fc, fbias, proj, pbias
    )
    return tuple(
        wide(lax.psum(low(lax.psum_scatter(wide(v), "dp", scatter_dimension=0, tiled=True)), "rep"))
        for v in values
    )


def forward(tokens, lengths, count, back, weights):
    weight, mlp, gain_a, shift_a, qbias, obias, gain_m, shift_m, fbias, pbias = weights
    state, kept = (tokens, [])
    for use in range(USES):
        normed_a, mixed, att, lse, hidden, normed_m = attention_forward(
            lengths, state, count, back, gain_a, shift_a, weight, qbias, obias, gain_m, shift_m
        )
        expanded, after_mlp = mlp_forward(hidden, normed_m, mlp, fbias, pbias, use == USES - 1)
        kept.append((state, normed_a, mixed, att, lse, hidden, normed_m, expanded))
        state = after_mlp
    return (state, kept)


def shards(custom, tokens, doc_lengths, cotangent, *weights):
    micro, count, width = tokens.shape
    dp, core = (lax.axis_index("dp"), lax.axis_index("rep"))
    spot = (dp // 8, dp // 4 % 2, dp // 2 % 2, dp % 2, core)
    me = (dp * 2 + core).astype(jnp.int32).reshape(1)
    places = jnp.stack(spot).astype(jnp.int32)
    side = core.astype(jnp.int32).reshape(1) if custom else jnp.zeros((1,), jnp.int32)
    back = -(-(LONGEST - 1) // BLOCK)
    lengths = doc_lengths.reshape(micro, doc_lengths.shape[-1])
    whole_ones = gather_all(weights, spot, me) if custom else gather_plain(weights)
    state, kept = forward(
        tokens.reshape(micro * count, width), lengths, count, back, whole_ones
    )
    weight, mlp, gain_a, gain_m = (whole_ones[0], whole_ones[1], whole_ones[2], whole_ones[6])
    grad, mlp_terms, terms, norm = (cotangent.reshape(micro * count, width), None, None, None)
    delayed = None
    for use in range(USES - 1, -1, -1):
        before, normed_a, mixed, att, lse, hidden, normed_m, expanded = kept[use]
        dhid, *mlp_terms = mlp_backward(
            side, grad, hidden, normed_m, att, expanded, mlp, gain_m, mlp_terms
        )
        sending = custom and use == 0
        if delayed is not None:
            terms = delayed()
        if sending:
            fc_mine, fc_theirs, proj_mine, proj_theirs, out_mine, out_theirs = [
                part.reshape(16, -1, part.shape[-1]) for part in mlp_terms[:6]
            ]
            sums = Reduction(
                places, (fc_mine, proj_mine, out_mine), (fc_theirs, proj_theirs, out_theirs)
            )
            sums.got, terms = lax.optimization_barrier((sums.got, terms))
            dhid = after(dhid, sums.first())
        gmix = [
            attention_backward(
                index, lengths, dhid, count, back, att, mixed, lse, weight,
                pltpu.HBM if use else jax.ShapeDtypeStruct,
            )
            for index in range(micro)
        ]
        if use:
            delayed = functools.partial(attention_terms, side, normed_a, gmix)
        else:
            terms = attention_terms(side, normed_a, gmix, terms)
        if sending:
            qkv_sums = Reduction(
                places, *[(part.reshape(16, -1, part.shape[-1]),) for part in terms[:2]]
            )
            sums.got, terms = lax.optimization_barrier((sums.got, terms))
            gmix = after(gmix, sums.second())
        kind = jnp.float32 if use else jnp.bfloat16
        grad, *norm = attention_input(dhid, before, gmix, weight, gain_a, kind, norm)
        if sending:
            sums.got, qkv_sums.got, norm = lax.optimization_barrier(
                (sums.got, qkv_sums.got, norm)
            )
    small = (norm[0], norm[1], terms[2], mlp_terms[6], mlp_terms[9], mlp_terms[10])
    small += (mlp_terms[7], mlp_terms[8])
    if custom:
        small = jnp.concatenate([part.reshape(-1, width) for part in small])
        qkv_sums.first()
        sums.third()
        small = small + swap(small, CORE)
        got = swap(small, X)
        sums.got, qkv_sums.got, got = lax.optimization_barrier((sums.got, qkv_sums.got, got))
        qkv_sums.second()
        sums.fourth()
        small = small + got
        got = swap(small, Y)
        sums.got, qkv_sums.got, got = lax.optimization_barrier((sums.got, qkv_sums.got, got))
        qkv_sums.third()
        sums.fifth()
        small = small + got
        got = swap(small, Z1)
        sums.got, qkv_sums.got, got = lax.optimization_barrier((sums.got, qkv_sums.got, got))
        qkv_sums.fourth()
        small = small + got
        got = swap(small, Z2)
        qkv_sums.got, got = lax.optimization_barrier((qkv_sums.got, got))
        qkv_sums.fifth()
        fc, proj, out = sums.whole(side, ((4, 48), (1, 192), (1, 48)))
        (qkv,) = qkv_sums.whole(side, ((3, 48),))
        small = own_small(small + got, dp)
        gain_a, shift_a, qbias, obias, gain_m, shift_m, fbias, pbias = small
        final = (
            gain_a, shift_a, qkv, qbias, out, obias, gain_m, shift_m, fc, fbias, proj, pbias
        )
    else:
        matrices = (terms[:2], mlp_terms[4:6], mlp_terms[:2], mlp_terms[2:4])
        final = reduce_plain(matrices, small)
    return (state.reshape(tokens.shape), grad.reshape(tokens.shape), *final)


def solution(mesh):
    custom = mesh.shape["dp"] == 16 and mesh.shape["rep"] == 2
    placed = tuple(
        P("dp", None) if index in (2, 4, 8, 10) else P("dp") for index in range(12)
    )
    rows = P(None, BOTH, None)
    return jax.shard_map(
        functools.partial(shards, custom),
        mesh=mesh,
        in_specs=(rows, rows, rows, *placed),
        out_specs=(rows, rows, *placed),
        check_vma=False,
    )
```

```python
import functools
import math

import jax
import jax.numpy as jnp
from jax import lax
from jax.experimental import pallas as pl
from jax.experimental.pallas import tpu as pltpu
from jax.sharding import PartitionSpec as P

H = 12
HD = 64
USES = 2
LONGEST = 256
BOTH = ("dp", "rep")


NORM_EPS = 1e-05
BLOCK = 128
FEATURES = H * HD
VMEM_LIMIT = 40 << 20
COST_SCALE = 8


def dot(left, right):
    return jnp.dot(left, right, preferred_element_type=jnp.float32)


def transposed_dot(left, right):
    return lax.dot_general(
        left, right, (((0,), (0,)), ((), ())), preferred_element_type=jnp.float32
    )


def dot_transposed(left, right):
    return lax.dot_general(
        left, right, (((1,), (1,)), ((), ())), preferred_element_type=jnp.float32
    )


def norm_parts(values):
    center = values - jnp.mean(values, axis=-1, keepdims=True)
    spread = jnp.mean(center * center, axis=-1, keepdims=True)
    scale = lax.rsqrt(spread + NORM_EPS)
    return (center * scale, scale)


def norm_back(normed, scale, gain, grad):
    inner = grad * gain
    first = jnp.mean(inner, axis=-1, keepdims=True)
    second = jnp.mean(inner * normed, axis=-1, keepdims=True)
    return (inner - first - normed * second) * scale


def segment_of(places, lengths, docs):
    end = jnp.int32(0)
    segment = jnp.zeros(places.shape, jnp.int32)
    for doc in range(docs):
        end = end + lengths[doc]
        segment = segment + (places >= end).astype(jnp.int32)
    return segment


def allowed_bias(count, lengths, docs, query_axis):
    query_shape = (count, 1) if query_axis == 0 else (1, count)
    key_shape = (1, count) if query_axis == 0 else (count, 1)
    query = lax.broadcasted_iota(jnp.int32, query_shape, query_axis)
    key = lax.broadcasted_iota(jnp.int32, key_shape, 1 - query_axis)
    same = segment_of(query, lengths, docs) == segment_of(key, lengths, docs)
    return jnp.where(same & (key <= query), 0.0, -1e30).astype(jnp.float32)


GROUP = 4
LANES = GROUP * HD


def head_split(array):
    head = lax.broadcasted_iota(jnp.int32, array.shape, 1) // HD
    zero = jnp.zeros_like(array)
    return jnp.concatenate([jnp.where(head == h, array, zero) for h in range(GROUP)], axis=0)


def head_join(stacked):
    count = stacked.shape[0] // GROUP
    head = lax.broadcasted_iota(jnp.int32, (count, LANES), 1) // HD
    joined = stacked[:count]
    for h in range(1, GROUP):
        joined = jnp.where(head == h, stacked[h * count : (h + 1) * count], joined)
    return joined


def attention_forward_kernel(
    docs,
    back,
    lengths_ref,
    state_ref,
    gain_ref,
    shift_ref,
    weight_ref,
    qbias_ref,
    obias_ref,
    gain2_ref,
    shift2_ref,
    normed_ref,
    mixed_ref,
    att_ref,
    lse_ref,
    hidden_ref,
    normed2_ref,
    bias_ref,
    lse_cols,
):
    micro = pl.program_id(0)
    state = state_ref[...].astype(jnp.float32)
    count = state.shape[0]
    normed = (norm_parts(state)[0] * gain_ref[...] + shift_ref[...]).astype(jnp.bfloat16)
    normed_ref[...] = normed
    for part in range(3):
        columns = slice(part * FEATURES, (part + 1) * FEATURES)
        mixed_ref[:, columns] = (dot(normed, weight_ref[part]) + qbias_ref[:, columns]).astype(
            jnp.bfloat16
        )
    bias_ref[...] = allowed_bias(count, [lengths_ref[micro, d] for d in range(docs)], docs, 0)
    lse_cols[...] = jnp.zeros_like(lse_cols)

    def one_group(group, carry):
        lanes = pl.multiple_of(group * LANES, LANES)
        for block in range(count // BLOCK):
            rows = slice(block * BLOCK, (block + 1) * BLOCK)
            low_key = max(0, block - back) * BLOCK
            keys = slice(low_key, (block + 1) * BLOCK)
            query = head_split(mixed_ref[rows, pl.ds(lanes, LANES)])
            key = mixed_ref[keys, pl.ds(FEATURES + lanes, LANES)]
            value = mixed_ref[keys, pl.ds(2 * FEATURES + lanes, LANES)]
            scores = dot_transposed(query, key)
            bias = bias_ref[rows, keys]
            scores = scores * 0.125 + jnp.concatenate([bias] * GROUP, axis=0)
            top = jnp.max(scores, axis=-1, keepdims=True)
            expo = jnp.exp(scores - top)
            total_expo = jnp.sum(expo, axis=-1, keepdims=True)
            result = dot(expo.astype(jnp.bfloat16), value) / total_expo
            att_ref[rows, pl.ds(lanes, LANES)] = head_join(result).astype(jnp.bfloat16)
            lse = top + jnp.log(total_expo)
            lane = lax.broadcasted_iota(jnp.int32, (BLOCK, 128), 1)
            for h in range(GROUP):
                lse_cols[rows, :] += jnp.where(
                    lane == GROUP * group + h, lse[h * BLOCK : (h + 1) * BLOCK], 0.0
                )
        return carry

    lax.fori_loop(0, H // GROUP, one_group, 0, unroll=H // GROUP)
    lse = jnp.transpose(lse_cols[...])
    for index in range(H):
        lse_ref[index] = lse[index : index + 1]
    hidden = state + (dot(att_ref[...], weight_ref[3]) + obias_ref[...])
    hidden_ref[...] = hidden
    normed2_ref[...] = (norm_parts(hidden)[0] * gain2_ref[...] + shift2_ref[...]).astype(
        jnp.bfloat16
    )


def whole(array):
    dims = len(array.shape)
    return pl.BlockSpec(array.shape, lambda *unused: (0,) * dims, pipeline_mode=pl.Buffered(1))


SMEM = pl.BlockSpec(memory_space=pltpu.SMEM)


def in_hbm(arrays):
    return [pltpu.with_memory_space_constraint(array, pltpu.HBM) for array in arrays]


def rows_of(count, width):
    return pl.BlockSpec((count, width), lambda i: (i, 0))


def params(limit=VMEM_LIMIT):
    return pltpu.CompilerParams(vmem_limit_bytes=limit)


def cost(flops, transcendentals, *arrays):
    size = sum(math.prod(a.shape) * a.dtype.itemsize for a in arrays)
    return pl.CostEstimate(
        flops=int(flops) // COST_SCALE,
        transcendentals=int(transcendentals) // COST_SCALE,
        bytes_accessed=int(size) // COST_SCALE,
    )


def attention_forward(lengths, state, count, back, gain, shift, weight, qbias, obias, gain2, shift2):
    rows = state.shape[0]
    micro, docs = lengths.shape
    width = FEATURES
    shape = pltpu.HBM
    outs = (
        shape((rows, width), jnp.bfloat16),
        shape((rows, 3 * width), jnp.bfloat16),
        shape((rows, width), jnp.bfloat16),
        shape((micro * H, 1, count), jnp.float32),
        shape((rows, width), jnp.float32),
        shape((rows, width), jnp.bfloat16),
    )
    weights = (gain, shift, weight, qbias, obias, gain2, shift2)
    return pl.pallas_call(
        functools.partial(attention_forward_kernel, docs, back),
        grid=(micro,),
        out_shape=outs,
        in_specs=[SMEM, rows_of(count, width)] + [whole(w) for w in weights],
        out_specs=(
            rows_of(count, width),
            rows_of(count, 3 * width),
            rows_of(count, width),
            pl.BlockSpec((H, 1, count), lambda i: (i, 0, 0)),
            rows_of(count, width),
            rows_of(count, width),
        ),
        scratch_shapes=[
            pltpu.VMEM((count, count), jnp.float32),
            pltpu.VMEM((count, 128), jnp.float32),
        ],
        compiler_params=params(),
        cost_estimate=cost(
            8 * rows * width * width + 4 * rows * count * width, rows * count * H, state, *weights, *outs
        ),
        name="attention_forward",
    )(lengths, *in_hbm((state, *weights)))


GELU_C = 0.7978845608028654
GELU_K = 0.044715 * GELU_C


def gelu_gate(value):
    square = value * value
    gate = 0.5 * jnp.tanh(value * (GELU_C + GELU_K * square)) + 0.5
    return (gate, square)


def mlp_forward_kernel(
    hidden_ref, normed_ref, fc_ref, fbias_ref, proj_ref, pbias_ref, expanded_ref, state_ref
):
    step = pl.program_id(0)
    chunk = 256

    @pl.when(step == 0)
    def _():
        state_ref[...] = hidden_ref[...] + pbias_ref[...]

    for start in range(0, normed_ref.shape[0], chunk):
        rows = slice(start, start + chunk)
        expanded = dot(normed_ref[rows, :], square_of(fc_ref)) + fbias_ref[...]
        expanded_ref[rows, :] = expanded.astype(expanded_ref.dtype)
        gate, unused = gelu_gate(expanded)
        activated = (expanded * gate).astype(jnp.bfloat16)
        state_ref[rows, :] += dot(activated, square_of(proj_ref))


DEVICE_GROUPS = 16


def square_of(ref):
    return ref[...].reshape(FEATURES, FEATURES)


def fc_at(step):
    return jnp.minimum(step, 3)


FC_BLOCK = pl.BlockSpec((16, 1, 1, 48, FEATURES), lambda i: (0, fc_at(i) // 2, fc_at(i) % 2, 0, 0))
PROJ_BLOCK = pl.BlockSpec((4, 2, 2, 48, FEATURES), lambda i: (fc_at(i), 0, 1, 0, 0))


def mlp_forward(hidden, normed, mlp, fbias, pbias):
    rows, width = hidden.shape
    block = width
    hidden_units = 4 * block
    shape = pltpu.HBM
    outs = (
        shape((rows, hidden_units), jnp.bfloat16),
        shape((rows, width), jnp.float32),
    )
    specs = (
        pl.BlockSpec((rows, block), lambda i: (0, i)),
        pl.BlockSpec((rows, width), lambda i: (0, 0)),
    )
    return pl.pallas_call(
        mlp_forward_kernel,
        grid=(hidden_units // block,),
        out_shape=outs,
        in_specs=[
            whole(hidden),
            whole(normed),
            FC_BLOCK,
            pl.BlockSpec((1, block), lambda i: (0, i)),
            PROJ_BLOCK,
            whole(pbias),
        ],
        out_specs=specs,
        compiler_params=params(),
        cost_estimate=cost(
            4 * rows * width * hidden_units, rows * hidden_units, hidden, normed, mlp, *outs
        ),
        name="mlp_forward",
    )(*in_hbm((hidden, normed, mlp, fbias, mlp, pbias)))


def transposed_dot(left, right):
    return lax.dot_general(
        left, right, (((0,), (0,)), ((), ())), preferred_element_type=jnp.float32
    )


def dot_transposed(left, right):
    return lax.dot_general(
        left, right, (((1,), (1,)), ((), ())), preferred_element_type=jnp.float32
    )


def store_halves(core, value, mine_ref, theirs_ref, earlier):
    half = value.shape[1] // 2
    left, right = (value[:, :half], value[:, half:])
    mine = jnp.where(core == 0, left, right)
    theirs = jnp.where(core == 0, right, left)
    shape = mine_ref.shape
    mine, theirs = (mine.reshape(shape), theirs.reshape(shape))
    if earlier is not None:
        mine = mine + earlier[0][...].astype(jnp.float32)
        theirs = theirs + earlier[1][...].astype(jnp.float32)
    mine_ref[...] = mine.astype(mine_ref.dtype)
    theirs_ref[...] = theirs.astype(theirs_ref.dtype)


def mlp_backward_kernel(
    more,
    forward,
    core_ref,
    grad_ref,
    hidden_ref,
    normed_ref,
    att_ref,
    *rest,
):
    if forward:
        fbias_ref, pbias_ref, fc_ref, proj_ref, gain_ref, *rest = rest
    else:
        expanded_ref, fc_ref, proj_ref, gain_ref, *rest = rest
    earlier = rest[:11] if more else (None,) * 11
    if more:
        rest = rest[11:]
    if forward:
        final_ref, *rest, state_ref = rest
    (
        dhid_ref,
        fc_mine,
        fc_theirs,
        proj_mine,
        proj_theirs,
        out_mine,
        out_theirs,
        dobias_ref,
        dfbias_ref,
        dpbias_ref,
        dgain_ref,
        dshift_ref,
        low_ref,
        normed_t,
        acc_ref,
        act_ref,
        ge_ref,
        hidden_buf,
        att_buf,
        sems,
    ) = rest
    step = pl.program_id(0)
    core = core_ref[0]
    rows = grad_ref.shape[0]
    blocks = pl.num_programs(0) - 1
    chunk = 256
    chunks = [slice(start, start + chunk) for start in range(0, rows, chunk)]
    late = [
        pltpu.make_async_copy(hidden_ref, hidden_buf, sems.at[0]),
        pltpu.make_async_copy(att_ref, att_buf, sems.at[1]),
    ]

    @pl.when(step == 0)
    def _():
        for copy in late:
            copy.start()
        low_grad = grad_ref[...].astype(jnp.bfloat16)
        low_ref[...] = low_grad
        dpbias = jnp.sum(low_grad.astype(jnp.float32), axis=0, keepdims=True)
        dpbias_ref[...] = dpbias + earlier[8][...] if more else dpbias
        normed_t[...] = jnp.transpose(normed_ref[...])
        acc_ref[...] = jnp.zeros_like(acc_ref)
        if forward:
            state_ref[...] = jnp.zeros_like(state_ref)

    @pl.when(step < blocks)
    def _():
        bias_sum = jnp.zeros(dfbias_ref.shape[1:], jnp.float32)
        for part in chunks:
            grad_act = dot_transposed(low_ref[part, :], square_of(proj_ref))
            if forward:
                value = dot(normed_ref[part, :], square_of(fc_ref)) + fbias_ref[...]
            else:
                value = expanded_ref[part, :].astype(jnp.float32)
            gate, square = gelu_gate(value)
            act = value * gate
            slope = gate + act * (1.0 - gate) * (2 * GELU_C + 6 * GELU_K * square)
            activated = act.astype(jnp.bfloat16)
            act_ref[part, :] = activated
            if forward:
                state_ref[part, :] += dot(activated, square_of(proj_ref))
            grad_exp = (grad_act * slope).astype(jnp.bfloat16)
            ge_ref[part, :] = grad_exp
            bias_sum = bias_sum + jnp.sum(grad_exp.astype(jnp.float32), axis=0, keepdims=True)
            acc_ref[part, :] += dot_transposed(grad_exp, square_of(fc_ref))
        dfbias_ref[0] = bias_sum + earlier[7][0] if more else bias_sum
        dproj = transposed_dot(act_ref[...], low_ref[...])
        store_halves(core, dproj, proj_mine, proj_theirs, earlier[2:4] if more else None)
        dfc = dot(normed_t[...], ge_ref[...])
        store_halves(core, dfc, fc_mine, fc_theirs, earlier[:2] if more else None)

    @pl.when(step == blocks)
    def _():
        for copy in late:
            copy.wait()
        dgain = jnp.zeros(dgain_ref.shape, jnp.float32)
        dshift, dobias = (dgain, dgain)
        copies = []
        for index, part in enumerate(chunks):
            hidden = hidden_buf[part, :]
            if forward:
                final = hidden + (state_ref[part, :] + pbias_ref[...])
                final_ref[part, :] = final.astype(jnp.bfloat16)
            normed, scale = norm_parts(hidden)
            grad_norm = acc_ref[part, :]
            dgain = dgain + jnp.sum(grad_norm * normed, axis=0, keepdims=True)
            dshift = dshift + jnp.sum(grad_norm, axis=0, keepdims=True)
            dhid = grad_ref[part, :].astype(jnp.float32) + norm_back(
                normed, scale, gain_ref[...], grad_norm
            )
            hidden_buf[part, :] = dhid
            copies.append(
                pltpu.make_async_copy(
                    hidden_buf.at[part, :], dhid_ref.at[part, :], sems.at[2 + index]
                )
            )
            copies[-1].start()
            low_dhid = dhid.astype(jnp.bfloat16)
            low_ref[part, :] = low_dhid
            dobias = dobias + jnp.sum(low_dhid.astype(jnp.float32), axis=0, keepdims=True)
        dgain_ref[...] = dgain + earlier[9][...] if more else dgain
        dshift_ref[...] = dshift + earlier[10][...] if more else dshift
        dobias_ref[...] = dobias + earlier[6][...] if more else dobias
        dout = transposed_dot(att_buf[...], low_ref[...])
        store_halves(core, dout, out_mine, out_theirs, earlier[4:6] if more else None)
        for copy in copies:
            copy.wait()


def mlp_backward(core, grad, hidden, normed, att, expanded, mlp, gain, earlier=None, biases=None):
    rows, width = hidden.shape
    blocks, block = (4, width)
    shape = pltpu.HBM
    groups = DEVICE_GROUPS
    each = width // groups
    fc_half = shape((groups, blocks, each, width // 2), jnp.bfloat16)
    proj_half = shape((blocks * width, width // 2), jnp.bfloat16)
    out_half = shape((groups, each, width // 2), jnp.bfloat16)
    row = shape((1, width), jnp.float32)
    outs = (
        shape((rows, width), jnp.float32),
        fc_half,
        fc_half,
        proj_half,
        proj_half,
        out_half,
        out_half,
        row,
        shape((blocks, 1, block), jnp.float32),
        row,
        row,
        row,
    )
    fc_spec = pl.BlockSpec((groups, None, each, width // 2), lambda i: (0, jnp.minimum(i, 3), 0, 0))
    proj_spec = pl.BlockSpec((width, width // 2), lambda i: (jnp.minimum(i, 3), 0))
    out_spec = pl.BlockSpec((groups, each, width // 2), lambda i: (0, 0, 0))
    bias = pl.BlockSpec((1, 1, block), lambda i: (jnp.minimum(i, 3), 0, 0))
    vector = pl.BlockSpec((1, width), lambda i: (0, 0))
    inputs = [grad, hidden, normed, att]
    raw = pl.BlockSpec(memory_space=pltpu.HBM)
    specs = [whole(grad), raw, whole(normed), raw]
    out_specs = [raw]
    scratch = []
    if biases is None:
        inputs.append(expanded)
        specs.append(pl.BlockSpec((rows, block), lambda i: (0, jnp.minimum(i, 3))))
    else:
        inputs += list(biases)
        specs += [pl.BlockSpec((1, block), lambda i: (0, jnp.minimum(i, 3))), whole(biases[1])]
        outs = (shape((rows, width), jnp.bfloat16), *outs)
        out_specs = [pl.BlockSpec((rows, width), lambda i: (0, 0)), raw]
        scratch = [pltpu.VMEM((rows, width), jnp.float32)]
    inputs += [mlp, mlp, gain]
    specs += [FC_BLOCK, PROJ_BLOCK, whole(gain)]
    summed = [fc_spec, fc_spec, proj_spec, proj_spec, out_spec, out_spec, vector, bias]
    summed += [vector, vector, vector]
    if earlier is not None:
        inputs += list(earlier)
        specs += summed
    return pl.pallas_call(
        functools.partial(mlp_backward_kernel, earlier is not None, biases is not None),
        grid=(blocks + 1,),
        out_shape=outs,
        in_specs=[SMEM] + specs,
        out_specs=out_specs + summed,
        scratch_shapes=[
            pltpu.VMEM((rows, width), jnp.bfloat16),
            pltpu.VMEM((width, rows), jnp.bfloat16),
            pltpu.VMEM((rows, width), jnp.float32),
            pltpu.VMEM((rows, block), jnp.bfloat16),
            pltpu.VMEM((rows, block), jnp.bfloat16),
            pltpu.VMEM((rows, width), jnp.float32),
            pltpu.VMEM((rows, width), jnp.bfloat16),
            pltpu.SemaphoreType.DMA((2 + rows // 256,)),
            *scratch,
        ],
        compiler_params=params(54 << 20),
        cost_estimate=cost(8 * rows * width * blocks * block, rows * blocks * block, *inputs, *outs),
        name="mlp_backward",
    )(core, grad, *in_hbm(inputs[1:]))


def input_gradient(
    dhid_ref, state_ref, gmix_ref, weight_ref, gain_ref, earlier, grad_ref, dgain_ref, dshift_ref
):
    step = pl.program_id(0)
    grad_norm = dot_transposed(gmix_ref[:, :FEATURES], weight_ref[0])
    for part in range(1, 3):
        grad_norm = grad_norm + dot_transposed(
            gmix_ref[:, part * FEATURES : (part + 1) * FEATURES], weight_ref[part]
        )
    normed, scale = norm_parts(state_ref[...].astype(jnp.float32))
    dgain = jnp.sum(grad_norm * normed, axis=0, keepdims=True)
    dshift = jnp.sum(grad_norm, axis=0, keepdims=True)

    @pl.when(step == 0)
    def _():
        dgain_ref[...] = dgain if earlier is None else dgain + earlier[0][...]
        dshift_ref[...] = dshift if earlier is None else dshift + earlier[1][...]

    @pl.when(step > 0)
    def _():
        dgain_ref[...] += dgain
        dshift_ref[...] += dshift

    grad = dhid_ref[...] + norm_back(normed, scale, gain_ref[...], grad_norm)
    grad_ref[...] = grad.astype(grad_ref.dtype)


def attention_backward_kernel(
    docs,
    back,
    micro,
    lengths_ref,
    dhid_ref,
    att_ref,
    mixed_ref,
    lse_ref,
    out_ref,
    *rest,
):
    if micro is None:
        micro = pl.program_id(0)
        state_ref, gain_ref, gmix_ref, grad_ref, dgain_ref, dshift_ref, *rest = rest
        finish = functools.partial(
            input_gradient, dhid_ref, state_ref, gmix_ref, out_ref, gain_ref, None,
            grad_ref, dgain_ref, dshift_ref,
        )
    else:
        gmix_ref, *rest = rest
        finish = None
    datt_ref, bias_ref, delta_ref, dq_ref = rest
    count = dhid_ref.shape[0]
    low_grad = dhid_ref[...].astype(jnp.bfloat16)
    datt = dot_transposed(low_grad, out_ref[out_ref.shape[0] - 1]).astype(jnp.bfloat16)
    datt_ref[...] = datt
    product = datt.astype(jnp.float32) * att_ref[...].astype(jnp.float32)
    high = product.astype(jnp.bfloat16)
    rest_low = (product - high.astype(jnp.float32)).astype(jnp.bfloat16)
    feature = lax.broadcasted_iota(jnp.int32, (16, FEATURES), 1)
    head = lax.broadcasted_iota(jnp.int32, (16, FEATURES), 0)
    chosen = ((feature >= head * HD) & (feature < (head + 1) * HD)).astype(jnp.bfloat16)
    delta = dot_transposed(chosen, high) + dot_transposed(chosen, rest_low)
    for index in range(H):
        delta_ref[index] = delta[index : index + 1]
    bias_ref[...] = allowed_bias(count, [lengths_ref[micro, d] for d in range(docs)], docs, 1)

    def one_group(group, carry):
        lanes = pl.multiple_of(group * LANES, LANES)
        dq_ref[...] = jnp.zeros_like(dq_ref)
        for block in range(count // BLOCK):
            keys = slice(block * BLOCK, (block + 1) * BLOCK)
            rows = slice(block * BLOCK, min(count, (block + 1 + back) * BLOCK))
            key = head_split(mixed_ref[keys, pl.ds(FEATURES + lanes, LANES)])
            value = head_split(mixed_ref[keys, pl.ds(2 * FEATURES + lanes, LANES)])
            query = mixed_ref[rows, pl.ds(lanes, LANES)]
            datt_group = datt_ref[rows, pl.ds(lanes, LANES)]
            scores = dot_transposed(key, query)
            dprobs = dot_transposed(value, datt_group)
            bias = bias_ref[keys, rows]
            probs_low, dscores_low = ([], [])
            for h in range(GROUP):
                part = slice(h * BLOCK, (h + 1) * BLOCK)
                lse = lse_ref[GROUP * group + h, :, rows]
                delta = delta_ref[GROUP * group + h, :, rows]
                probs = jnp.exp((scores[part] * 0.125 + bias) - lse)
                dscores = probs * (dprobs[part] - delta)
                probs_low.append(probs.astype(jnp.bfloat16))
                dscores_low.append(dscores.astype(jnp.bfloat16))
            probs_low = jnp.concatenate(probs_low, axis=0)
            dscores_low = jnp.concatenate(dscores_low, axis=0)
            dvalue = head_join(dot(probs_low, datt_group))
            dkey = head_join(dot(dscores_low, query)) * 0.125
            dq_ref[rows, :] += transposed_dot(dscores_low, key)
            gmix_ref[keys, pl.ds(FEATURES + lanes, LANES)] = dkey.astype(jnp.bfloat16)
            gmix_ref[keys, pl.ds(2 * FEATURES + lanes, LANES)] = dvalue.astype(jnp.bfloat16)
        gmix_ref[:, pl.ds(lanes, LANES)] = (dq_ref[...] * 0.125).astype(jnp.bfloat16)
        return carry

    lax.fori_loop(0, H // GROUP, one_group, 0, unroll=H // GROUP)
    if finish is not None:
        finish()


def attention_backward(micro, lengths, dhid, count, back, att, mixed, lse, weight):
    width = dhid.shape[1]
    docs = lengths.shape[1]
    outs = jax.ShapeDtypeStruct((count, 3 * width), jnp.bfloat16)
    inputs = [dhid, att, mixed, lse, weight]
    return pl.pallas_call(
        functools.partial(attention_backward_kernel, docs, back, micro),
        grid=(1,),
        out_shape=outs,
        in_specs=[
            SMEM,
            pl.BlockSpec((count, width), lambda i: (micro, 0)),
            pl.BlockSpec((count, width), lambda i: (micro, 0)),
            pl.BlockSpec((count, 3 * width), lambda i: (micro, 0)),
            pl.BlockSpec((H, 1, count), lambda i: (micro, 0, 0)),
            pl.BlockSpec((1, width, width), lambda i: (3, 0, 0)),
        ],
        out_specs=pl.BlockSpec((count, 3 * width), lambda i: (0, 0)),
        scratch_shapes=[
            pltpu.VMEM((count, width), jnp.bfloat16),
            pltpu.VMEM((count, count), jnp.float32),
            pltpu.VMEM((H, 1, count), jnp.float32),
            pltpu.VMEM((count, LANES), jnp.float32),
        ],
        compiler_params=params(),
        cost_estimate=cost(
            2 * count * width * width + 10 * count * count * width, count * count * H, outs, outs
        ),
        name="attention_backward",
    )(lengths, *in_hbm(inputs))


def attention_backward_all(lengths, dhid, count, back, att, mixed, lse, weight, state, gain):
    rows, width = dhid.shape
    micro, docs = lengths.shape
    vector = pl.BlockSpec((1, width), lambda i: (0, 0))
    outs = (
        pltpu.HBM((rows, 3 * width), jnp.bfloat16),
        jax.ShapeDtypeStruct((rows, width), jnp.float32),
        jax.ShapeDtypeStruct((1, width), jnp.float32),
        jax.ShapeDtypeStruct((1, width), jnp.float32),
    )
    inputs = [dhid, att, mixed, lse, weight, state, gain]
    return pl.pallas_call(
        functools.partial(attention_backward_kernel, docs, back, None),
        grid=(micro,),
        out_shape=outs,
        in_specs=[
            SMEM,
            rows_of(count, width),
            rows_of(count, width),
            rows_of(count, 3 * width),
            pl.BlockSpec((H, 1, count), lambda i: (i, 0, 0)),
            whole(weight),
            rows_of(count, width),
            whole(gain),
        ],
        out_specs=[rows_of(count, 3 * width), rows_of(count, width), vector, vector],
        scratch_shapes=[
            pltpu.VMEM((count, width), jnp.bfloat16),
            pltpu.VMEM((count, count), jnp.float32),
            pltpu.VMEM((H, 1, count), jnp.float32),
            pltpu.VMEM((count, LANES), jnp.float32),
        ],
        compiler_params=params(44 << 20),
        cost_estimate=cost(
            8 * rows * width * width + 10 * rows * count * width, rows * count * H, *inputs, *outs
        ),
        name="attention_backward_all",
    )(lengths, *in_hbm(inputs))


def attention_terms_kernel(more, micro, core_ref, normed_ref, *rest):
    gmix_refs, rest = (rest[:micro], rest[micro:])
    earlier = rest[:3] if more else (None,) * 3
    if more:
        rest = rest[3:]
    mine_ref, theirs_ref, dbias_ref, right_ref = rest
    core = core_ref[0]
    for index, gmix_ref in enumerate(gmix_refs):
        count = gmix_ref.shape[0]
        right_ref[index * count : (index + 1) * count] = gmix_ref[...]
    right = right_ref[...]
    dbias = jnp.sum(right.astype(jnp.float32), axis=0, keepdims=True)
    dbias_ref[0] = dbias + earlier[2][0] if more else dbias
    terms = transposed_dot(normed_ref[...], right)
    store_halves(core, terms, mine_ref, theirs_ref, earlier[:2] if more else None)


def attention_terms(core, normed, gmix, earlier=None):
    rows, width = normed.shape
    groups = DEVICE_GROUPS
    each = width // groups
    shape = pltpu.HBM
    half = shape((groups, 3, each, width // 2), jnp.bfloat16)
    outs = (half, half, shape((3, 1, width), jnp.float32))
    halves = pl.BlockSpec((groups, None, each, width // 2), lambda i: (0, i, 0, 0))
    summed = [halves, halves, pl.BlockSpec((1, 1, width), lambda i: (i, 0, 0))]
    inputs = [normed, *gmix]
    specs = [whole(normed)] + [
        pl.BlockSpec((part.shape[0], width), lambda i: (0, i)) for part in gmix
    ]
    if earlier is not None:
        inputs += list(earlier)
        specs += summed
    return pl.pallas_call(
        functools.partial(attention_terms_kernel, earlier is not None, len(gmix)),
        grid=(3,),
        out_shape=outs,
        in_specs=[SMEM] + specs,
        out_specs=summed,
        scratch_shapes=[pltpu.VMEM((rows, width), jnp.bfloat16)],
        compiler_params=params(),
        cost_estimate=cost(6 * rows * width * width, 0, *inputs, *outs),
        name="attention_terms",
    )(core, *in_hbm(inputs[:1]), *gmix, *in_hbm(inputs[1 + len(gmix) :]))


def attention_input_kernel(more, micro, dhid_ref, state_ref, weight_ref, gain_ref, *rest):
    gmix_refs, rest = (rest[:micro], rest[micro:])
    earlier = rest[:2] if more else None
    if more:
        rest = rest[2:]
    grad_ref, dgain_ref, dshift_ref, gmix_ref = rest
    each = pl.num_programs(0) // micro
    for index, part_ref in enumerate(gmix_refs):

        @pl.when(pl.program_id(0) // each == index)
        def _(part_ref=part_ref):
            gmix_ref[...] = part_ref[...]

    input_gradient(
        dhid_ref, state_ref, gmix_ref, weight_ref, gain_ref, earlier, grad_ref, dgain_ref, dshift_ref
    )


def attention_input(dhid, state, gmix, weight, gain, kind, earlier=None, chunk=256):
    rows, width = dhid.shape
    shape = jax.ShapeDtypeStruct
    vector = pl.BlockSpec((1, width), lambda i: (0, 0))
    outs = (shape((rows, width), kind), shape((1, width), jnp.float32), shape((1, width), jnp.float32))
    inputs = [dhid, state, weight, gain, *gmix]
    each = rows // chunk // len(gmix)
    specs = [
        rows_of(chunk, width),
        rows_of(chunk, width),
        pl.BlockSpec((3, width, width), lambda i: (0, 0, 0), pipeline_mode=pl.Buffered(1)),
        whole(gain),
    ]
    for index in range(len(gmix)):
        specs.append(
            pl.BlockSpec(
                (chunk, 3 * width),
                lambda i, index=index: (jnp.clip(i - index * each, 0, each - 1), 0),
            )
        )
    if earlier is not None:
        inputs += list(earlier)
        specs += [vector, vector]
    return pl.pallas_call(
        functools.partial(attention_input_kernel, earlier is not None, len(gmix)),
        grid=(rows // chunk,),
        out_shape=outs,
        in_specs=specs,
        out_specs=[rows_of(chunk, width), vector, vector],
        scratch_shapes=[pltpu.VMEM((chunk, 3 * width), jnp.bfloat16)],
        compiler_params=params(),
        cost_estimate=cost(6 * rows * width * width, 0, *inputs, *outs),
        name="attention_input",
    )(*in_hbm(inputs[:4]), *gmix, *in_hbm(inputs[4 + len(gmix) :]))


def place_small_kernel(sizes, me_ref, *refs):
    smalls, outs = (refs[:4], refs[4:])
    dp = me_ref[0] // 2
    slot = lax.broadcasted_iota(jnp.int32, (16, 1), 0)
    owner = ((slot % 4) * 4 + (slot // 8) * 2 + slot // 4 % 2) ^ dp
    for index, (size, out_ref) in enumerate(zip(sizes, outs)):
        width = 16 * size
        lane = lax.broadcasted_iota(jnp.int32, (256, width), 0)
        column = lax.broadcasted_iota(jnp.int32, (256, width), 1)
        spread = (column % size == lane).astype(jnp.bfloat16)
        rows = jnp.concatenate([ref[z, index : index + 1] for ref in smalls for z in range(4)], axis=0)
        spread_rows = dot(rows, spread)
        column = lax.broadcasted_iota(jnp.int32, (1, width), 1)
        out_ref[...] = jnp.sum(
            jnp.where(column // size == owner, spread_rows, 0.0), axis=0, keepdims=True
        )


def place_small(me, smalls, sizes):
    return pl.pallas_call(
        functools.partial(place_small_kernel, sizes),
        out_shape=[jax.ShapeDtypeStruct((1, 16 * size), jnp.float32) for size in sizes],
        in_specs=[SMEM] + [pl.BlockSpec(memory_space=pltpu.VMEM)] * len(smalls),
        out_specs=[pl.BlockSpec(memory_space=pltpu.VMEM)] * len(sizes),
        name="place_small",
    )(me, *smalls)


def swap(value, bits):
    return lax.ppermute(value, BOTH, [(i, i ^ bits) for i in range(32)])


CORE, X, Y, Z1, Z2, Z3 = (1, 2, 4, 8, 16, 24)


def place_kernel(slots, me_ref, *refs):
    sources, (out, sems) = (refs[: len(slots)], refs[len(slots) :])
    me = me_ref[0]
    copies = []
    for source, rels in zip(sources, slots):
        for inner, rel in enumerate(rels):
            copies.append(
                pltpu.make_async_copy(
                    source.at[inner], out.at[:, rel ^ me], sems.at[len(copies)]
                )
            )
    for copy in copies:
        copy.start()
    for copy in copies:
        copy.wait()


def place(me, sources, slots):
    placed = pl.pallas_call(
        functools.partial(place_kernel, slots),
        out_shape=jax.ShapeDtypeStruct((4, 32, 24, FEATURES), jnp.bfloat16),
        in_specs=[SMEM] + [pl.BlockSpec(memory_space=pl.ANY)] * len(sources),
        out_specs=pl.BlockSpec(memory_space=pltpu.VMEM),
        scratch_shapes=[pltpu.SemaphoreType.DMA((32,))],
        name="place",
    )(me, *sources)
    return placed.reshape(4, FEATURES, FEATURES)


def after(values, *others):
    return lax.optimization_barrier((values, others))[0]


def gather_first(piece, small, me):
    base = (0, Z1, Z2, Z3)
    pieces = lax.optimization_barrier(
        [piece] + [swap(piece, bits) for bits in base[1:]]
        + [small] + [swap(small, bits) for bits in base[1:]]
    )
    four, small = (jnp.concatenate(pieces[:4]), jnp.concatenate(pieces[4:]))
    four_x, four_y, four_core, small_x, small_y = lax.optimization_barrier(
        (swap(four, X), swap(four, Y), swap(four, CORE), swap(small, X), swap(small, Y))
    )
    near_xy, far_xy, x_core, y_core, small_xy = lax.optimization_barrier(
        (
            swap(four_y[:2], X), swap(four_x[2:], Y), swap(four_x, CORE), swap(four_y, CORE),
            swap(small_y, X),
        )
    )
    parts = [four, four_x, four_y, near_xy, far_xy]
    parts += [four_core, x_core, y_core, swap(near_xy, CORE), swap(far_xy, CORE)]
    slots = [base] + [tuple(rel ^ bits for rel in base) for bits in (X, Y)]
    slots += [(X ^ Y, X ^ Y ^ Z1), (X ^ Y ^ Z2, X ^ Y ^ Z3)]
    slots += [tuple(rel ^ CORE for rel in rels) for rels in slots]
    return (place(me, parts, slots), (small, small_x, small_y, small_xy))


def pick(array, axis, index):
    return lax.dynamic_index_in_dim(array, index, axis, keepdims=False)


def low(value):
    return value.astype(jnp.bfloat16)


def wide(value):
    return value.astype(jnp.float32)


def add(*terms):
    total = wide(terms[0])
    for term in terms[1:]:
        total = total + wide(term)
    return total


def device_at(z_pair, z_low, y, x):
    return z_pair * 8 + z_low * 4 + y * 2 + x


def total(*terms):
    result = terms[0].astype(jnp.float32)
    for term in terms[1:]:
        result = result + term.astype(jnp.float32)
    return result


def first_sums_kernel(views, spot_ref, *refs):
    mine, got = (refs[:views], refs[views : 2 * views])
    near_sent, far_sent, near_kept, far_kept = refs[2 * views :]
    z_pair, y, x = (spot_ref[0], spot_ref[2], spot_ref[3])
    for low_z in range(2):
        for other in range(2):
            for out, device in (
                (near_sent, device_at(z_pair, low_z, other, 1 - x)),
                (far_sent, device_at(1 - z_pair, low_z, 1 - y, other)),
                (near_kept, device_at(z_pair, low_z, other, x)),
                (far_kept, device_at(1 - z_pair, low_z, y, other)),
            ):
                start = 0
                for left, right in zip(mine, got):
                    count = left.shape[1]
                    out[low_z, other, start : start + count] = total(
                        left[device], right[device]
                    ).astype(jnp.bfloat16)
                    start += count


def second_sums_kernel(spot_ref, near, far, near_in, far_in, *outs):
    near_sent, far_sent, near_kept, far_kept = outs
    y, x = (spot_ref[2], spot_ref[3])
    for low_z in range(2):
        for out, kept, got, index in (
            (near_sent, near, near_in, 1 - y),
            (far_sent, far, far_in, 1 - x),
            (near_kept, near, near_in, y),
            (far_kept, far, far_in, x),
        ):
            out[low_z] = total(kept[low_z, index], got[low_z, index]).astype(jnp.bfloat16)


def third_sums_kernel(spot_ref, near, far, near_in, far_in, first, second, third, kept):
    low_z = spot_ref[1]
    first[...] = total(near[1 - low_z], near_in[1 - low_z]).astype(jnp.bfloat16)
    second[...] = total(far[low_z], far_in[low_z]).astype(jnp.bfloat16)
    third[...] = total(far[1 - low_z], far_in[1 - low_z]).astype(jnp.bfloat16)
    kept[...] = total(near[low_z], near_in[low_z])


def assemble_kernel(layouts, core_ref, half_ref, other_ref, *outs):
    core = core_ref[0]
    half, other = (half_ref[...], other_ref[...])
    left = jnp.where(core == 0, half, other)
    right = jnp.where(core == 0, other, half)
    start, wide_half = (0, half.shape[1])
    for (blocks, rows), out in zip(layouts, outs):
        for block in range(blocks):
            part = slice(start, start + rows)
            column = 2 * block * wide_half
            out[:, column : column + wide_half] = left[part]
            out[:, column + wide_half : column + 2 * wide_half] = right[part]
            start += rows


def pack_rows_kernel(unused_ref, *refs):
    *parts, out = refs
    start = 0
    for part in parts:
        if len(part.shape) == 2:
            out[start : start + 1] = part[...]
            start += 1
        else:
            for index in range(part.shape[0]):
                out[start : start + 1] = part[index]
                start += 1


def in_vmem(kernel, name, outs, *args):
    vmem = pl.BlockSpec(memory_space=pltpu.VMEM)
    return pl.pallas_call(
        kernel,
        out_shape=outs,
        in_specs=[SMEM] + [vmem] * (len(args) - 1),
        out_specs=[vmem] * len(outs),
        compiler_params=params(),
        cost_estimate=cost(0, 0, *args, *outs),
        name=name,
    )(*args)


class Reduction:
    def __init__(self, spot, mine, theirs):
        self.spot = spot
        self.mine = list(mine)
        self.got = [swap(part, CORE) for part in theirs]
        self.count = sum(part.shape[1] for part in self.mine)
        self.width = self.mine[0].shape[2]

    def like(self, *lead, kind=jnp.bfloat16):
        return jax.ShapeDtypeStruct((*lead, self.count, self.width), kind)

    def first(self):
        near_sent, far_sent, *self.kept = in_vmem(
            functools.partial(first_sums_kernel, len(self.mine)),
            "first_sums",
            [self.like(2, 2)] * 4,
            self.spot,
            *self.mine,
            *self.got,
        )
        self.got = [swap(near_sent, X), swap(far_sent, Y)]
        return self.kept

    def second(self):
        near_sent, far_sent, *self.kept = in_vmem(
            second_sums_kernel, "second_sums", [self.like(2)] * 4, self.spot, *self.kept, *self.got
        )
        self.got = [swap(near_sent, Y), swap(far_sent, X)]
        return self.kept

    def third(self):
        *sent, kept = in_vmem(
            third_sums_kernel,
            "third_sums",
            [self.like()] * 3 + [self.like(kind=jnp.float32)],
            self.spot,
            *self.kept,
            *self.got,
        )
        self.kept = [kept]
        self.got = [swap(part, bits) for part, bits in zip(sent, (Z1, Z2, Z3))]
        return self.kept

    def fourth(self):
        half = total(*self.kept, *self.got)
        self.kept, self.got = ([half], [swap(half, CORE)])

    def whole(self, core, layouts):
        outs = [
            jax.ShapeDtypeStruct((rows, 2 * self.width * blocks), jnp.float32)
            for blocks, rows in layouts
        ]
        return in_vmem(
            functools.partial(assemble_kernel, layouts), "assemble", outs, core, *self.kept, *self.got
        )


def own_small(small, dp):
    def own(start, rows):
        vector = small[start : start + rows].reshape(-1)
        size = vector.shape[0] // 16
        return lax.dynamic_slice_in_dim(vector, dp * size, size)

    return [own(0, 1), own(1, 1), own(2, 3), own(5, 1), own(6, 1), own(7, 1), own(8, 4), own(12, 1)]


def gather_all(weights, spot, me):
    gain_a, shift_a, qkv, qbias, out, obias, gain_m, shift_m, fc, fbias, proj, pbias = weights
    core = spot[4]

    def half(weight):
        part = lax.dynamic_slice_in_dim(weight, core * 24, 24, 0)
        return jnp.transpose(part.reshape(24, -1, FEATURES), (1, 0, 2))

    columns = lax.dynamic_slice_in_dim(fc, core * 2 * FEATURES, 2 * FEATURES, 1)
    columns = jnp.transpose(columns.reshape(48, 2, FEATURES), (1, 0, 2))
    across = lax.dynamic_slice_in_dim(proj, core * 96, 96, 0).reshape(2, 48, FEATURES)
    mlp = lax.all_gather(jnp.concatenate([columns, across]), BOTH)
    mlp = mlp.reshape(16, 2, 4, 48, FEATURES)
    vectors = [gain_a, shift_a, qbias, obias, gain_m, shift_m, fbias, pbias]
    sizes = tuple(vector.shape[0] for vector in vectors)
    small = jnp.stack([jnp.pad(v, (0, 256 - size)) for v, size in zip(vectors, sizes)])
    first, smalls = gather_first(jnp.concatenate([half(qkv), half(out)])[None], small[None], me)
    return (first, mlp, *place_small(me, smalls, sizes))


def gather_plain(weights):
    whole_ones = [lax.all_gather(weight, "dp", axis=0, tiled=True) for weight in weights]
    gain_a, shift_a, qkv, qbias, out, obias, gain_m, shift_m, fc, fbias, proj, pbias = whole_ones

    def blocks(weight):
        return jnp.transpose(weight.reshape(FEATURES, -1, FEATURES), (1, 0, 2))

    rows = [
        wide(v).reshape(1, -1)
        for v in (gain_a, shift_a, qbias, obias, gain_m, shift_m, fbias, pbias)
    ]
    first = jnp.concatenate([blocks(qkv), blocks(out)])
    fc = blocks(fc).reshape(2, 2, 16, 48, FEATURES)
    fc = jnp.transpose(fc, (2, 0, 1, 3, 4))
    mlp = jnp.concatenate([fc, proj.reshape(16, 2, 2, 48, FEATURES)], axis=2)
    return (first, mlp, *rows)


def reduce_plain(matrices, small):
    def joined(left, right):
        both = jnp.concatenate([left, right], axis=-1)
        if both.ndim == 4:
            both = jnp.transpose(both, (0, 2, 1, 3)).reshape(FEATURES, -1)
        return both.reshape(-1, both.shape[-1])

    qkv, out, fc, proj = [joined(*pair) for pair in matrices]
    gain_a, shift_a, qbias, obias, gain_m, shift_m, fbias, pbias = [v.reshape(-1) for v in small]
    values = (
        gain_a, shift_a, qkv, qbias, out, obias, gain_m, shift_m, fc, fbias, proj, pbias
    )
    return tuple(
        wide(lax.psum(low(lax.psum_scatter(wide(v), "dp", scatter_dimension=0, tiled=True)), "rep"))
        for v in values
    )


def forward(tokens, lengths, count, back, weights):
    weight, mlp, gain_a, shift_a, qbias, obias, gain_m, shift_m, fbias, pbias = weights
    state, kept = (tokens, [])
    for use in range(USES):
        normed_a, mixed, att, lse, hidden, normed_m = attention_forward(
            lengths, state, count, back, gain_a, shift_a, weight, qbias, obias, gain_m, shift_m
        )
        expanded, after_mlp = (None, None)
        if use < USES - 1:
            expanded, after_mlp = mlp_forward(hidden, normed_m, mlp, fbias, pbias)
        kept.append((state, normed_a, mixed, att, lse, hidden, normed_m, expanded))
        state = after_mlp
    return kept


def shards(custom, tokens, doc_lengths, cotangent, *weights):
    micro, count, width = tokens.shape
    dp, core = (lax.axis_index("dp"), lax.axis_index("rep"))
    spot = (dp // 8, dp // 4 % 2, dp // 2 % 2, dp % 2, core)
    me = (dp * 2 + core).astype(jnp.int32).reshape(1)
    places = jnp.stack(spot).astype(jnp.int32)
    side = core.astype(jnp.int32).reshape(1) if custom else jnp.zeros((1,), jnp.int32)
    back = -(-(LONGEST - 1) // BLOCK)
    lengths = doc_lengths.reshape(micro, doc_lengths.shape[-1])
    whole_ones = gather_all(weights, spot, me) if custom else gather_plain(weights)
    kept = forward(tokens.reshape(micro * count, width), lengths, count, back, whole_ones)
    weight, mlp, gain_a, gain_m = (whole_ones[0], whole_ones[1], whole_ones[2], whole_ones[6])
    grad, mlp_terms, terms, norm = (cotangent.reshape(micro * count, width), None, None, None)
    delayed = None
    for use in range(USES - 1, -1, -1):
        before, normed_a, mixed, att, lse, hidden, normed_m, expanded = kept[use]
        last = use == USES - 1
        dhid, *mlp_terms = mlp_backward(
            side, grad, hidden, normed_m, att, expanded, mlp, gain_m, mlp_terms,
            whole_ones[-2:] if last else None,
        )
        if last:
            state, (dhid, *mlp_terms) = (dhid, mlp_terms)
        sending = custom and use == 0
        if delayed is not None:
            terms = delayed()
        if sending:
            fc_mine, fc_theirs, proj_mine, proj_theirs, out_mine, out_theirs = [
                part.reshape(16, -1, part.shape[-1]) for part in mlp_terms[:6]
            ]
            sums = Reduction(
                places, (fc_mine, proj_mine, out_mine), (fc_theirs, proj_theirs, out_theirs)
            )
            sums.got, terms = lax.optimization_barrier((sums.got, terms))
            dhid = after(dhid, sums.first())
        if use:
            gmix, grad, *norm = attention_backward_all(
                lengths, dhid, count, back, att, mixed, lse, weight, before, gain_a
            )
            delayed = functools.partial(attention_terms, side, normed_a, [gmix])
            continue
        gmix = [
            attention_backward(index, lengths, dhid, count, back, att, mixed, lse, weight)
            for index in range(micro)
        ]
        terms = attention_terms(side, normed_a, gmix, terms)
        if sending:
            qkv_sums = Reduction(
                places, *[(part.reshape(16, -1, part.shape[-1]),) for part in terms[:2]]
            )
            sums.got, terms = lax.optimization_barrier((sums.got, terms))
            gmix = after(gmix, sums.second())
        grad, *norm = attention_input(dhid, before, gmix, weight, gain_a, jnp.bfloat16, norm)
        if sending:
            sums.got, qkv_sums.got, norm = lax.optimization_barrier(
                (sums.got, qkv_sums.got, norm)
            )
    small = (norm[0], norm[1], terms[2], mlp_terms[6], mlp_terms[9], mlp_terms[10])
    small += (mlp_terms[7], mlp_terms[8])
    if custom:
        (small,) = in_vmem(
            pack_rows_kernel, "pack_rows", [jax.ShapeDtypeStruct((13, width), jnp.float32)], side, *small
        )
        qkv_sums.first()
        sums.third()
        small = small + swap(small, CORE)
        got = swap(small, X)
        qkv_sums.got, got = lax.optimization_barrier((qkv_sums.got, got))
        qkv_sums.second()
        small = small + got
        got = swap(small, Y)
        qkv_sums.got, got = lax.optimization_barrier((qkv_sums.got, got))
        qkv_sums.third()
        small = small + got
        got = [swap(small, bits) for bits in (Z1, Z2, Z3)]
        sums.fourth()
        qkv_sums.got, got = lax.optimization_barrier((qkv_sums.got, got))
        qkv_sums.fourth()
        fc, proj, out = sums.whole(side, ((4, 48), (1, 192), (1, 48)))
        (qkv,) = qkv_sums.whole(side, ((3, 48),))
        small = own_small(total(small, *got), dp)
        gain_a, shift_a, qbias, obias, gain_m, shift_m, fbias, pbias = small
        final = (
            gain_a, shift_a, qkv, qbias, out, obias, gain_m, shift_m, fc, fbias, proj, pbias
        )
    else:
        matrices = (terms[:2], mlp_terms[4:6], mlp_terms[:2], mlp_terms[2:4])
        final = reduce_plain(matrices, small)
    return (state.reshape(tokens.shape), grad.reshape(tokens.shape), *final)


def solution(mesh):
    custom = mesh.shape["dp"] == 16 and mesh.shape["rep"] == 2
    placed = tuple(
        P("dp", None) if index in (2, 4, 8, 10) else P("dp") for index in range(12)
    )
    rows = P(None, BOTH, None)
    return jax.shard_map(
        functools.partial(shards, custom),
        mesh=mesh,
        in_specs=(rows, rows, rows, *placed),
        out_specs=(rows, rows, *placed),
        check_vma=False,
    )
```

```python
import functools
import math

import jax
import jax.numpy as jnp
from jax import lax
from jax.experimental import pallas as pl
from jax.experimental.pallas import tpu as pltpu
from jax.sharding import PartitionSpec as P

H = 12
HD = 64
USES = 2
LONGEST = 256
BOTH = ("dp", "rep")


NORM_EPS = 1e-05
BLOCK = 128
FEATURES = H * HD
VMEM_LIMIT = 40 << 20
COST_SCALE = 8


def dot(left, right):
    return jnp.dot(left, right, preferred_element_type=jnp.float32)


def transposed_dot(left, right):
    return lax.dot_general(
        left, right, (((0,), (0,)), ((), ())), preferred_element_type=jnp.float32
    )


def dot_transposed(left, right):
    return lax.dot_general(
        left, right, (((1,), (1,)), ((), ())), preferred_element_type=jnp.float32
    )


def norm_parts(values):
    center = values - jnp.mean(values, axis=-1, keepdims=True)
    spread = jnp.mean(center * center, axis=-1, keepdims=True)
    scale = lax.rsqrt(spread + NORM_EPS)
    return (center * scale, scale)


def norm_back(normed, scale, gain, grad):
    inner = grad * gain
    first = jnp.mean(inner, axis=-1, keepdims=True)
    second = jnp.mean(inner * normed, axis=-1, keepdims=True)
    return (inner - first - normed * second) * scale


def segment_of(places, lengths, docs):
    end = jnp.int32(0)
    segment = jnp.zeros(places.shape, jnp.int32)
    for doc in range(docs):
        end = end + lengths[doc]
        segment = segment + (places >= end).astype(jnp.int32)
    return segment


def allowed_bias(count, lengths, docs, query_axis):
    query_shape = (count, 1) if query_axis == 0 else (1, count)
    key_shape = (1, count) if query_axis == 0 else (count, 1)
    query = lax.broadcasted_iota(jnp.int32, query_shape, query_axis)
    key = lax.broadcasted_iota(jnp.int32, key_shape, 1 - query_axis)
    same = segment_of(query, lengths, docs) == segment_of(key, lengths, docs)
    return jnp.where(same & (key <= query), 0.0, -1e30).astype(jnp.float32)


GROUP = 4
LANES = GROUP * HD


def head_split(array):
    head = lax.broadcasted_iota(jnp.int32, array.shape, 1) // HD
    zero = jnp.zeros_like(array)
    return jnp.concatenate([jnp.where(head == h, array, zero) for h in range(GROUP)], axis=0)


def head_join(stacked):
    count = stacked.shape[0] // GROUP
    head = lax.broadcasted_iota(jnp.int32, (count, LANES), 1) // HD
    joined = stacked[:count]
    for h in range(1, GROUP):
        joined = jnp.where(head == h, stacked[h * count : (h + 1) * count], joined)
    return joined


def attention_forward_kernel(
    docs,
    back,
    lengths_ref,
    state_ref,
    gain_ref,
    shift_ref,
    weight_ref,
    qbias_ref,
    obias_ref,
    gain2_ref,
    shift2_ref,
    normed_ref,
    mixed_ref,
    att_ref,
    lse_ref,
    hidden_ref,
    normed2_ref,
    bias_ref,
    lse_cols,
):
    micro = pl.program_id(0)
    state = state_ref[...].astype(jnp.float32)
    count = state.shape[0]
    normed = (norm_parts(state)[0] * gain_ref[...] + shift_ref[...]).astype(jnp.bfloat16)
    normed_ref[...] = normed
    for part in range(3):
        columns = slice(part * FEATURES, (part + 1) * FEATURES)
        mixed_ref[:, columns] = (dot(normed, weight_ref[part]) + qbias_ref[:, columns]).astype(
            jnp.bfloat16
        )
    bias_ref[...] = allowed_bias(count, [lengths_ref[micro, d] for d in range(docs)], docs, 0)
    lse_cols[...] = jnp.zeros_like(lse_cols)

    def one_group(group, carry):
        lanes = pl.multiple_of(group * LANES, LANES)
        for block in range(count // BLOCK):
            rows = slice(block * BLOCK, (block + 1) * BLOCK)
            low_key = max(0, block - back) * BLOCK
            keys = slice(low_key, (block + 1) * BLOCK)
            query = head_split(mixed_ref[rows, pl.ds(lanes, LANES)])
            key = mixed_ref[keys, pl.ds(FEATURES + lanes, LANES)]
            value = mixed_ref[keys, pl.ds(2 * FEATURES + lanes, LANES)]
            scores = dot_transposed(query, key)
            bias = bias_ref[rows, keys]
            scores = scores * 0.125 + jnp.concatenate([bias] * GROUP, axis=0)
            top = jnp.max(scores, axis=-1, keepdims=True)
            expo = jnp.exp(scores - top)
            total_expo = jnp.sum(expo, axis=-1, keepdims=True)
            result = dot(expo.astype(jnp.bfloat16), value) / total_expo
            att_ref[rows, pl.ds(lanes, LANES)] = head_join(result).astype(jnp.bfloat16)
            lse = top + jnp.log(total_expo)
            lane = lax.broadcasted_iota(jnp.int32, (BLOCK, 128), 1)
            for h in range(GROUP):
                lse_cols[rows, :] += jnp.where(
                    lane == GROUP * group + h, lse[h * BLOCK : (h + 1) * BLOCK], 0.0
                )
        return carry

    lax.fori_loop(0, H // GROUP, one_group, 0, unroll=H // GROUP)
    lse = jnp.transpose(lse_cols[...])
    for index in range(H):
        lse_ref[index] = lse[index : index + 1]
    hidden = state + (dot(att_ref[...], weight_ref[3]) + obias_ref[...])
    hidden_ref[...] = hidden
    normed2_ref[...] = (norm_parts(hidden)[0] * gain2_ref[...] + shift2_ref[...]).astype(
        jnp.bfloat16
    )


def whole(array):
    dims = len(array.shape)
    return pl.BlockSpec(array.shape, lambda *unused: (0,) * dims, pipeline_mode=pl.Buffered(1))


SMEM = pl.BlockSpec(memory_space=pltpu.SMEM)


def in_hbm(arrays):
    return [pltpu.with_memory_space_constraint(array, pltpu.HBM) for array in arrays]


def rows_of(count, width):
    return pl.BlockSpec((count, width), lambda i: (i, 0))


def params(limit=VMEM_LIMIT):
    return pltpu.CompilerParams(vmem_limit_bytes=limit)


def cost(flops, transcendentals, *arrays):
    size = sum(math.prod(a.shape) * a.dtype.itemsize for a in arrays)
    return pl.CostEstimate(
        flops=int(flops) // COST_SCALE,
        transcendentals=int(transcendentals) // COST_SCALE,
        bytes_accessed=int(size) // COST_SCALE,
    )


def attention_forward(lengths, state, count, back, gain, shift, weight, qbias, obias, gain2, shift2):
    rows = state.shape[0]
    micro, docs = lengths.shape
    width = FEATURES
    shape = pltpu.HBM
    outs = (
        shape((rows, width), jnp.bfloat16),
        shape((rows, 3 * width), jnp.bfloat16),
        shape((rows, width), jnp.bfloat16),
        shape((micro * H, 1, count), jnp.float32),
        shape((rows, width), jnp.float32),
        shape((rows, width), jnp.bfloat16),
    )
    weights = (gain, shift, weight, qbias, obias, gain2, shift2)
    return pl.pallas_call(
        functools.partial(attention_forward_kernel, docs, back),
        grid=(micro,),
        out_shape=outs,
        in_specs=[SMEM, rows_of(count, width)] + [whole(w) for w in weights],
        out_specs=(
            rows_of(count, width),
            rows_of(count, 3 * width),
            rows_of(count, width),
            pl.BlockSpec((H, 1, count), lambda i: (i, 0, 0)),
            rows_of(count, width),
            rows_of(count, width),
        ),
        scratch_shapes=[
            pltpu.VMEM((count, count), jnp.float32),
            pltpu.VMEM((count, 128), jnp.float32),
        ],
        compiler_params=params(),
        cost_estimate=cost(
            8 * rows * width * width + 4 * rows * count * width, rows * count * H, state, *weights, *outs
        ),
        name="attention_forward",
    )(lengths, *in_hbm((state, *weights)))


GELU_C = 0.7978845608028654
GELU_K = 0.044715 * GELU_C


def gelu_gate(value):
    square = value * value
    gate = 0.5 * jnp.tanh(value * (GELU_C + GELU_K * square)) + 0.5
    return (gate, square)


def mlp_forward_kernel(
    hidden_ref, normed_ref, fc_ref, fbias_ref, proj_ref, pbias_ref, expanded_ref, state_ref
):
    chunk = 256

    @pl.when(pl.program_id(0) == 0)
    def _():
        state_ref[...] = hidden_ref[...] + pbias_ref[...]

    for start in range(0, normed_ref.shape[0], chunk):
        rows = slice(start, start + chunk)
        expanded = dot(normed_ref[rows, :], square_of(fc_ref)) + fbias_ref[...]
        expanded_ref[rows, :] = expanded.astype(expanded_ref.dtype)
        gate, unused = gelu_gate(expanded)
        activated = (expanded * gate).astype(jnp.bfloat16)
        state_ref[rows, :] += dot(activated, square_of(proj_ref))


DEVICE_GROUPS = 16


def square_of(ref):
    return ref[...].reshape(FEATURES, FEATURES)


def fc_at(step):
    return jnp.minimum(step, 3)


FC_BLOCK = pl.BlockSpec((16, 1, 1, 48, FEATURES), lambda i: (0, fc_at(i) // 2, fc_at(i) % 2, 0, 0))
PROJ_BLOCK = pl.BlockSpec((4, 2, 2, 48, FEATURES), lambda i: (fc_at(i), 0, 1, 0, 0))


def mlp_forward(hidden, normed, mlp, fbias, pbias):
    rows, width = hidden.shape
    block = width
    hidden_units = 4 * block
    shape = pltpu.HBM
    outs = (
        shape((rows, hidden_units), jnp.bfloat16),
        shape((rows, width), jnp.float32),
    )
    specs = (
        pl.BlockSpec((rows, block), lambda i: (0, i)),
        pl.BlockSpec((rows, width), lambda i: (0, 0)),
    )
    return pl.pallas_call(
        mlp_forward_kernel,
        grid=(hidden_units // block,),
        out_shape=outs,
        in_specs=[
            whole(hidden),
            whole(normed),
            FC_BLOCK,
            pl.BlockSpec((1, block), lambda i: (0, i)),
            PROJ_BLOCK,
            whole(pbias),
        ],
        out_specs=specs,
        compiler_params=params(),
        cost_estimate=cost(
            4 * rows * width * hidden_units, rows * hidden_units, hidden, normed, mlp, *outs
        ),
        name="mlp_forward",
    )(*in_hbm((hidden, normed, mlp, fbias, mlp, pbias)))


def transposed_dot(left, right):
    return lax.dot_general(
        left, right, (((0,), (0,)), ((), ())), preferred_element_type=jnp.float32
    )


def dot_transposed(left, right):
    return lax.dot_general(
        left, right, (((1,), (1,)), ((), ())), preferred_element_type=jnp.float32
    )


def store_halves(core, value, mine_ref, theirs_ref, earlier):
    half = value.shape[1] // 2
    left, right = (value[:, :half], value[:, half:])
    mine = jnp.where(core == 0, left, right)
    theirs = jnp.where(core == 0, right, left)
    shape = mine_ref.shape
    mine, theirs = (mine.reshape(shape), theirs.reshape(shape))
    if earlier is not None:
        mine = mine + earlier[0][...].astype(jnp.float32)
        theirs = theirs + earlier[1][...].astype(jnp.float32)
    mine_ref[...] = mine.astype(mine_ref.dtype)
    theirs_ref[...] = theirs.astype(theirs_ref.dtype)


def mlp_backward_kernel(
    more,
    forward,
    core_ref,
    grad_ref,
    hidden_ref,
    normed_ref,
    att_ref,
    *rest,
):
    if forward:
        fbias_ref, pbias_ref, fc_ref, proj_ref, gain_ref, *rest = rest
    else:
        expanded_ref, fc_ref, proj_ref, gain_ref, *rest = rest
    earlier = rest[:11] if more else (None,) * 11
    if more:
        rest = rest[11:]
    if forward:
        final_ref, *rest, state_ref = rest
    (
        dhid_ref,
        fc_mine,
        fc_theirs,
        proj_mine,
        proj_theirs,
        out_mine,
        out_theirs,
        dobias_ref,
        dfbias_ref,
        dpbias_ref,
        dgain_ref,
        dshift_ref,
        low_ref,
        normed_t,
        acc_ref,
        act_ref,
        ge_ref,
        hidden_buf,
        att_buf,
        sems,
    ) = rest
    step = pl.program_id(0)
    core = core_ref[0]
    rows = grad_ref.shape[0]
    blocks = pl.num_programs(0) - 1
    chunk = 256
    chunks = [slice(start, start + chunk) for start in range(0, rows, chunk)]
    late = [
        pltpu.make_async_copy(hidden_ref, hidden_buf, sems.at[0]),
        pltpu.make_async_copy(att_ref, att_buf, sems.at[1]),
    ]

    @pl.when(step == 0)
    def _():
        for copy in late:
            copy.start()
        low_grad = grad_ref[...].astype(jnp.bfloat16)
        low_ref[...] = low_grad
        dpbias = jnp.sum(low_grad.astype(jnp.float32), axis=0, keepdims=True)
        dpbias_ref[...] = dpbias + earlier[8][...] if more else dpbias
        normed_t[...] = jnp.transpose(normed_ref[...])
        acc_ref[...] = jnp.zeros_like(acc_ref)
        if forward:
            state_ref[...] = jnp.zeros_like(state_ref)

    @pl.when(step < blocks)
    def _():
        bias_sum = jnp.zeros(dfbias_ref.shape[1:], jnp.float32)
        for part in chunks:
            grad_act = dot_transposed(low_ref[part, :], square_of(proj_ref))
            if forward:
                value = dot(normed_ref[part, :], square_of(fc_ref)) + fbias_ref[...]
            else:
                value = expanded_ref[part, :].astype(jnp.float32)
            gate, square = gelu_gate(value)
            act = value * gate
            slope = gate + act * (1.0 - gate) * (2 * GELU_C + 6 * GELU_K * square)
            activated = act.astype(jnp.bfloat16)
            act_ref[part, :] = activated
            if forward:
                state_ref[part, :] += dot(activated, square_of(proj_ref))
            grad_exp = (grad_act * slope).astype(jnp.bfloat16)
            ge_ref[part, :] = grad_exp
            bias_sum = bias_sum + jnp.sum(grad_exp.astype(jnp.float32), axis=0, keepdims=True)
            acc_ref[part, :] += dot_transposed(grad_exp, square_of(fc_ref))
        dfbias_ref[0] = bias_sum + earlier[7][0] if more else bias_sum
        dproj = transposed_dot(act_ref[...], low_ref[...])
        store_halves(core, dproj, proj_mine, proj_theirs, earlier[2:4] if more else None)
        dfc = dot(normed_t[...], ge_ref[...])
        store_halves(core, dfc, fc_mine, fc_theirs, earlier[:2] if more else None)

    @pl.when(step == blocks)
    def _():
        for copy in late:
            copy.wait()
        dgain = jnp.zeros(dgain_ref.shape, jnp.float32)
        dshift, dobias = (dgain, dgain)
        copies = []
        for index, part in enumerate(chunks):
            hidden = hidden_buf[part, :]
            if forward:
                final = hidden + (state_ref[part, :] + pbias_ref[...])
                final_ref[part, :] = final.astype(jnp.bfloat16)
            normed, scale = norm_parts(hidden)
            grad_norm = acc_ref[part, :]
            dgain = dgain + jnp.sum(grad_norm * normed, axis=0, keepdims=True)
            dshift = dshift + jnp.sum(grad_norm, axis=0, keepdims=True)
            dhid = grad_ref[part, :].astype(jnp.float32) + norm_back(
                normed, scale, gain_ref[...], grad_norm
            )
            hidden_buf[part, :] = dhid
            copies.append(
                pltpu.make_async_copy(
                    hidden_buf.at[part, :], dhid_ref.at[part, :], sems.at[2 + index]
                )
            )
            copies[-1].start()
            low_dhid = dhid.astype(jnp.bfloat16)
            low_ref[part, :] = low_dhid
            dobias = dobias + jnp.sum(low_dhid.astype(jnp.float32), axis=0, keepdims=True)
        dgain_ref[...] = dgain + earlier[9][...] if more else dgain
        dshift_ref[...] = dshift + earlier[10][...] if more else dshift
        dobias_ref[...] = dobias + earlier[6][...] if more else dobias
        dout = transposed_dot(att_buf[...], low_ref[...])
        store_halves(core, dout, out_mine, out_theirs, earlier[4:6] if more else None)
        for copy in copies:
            copy.wait()


def mlp_backward(core, grad, hidden, normed, att, expanded, mlp, gain, earlier=None, biases=None):
    rows, width = hidden.shape
    blocks, block = (4, width)
    shape = pltpu.HBM
    groups = DEVICE_GROUPS
    each = width // groups
    fc_half = shape((groups, blocks, each, width // 2), jnp.bfloat16)
    proj_half = shape((blocks * width, width // 2), jnp.bfloat16)
    out_half = shape((groups, each, width // 2), jnp.bfloat16)
    row = shape((1, width), jnp.float32)
    outs = (
        shape((rows, width), jnp.float32),
        fc_half,
        fc_half,
        proj_half,
        proj_half,
        out_half,
        out_half,
        row,
        shape((blocks, 1, block), jnp.float32),
        row,
        row,
        row,
    )
    fc_spec = pl.BlockSpec((groups, None, each, width // 2), lambda i: (0, jnp.minimum(i, 3), 0, 0))
    proj_spec = pl.BlockSpec((width, width // 2), lambda i: (jnp.minimum(i, 3), 0))
    out_spec = pl.BlockSpec((groups, each, width // 2), lambda i: (0, 0, 0))
    bias = pl.BlockSpec((1, 1, block), lambda i: (jnp.minimum(i, 3), 0, 0))
    vector = pl.BlockSpec((1, width), lambda i: (0, 0))
    inputs = [grad, hidden, normed, att]
    raw = pl.BlockSpec(memory_space=pltpu.HBM)
    specs = [whole(grad), raw, whole(normed), raw]
    out_specs = [raw]
    scratch = []
    if biases is None:
        inputs.append(expanded)
        specs.append(pl.BlockSpec((rows, block), lambda i: (0, jnp.minimum(i, 3))))
    else:
        inputs += list(biases)
        specs += [pl.BlockSpec((1, block), lambda i: (0, jnp.minimum(i, 3))), whole(biases[1])]
        outs = (shape((rows, width), jnp.bfloat16), *outs)
        out_specs = [pl.BlockSpec((rows, width), lambda i: (0, 0)), raw]
        scratch = [pltpu.VMEM((rows, width), jnp.float32)]
    inputs += [mlp, mlp, gain]
    specs += [FC_BLOCK, PROJ_BLOCK, whole(gain)]
    summed = [fc_spec, fc_spec, proj_spec, proj_spec, out_spec, out_spec, vector, bias]
    summed += [vector, vector, vector]
    if earlier is not None:
        inputs += list(earlier)
        specs += summed
    return pl.pallas_call(
        functools.partial(mlp_backward_kernel, earlier is not None, biases is not None),
        grid=(blocks + 1,),
        out_shape=outs,
        in_specs=[SMEM] + specs,
        out_specs=out_specs + summed,
        scratch_shapes=[
            pltpu.VMEM((rows, width), jnp.bfloat16),
            pltpu.VMEM((width, rows), jnp.bfloat16),
            pltpu.VMEM((rows, width), jnp.float32),
            pltpu.VMEM((rows, block), jnp.bfloat16),
            pltpu.VMEM((rows, block), jnp.bfloat16),
            pltpu.VMEM((rows, width), jnp.float32),
            pltpu.VMEM((rows, width), jnp.bfloat16),
            pltpu.SemaphoreType.DMA((2 + rows // 256,)),
            *scratch,
        ],
        compiler_params=params(54 << 20),
        cost_estimate=cost(8 * rows * width * blocks * block, rows * blocks * block, *inputs, *outs),
        name="mlp_backward",
    )(core, *in_hbm(inputs))


def input_gradient(
    dhid_ref, state_ref, gmix_ref, weight_ref, gain_ref, earlier, grad_ref, dgain_ref, dshift_ref
):
    step = pl.program_id(0)
    grad_norm = dot_transposed(gmix_ref[:, :FEATURES], weight_ref[0])
    for part in range(1, 3):
        grad_norm = grad_norm + dot_transposed(
            gmix_ref[:, part * FEATURES : (part + 1) * FEATURES], weight_ref[part]
        )
    normed, scale = norm_parts(state_ref[...].astype(jnp.float32))
    dgain = jnp.sum(grad_norm * normed, axis=0, keepdims=True)
    dshift = jnp.sum(grad_norm, axis=0, keepdims=True)

    @pl.when(step == 0)
    def _():
        dgain_ref[...] = dgain if earlier is None else dgain + earlier[0][...]
        dshift_ref[...] = dshift if earlier is None else dshift + earlier[1][...]

    @pl.when(step > 0)
    def _():
        dgain_ref[...] += dgain
        dshift_ref[...] += dshift

    grad = dhid_ref[...] + norm_back(normed, scale, gain_ref[...], grad_norm)
    grad_ref[...] = grad.astype(grad_ref.dtype)


def attention_backward_kernel(
    docs,
    back,
    micro,
    lengths_ref,
    dhid_ref,
    att_ref,
    mixed_ref,
    lse_ref,
    out_ref,
    *rest,
):
    if micro is None:
        micro = pl.program_id(0)
        state_ref, gain_ref, gmix_ref, grad_ref, dgain_ref, dshift_ref, *rest = rest
        finish = functools.partial(
            input_gradient, dhid_ref, state_ref, gmix_ref, out_ref, gain_ref, None,
            grad_ref, dgain_ref, dshift_ref,
        )
    else:
        gmix_ref, *rest = rest
        finish = None
    datt_ref, bias_ref, delta_ref, dq_ref = rest
    count = dhid_ref.shape[0]
    low_grad = dhid_ref[...].astype(jnp.bfloat16)
    datt = dot_transposed(low_grad, out_ref[out_ref.shape[0] - 1]).astype(jnp.bfloat16)
    datt_ref[...] = datt
    product = datt.astype(jnp.float32) * att_ref[...].astype(jnp.float32)
    high = product.astype(jnp.bfloat16)
    rest_low = (product - high.astype(jnp.float32)).astype(jnp.bfloat16)
    feature = lax.broadcasted_iota(jnp.int32, (16, FEATURES), 1)
    head = lax.broadcasted_iota(jnp.int32, (16, FEATURES), 0)
    chosen = ((feature >= head * HD) & (feature < (head + 1) * HD)).astype(jnp.bfloat16)
    delta = dot_transposed(chosen, high) + dot_transposed(chosen, rest_low)
    for index in range(H):
        delta_ref[index] = delta[index : index + 1]
    bias_ref[...] = allowed_bias(count, [lengths_ref[micro, d] for d in range(docs)], docs, 1)

    def one_group(group, carry):
        lanes = pl.multiple_of(group * LANES, LANES)
        dq_ref[...] = jnp.zeros_like(dq_ref)
        for block in range(count // BLOCK):
            keys = slice(block * BLOCK, (block + 1) * BLOCK)
            rows = slice(block * BLOCK, min(count, (block + 1 + back) * BLOCK))
            key = head_split(mixed_ref[keys, pl.ds(FEATURES + lanes, LANES)])
            value = head_split(mixed_ref[keys, pl.ds(2 * FEATURES + lanes, LANES)])
            query = mixed_ref[rows, pl.ds(lanes, LANES)]
            datt_group = datt_ref[rows, pl.ds(lanes, LANES)]
            scores = dot_transposed(key, query)
            dprobs = dot_transposed(value, datt_group)
            bias = bias_ref[keys, rows]
            probs_low, dscores_low = ([], [])
            for h in range(GROUP):
                part = slice(h * BLOCK, (h + 1) * BLOCK)
                lse = lse_ref[GROUP * group + h, :, rows]
                delta = delta_ref[GROUP * group + h, :, rows]
                probs = jnp.exp((scores[part] * 0.125 + bias) - lse)
                dscores = probs * (dprobs[part] - delta)
                probs_low.append(probs.astype(jnp.bfloat16))
                dscores_low.append(dscores.astype(jnp.bfloat16))
            probs_low = jnp.concatenate(probs_low, axis=0)
            dscores_low = jnp.concatenate(dscores_low, axis=0)
            dvalue = head_join(dot(probs_low, datt_group))
            dkey = head_join(dot(dscores_low, query)) * 0.125
            dq_ref[rows, :] += transposed_dot(dscores_low, key)
            gmix_ref[keys, pl.ds(FEATURES + lanes, LANES)] = dkey.astype(jnp.bfloat16)
            gmix_ref[keys, pl.ds(2 * FEATURES + lanes, LANES)] = dvalue.astype(jnp.bfloat16)
        gmix_ref[:, pl.ds(lanes, LANES)] = (dq_ref[...] * 0.125).astype(jnp.bfloat16)
        return carry

    lax.fori_loop(0, H // GROUP, one_group, 0, unroll=H // GROUP)
    if finish is not None:
        finish()


def attention_backward(micro, lengths, dhid, count, back, att, mixed, lse, weight):
    width = dhid.shape[1]
    docs = lengths.shape[1]
    outs = jax.ShapeDtypeStruct((count, 3 * width), jnp.bfloat16)
    inputs = [dhid, att, mixed, lse, weight]
    return pl.pallas_call(
        functools.partial(attention_backward_kernel, docs, back, micro),
        grid=(1,),
        out_shape=outs,
        in_specs=[
            SMEM,
            pl.BlockSpec((count, width), lambda i: (micro, 0)),
            pl.BlockSpec((count, width), lambda i: (micro, 0)),
            pl.BlockSpec((count, 3 * width), lambda i: (micro, 0)),
            pl.BlockSpec((H, 1, count), lambda i: (micro, 0, 0)),
            pl.BlockSpec((1, width, width), lambda i: (3, 0, 0)),
        ],
        out_specs=pl.BlockSpec((count, 3 * width), lambda i: (0, 0)),
        scratch_shapes=[
            pltpu.VMEM((count, width), jnp.bfloat16),
            pltpu.VMEM((count, count), jnp.float32),
            pltpu.VMEM((H, 1, count), jnp.float32),
            pltpu.VMEM((count, LANES), jnp.float32),
        ],
        compiler_params=params(),
        cost_estimate=cost(
            2 * count * width * width + 10 * count * count * width, count * count * H, outs, outs
        ),
        name="attention_backward",
    )(lengths, *in_hbm(inputs))


def attention_backward_all(lengths, dhid, count, back, att, mixed, lse, weight, state, gain):
    rows, width = dhid.shape
    micro, docs = lengths.shape
    vector = pl.BlockSpec((1, width), lambda i: (0, 0))
    outs = (
        pltpu.HBM((rows, 3 * width), jnp.bfloat16),
        pltpu.HBM((rows, width), jnp.float32),
        jax.ShapeDtypeStruct((1, width), jnp.float32),
        jax.ShapeDtypeStruct((1, width), jnp.float32),
    )
    inputs = [dhid, att, mixed, lse, weight, state, gain]
    return pl.pallas_call(
        functools.partial(attention_backward_kernel, docs, back, None),
        grid=(micro,),
        out_shape=outs,
        in_specs=[
            SMEM,
            rows_of(count, width),
            rows_of(count, width),
            rows_of(count, 3 * width),
            pl.BlockSpec((H, 1, count), lambda i: (i, 0, 0)),
            whole(weight),
            rows_of(count, width),
            whole(gain),
        ],
        out_specs=[rows_of(count, 3 * width), rows_of(count, width), vector, vector],
        scratch_shapes=[
            pltpu.VMEM((count, width), jnp.bfloat16),
            pltpu.VMEM((count, count), jnp.float32),
            pltpu.VMEM((H, 1, count), jnp.float32),
            pltpu.VMEM((count, LANES), jnp.float32),
        ],
        compiler_params=params(44 << 20),
        cost_estimate=cost(
            8 * rows * width * width + 10 * rows * count * width, rows * count * H, *inputs, *outs
        ),
        name="attention_backward_all",
    )(lengths, *in_hbm(inputs))


def attention_terms_kernel(more, micro, core_ref, normed_ref, *rest):
    gmix_refs, rest = (rest[:micro], rest[micro:])
    earlier = rest[:3] if more else (None,) * 3
    if more:
        rest = rest[3:]
    mine_ref, theirs_ref, dbias_ref = rest
    core = core_ref[0]
    terms, dbias, start = (0.0, 0.0, 0)
    for gmix_ref in gmix_refs:
        right = gmix_ref[...]
        stop = start + right.shape[0]
        terms = terms + transposed_dot(normed_ref[start:stop], right)
        dbias = dbias + jnp.sum(right.astype(jnp.float32), axis=0, keepdims=True)
        start = stop
    dbias_ref[0] = dbias + earlier[2][0] if more else dbias
    store_halves(core, terms, mine_ref, theirs_ref, earlier[:2] if more else None)


def attention_terms(core, normed, gmix, earlier=None):
    rows, width = normed.shape
    groups = DEVICE_GROUPS
    each = width // groups
    shape = pltpu.HBM
    half = shape((groups, 3, each, width // 2), jnp.bfloat16)
    outs = (half, half, shape((3, 1, width), jnp.float32))
    halves = pl.BlockSpec((groups, None, each, width // 2), lambda i: (0, i, 0, 0))
    summed = [halves, halves, pl.BlockSpec((1, 1, width), lambda i: (i, 0, 0))]
    inputs = [normed, *gmix]
    specs = [whole(normed)] + [
        pl.BlockSpec((part.shape[0], width), lambda i: (0, i)) for part in gmix
    ]
    if earlier is not None:
        inputs += list(earlier)
        specs += summed
    return pl.pallas_call(
        functools.partial(attention_terms_kernel, earlier is not None, len(gmix)),
        grid=(3,),
        out_shape=outs,
        in_specs=[SMEM] + specs,
        out_specs=summed,
        compiler_params=params(),
        cost_estimate=cost(6 * rows * width * width, 0, *inputs, *outs),
        name="attention_terms",
    )(core, *in_hbm(inputs[:1]), *gmix, *in_hbm(inputs[1 + len(gmix) :]))


def attention_input_kernel(more, micro, dhid_ref, state_ref, weight_ref, gain_ref, *rest):
    gmix_refs, rest = (rest[:micro], rest[micro:])
    earlier = rest[:2] if more else None
    if more:
        rest = rest[2:]
    grad_ref, dgain_ref, dshift_ref, gmix_ref = rest
    each = pl.num_programs(0) // micro
    for index, part_ref in enumerate(gmix_refs):

        @pl.when(pl.program_id(0) // each == index)
        def _(part_ref=part_ref):
            gmix_ref[...] = part_ref[...]

    input_gradient(
        dhid_ref, state_ref, gmix_ref, weight_ref, gain_ref, earlier, grad_ref, dgain_ref, dshift_ref
    )


def attention_input(dhid, state, gmix, weight, gain, kind, earlier=None, chunk=256):
    rows, width = dhid.shape
    shape = jax.ShapeDtypeStruct
    vector = pl.BlockSpec((1, width), lambda i: (0, 0))
    outs = (shape((rows, width), kind), shape((1, width), jnp.float32), shape((1, width), jnp.float32))
    inputs = [dhid, state, weight, gain, *gmix]
    each = rows // chunk // len(gmix)
    specs = [
        rows_of(chunk, width),
        rows_of(chunk, width),
        pl.BlockSpec((3, width, width), lambda i: (0, 0, 0), pipeline_mode=pl.Buffered(1)),
        whole(gain),
    ]
    for index in range(len(gmix)):
        specs.append(
            pl.BlockSpec(
                (chunk, 3 * width),
                lambda i, index=index: (jnp.clip(i - index * each, 0, each - 1), 0),
            )
        )
    if earlier is not None:
        inputs += list(earlier)
        specs += [vector, vector]
    return pl.pallas_call(
        functools.partial(attention_input_kernel, earlier is not None, len(gmix)),
        grid=(rows // chunk,),
        out_shape=outs,
        in_specs=specs,
        out_specs=[rows_of(chunk, width), vector, vector],
        scratch_shapes=[pltpu.VMEM((chunk, 3 * width), jnp.bfloat16)],
        compiler_params=params(),
        cost_estimate=cost(6 * rows * width * width, 0, *inputs, *outs),
        name="attention_input",
    )(*in_hbm(inputs[:4]), *gmix, *in_hbm(inputs[4 + len(gmix) :]))


def place_small_kernel(sizes, me_ref, *refs):
    smalls, outs = (refs[:4], refs[4:])
    dp = me_ref[0] // 2
    slot = lax.broadcasted_iota(jnp.int32, (16, 1), 0)
    owner = ((slot % 4) * 4 + (slot // 8) * 2 + slot // 4 % 2) ^ dp
    for index, (size, out_ref) in enumerate(zip(sizes, outs)):
        width = 16 * size
        lane = lax.broadcasted_iota(jnp.int32, (256, width), 0)
        column = lax.broadcasted_iota(jnp.int32, (256, width), 1)
        spread = (column % size == lane).astype(jnp.bfloat16)
        rows = jnp.concatenate([ref[z, index : index + 1] for ref in smalls for z in range(4)], axis=0)
        spread_rows = dot(rows, spread)
        column = lax.broadcasted_iota(jnp.int32, (1, width), 1)
        out_ref[...] = jnp.sum(
            jnp.where(column // size == owner, spread_rows, 0.0), axis=0, keepdims=True
        )


def place_small(me, smalls, sizes):
    return pl.pallas_call(
        functools.partial(place_small_kernel, sizes),
        out_shape=[jax.ShapeDtypeStruct((1, 16 * size), jnp.float32) for size in sizes],
        in_specs=[SMEM] + [pl.BlockSpec(memory_space=pltpu.VMEM)] * len(smalls),
        out_specs=[pl.BlockSpec(memory_space=pltpu.VMEM)] * len(sizes),
        name="place_small",
    )(me, *smalls)


def swap(value, bits):
    return lax.ppermute(value, BOTH, [(i, i ^ bits) for i in range(32)])


CORE, X, Y, Z1, Z2, Z3 = (1, 2, 4, 8, 16, 24)


def place_kernel(slots, me_ref, *refs):
    sources, (out, sems) = (refs[: len(slots)], refs[len(slots) :])
    me = me_ref[0]
    copies = []
    for source, rels in zip(sources, slots):
        for inner, rel in enumerate(rels):
            copies.append(
                pltpu.make_async_copy(
                    source.at[inner], out.at[:, rel ^ me], sems.at[len(copies)]
                )
            )
    for copy in copies:
        copy.start()
    for copy in copies:
        copy.wait()


def place(me, sources, slots):
    placed = pl.pallas_call(
        functools.partial(place_kernel, slots),
        out_shape=jax.ShapeDtypeStruct((4, 32, 24, FEATURES), jnp.bfloat16),
        in_specs=[SMEM] + [pl.BlockSpec(memory_space=pl.ANY)] * len(sources),
        out_specs=pl.BlockSpec(memory_space=pltpu.VMEM),
        scratch_shapes=[pltpu.SemaphoreType.DMA((32,))],
        name="place",
    )(me, *sources)
    return placed.reshape(4, FEATURES, FEATURES)


def after(values, *others):
    return lax.optimization_barrier((values, others))[0]


def gather_first(piece, small, me):
    base = (0, Z1, Z2, Z3)
    pieces = lax.optimization_barrier(
        [piece] + [swap(piece, bits) for bits in base[1:]]
        + [small] + [swap(small, bits) for bits in base[1:]]
    )
    four, small = (jnp.concatenate(pieces[:4]), jnp.concatenate(pieces[4:]))
    four_x, four_y, four_core, small_x, small_y = lax.optimization_barrier(
        (swap(four, X), swap(four, Y), swap(four, CORE), swap(small, X), swap(small, Y))
    )
    near_xy, far_xy, x_core, y_core, small_xy = lax.optimization_barrier(
        (
            swap(four_y[:2], X), swap(four_x[2:], Y), swap(four_x, CORE), swap(four_y, CORE),
            swap(small_y, X),
        )
    )
    parts = [four, four_x, four_y, near_xy, far_xy]
    parts += [four_core, x_core, y_core, swap(near_xy, CORE), swap(far_xy, CORE)]
    slots = [base] + [tuple(rel ^ bits for rel in base) for bits in (X, Y)]
    slots += [(X ^ Y, X ^ Y ^ Z1), (X ^ Y ^ Z2, X ^ Y ^ Z3)]
    slots += [tuple(rel ^ CORE for rel in rels) for rels in slots]
    return (place(me, parts, slots), (small, small_x, small_y, small_xy))


def pick(array, axis, index):
    return lax.dynamic_index_in_dim(array, index, axis, keepdims=False)


def low(value):
    return value.astype(jnp.bfloat16)


def wide(value):
    return value.astype(jnp.float32)


def add(*terms):
    total = wide(terms[0])
    for term in terms[1:]:
        total = total + wide(term)
    return total


def device_at(z_pair, z_low, y, x):
    return z_pair * 8 + z_low * 4 + y * 2 + x


def total(*terms):
    result = terms[0].astype(jnp.float32)
    for term in terms[1:]:
        result = result + term.astype(jnp.float32)
    return result


def first_sums_kernel(views, spot_ref, *refs):
    mine, got, alone = (refs[:views], refs[views : 2 * views], refs[2 * views : -4])
    near_sent, far_sent, near_kept, far_kept = refs[-4:]
    z_pair, y, x = (spot_ref[0], spot_ref[2], spot_ref[3])
    for low_z in range(2):
        for other in range(2):
            for out, device in (
                (near_sent, device_at(z_pair, low_z, other, 1 - x)),
                (far_sent, device_at(1 - z_pair, low_z, 1 - y, other)),
                (near_kept, device_at(z_pair, low_z, other, x)),
                (far_kept, device_at(1 - z_pair, low_z, y, other)),
            ):
                start = 0
                for left, right in zip(mine, got):
                    count = left.shape[1]
                    out[low_z, other, start : start + count] = total(
                        left[device], right[device]
                    ).astype(jnp.bfloat16)
                    start += count
                for only in alone:
                    out[low_z, other, start:] = only[device]


def second_sums_kernel(spot_ref, near, far, near_in, far_in, *outs):
    near_sent, far_sent, near_kept, far_kept = outs
    y, x = (spot_ref[2], spot_ref[3])
    for low_z in range(2):
        for out, kept, got, index in (
            (near_sent, near, near_in, 1 - y),
            (far_sent, far, far_in, 1 - x),
            (near_kept, near, near_in, y),
            (far_kept, far, far_in, x),
        ):
            out[low_z] = total(kept[low_z, index], got[low_z, index]).astype(jnp.bfloat16)


def third_sums_kernel(spot_ref, near, far, near_in, far_in, first, second, third, kept):
    low_z = spot_ref[1]
    first[...] = total(near[1 - low_z], near_in[1 - low_z]).astype(jnp.bfloat16)
    second[...] = total(far[low_z], far_in[low_z]).astype(jnp.bfloat16)
    third[...] = total(far[1 - low_z], far_in[1 - low_z]).astype(jnp.bfloat16)
    kept[...] = total(near[low_z], near_in[low_z])


def assemble_kernel(layouts, core_ref, half_ref, other_ref, *outs):
    if len(outs) > len(layouts):
        outs[-1][...] = half_ref[-16:] + other_ref[-16:]
    core = core_ref[0]
    half, other = (half_ref[...], other_ref[...])
    left = jnp.where(core == 0, half, other)
    right = jnp.where(core == 0, other, half)
    start, wide_half = (0, half.shape[1])
    for (blocks, rows), out in zip(layouts, outs):
        for block in range(blocks):
            part = slice(start, start + rows)
            column = 2 * block * wide_half
            out[:, column : column + wide_half] = left[part]
            out[:, column + wide_half : column + 2 * wide_half] = right[part]
            start += rows


SMALL_ROWS = ((48, 48, 144, 48, 48, 48), (192, 48))


def pack_small_kernel(unused_ref, *refs):
    *vectors, out = refs
    width = out.shape[2]
    device = lax.broadcasted_iota(jnp.int32, (16, 1), 0)
    rows, vectors = ([], iter(vectors))
    for sizes in SMALL_ROWS:
        row, start = (jnp.zeros((16, width), jnp.float32), 0)
        for size, ref in zip(sizes, vectors):
            if len(ref.shape) == 2:
                vector = ref[...]
            else:
                vector = jnp.concatenate([ref[i] for i in range(ref.shape[0])], axis=1)
            column = lax.broadcasted_iota(jnp.int32, (1, 16 * size), 1)
            parts = jnp.where(column // size == device, vector, 0.0).astype(jnp.bfloat16)
            place_in = lax.broadcasted_iota(jnp.int32, (16 * size, width), 0) % size + start
            lane = lax.broadcasted_iota(jnp.int32, (16 * size, width), 1)
            row = row + dot(parts, (place_in == lane).astype(jnp.bfloat16))
            start += size
        rows.append(row)
    line = lax.broadcasted_iota(jnp.int32, out.shape[1:], 0)
    for d in range(16):
        first, second = (rows[0][d : d + 1], rows[1][d : d + 1])
        value = jnp.where(line == 0, first, jnp.where(line == 1, second, 0.0))
        out[d] = value.astype(jnp.bfloat16)


def in_vmem(kernel, name, outs, *args):
    vmem = pl.BlockSpec(memory_space=pltpu.VMEM)
    return pl.pallas_call(
        kernel,
        out_shape=outs,
        in_specs=[SMEM] + [vmem] * (len(args) - 1),
        out_specs=[vmem] * len(outs),
        compiler_params=params(),
        cost_estimate=cost(0, 0, *args, *outs),
        name=name,
    )(*args)


class Reduction:
    def __init__(self, spot, mine, theirs):
        self.spot = spot
        self.mine = list(mine)
        self.got = [swap(part, CORE) for part in theirs]
        self.alone = []
        self.width = self.mine[0].shape[2]

    def like(self, *lead, kind=jnp.bfloat16):
        count = sum(part.shape[1] for part in (*self.mine, *self.alone))
        return jax.ShapeDtypeStruct((*lead, count, self.width), kind)

    def first(self):
        near_sent, far_sent, *self.kept = in_vmem(
            functools.partial(first_sums_kernel, len(self.mine)),
            "first_sums",
            [self.like(2, 2)] * 4,
            self.spot,
            *self.mine,
            *self.got,
            *self.alone,
        )
        self.got = [swap(near_sent, X), swap(far_sent, Y)]
        return self.kept

    def second(self):
        near_sent, far_sent, *self.kept = in_vmem(
            second_sums_kernel, "second_sums", [self.like(2)] * 4, self.spot, *self.kept, *self.got
        )
        self.got = [swap(near_sent, Y), swap(far_sent, X)]
        return self.kept

    def third(self):
        *sent, kept = in_vmem(
            third_sums_kernel,
            "third_sums",
            [self.like()] * 3 + [self.like(kind=jnp.float32)],
            self.spot,
            *self.kept,
            *self.got,
        )
        self.kept = [kept]
        self.got = [swap(part, bits) for part, bits in zip(sent, (Z1, Z2, Z3))]
        return self.kept

    def fourth(self):
        half = total(*self.kept, *self.got)
        self.kept, self.got = ([half], [swap(half, CORE)])

    def whole(self, core, layouts):
        outs = [
            jax.ShapeDtypeStruct((rows, 2 * self.width * blocks), jnp.float32)
            for blocks, rows in layouts
        ]
        if self.alone:
            outs.append(jax.ShapeDtypeStruct((16, self.width), jnp.float32))
        return in_vmem(
            functools.partial(assemble_kernel, layouts), "assemble", outs, core, *self.kept, *self.got
        )


def gather_all(weights, spot, me):
    gain_a, shift_a, qkv, qbias, out, obias, gain_m, shift_m, fc, fbias, proj, pbias = weights
    core = spot[4]

    def half(weight):
        part = lax.dynamic_slice_in_dim(weight, core * 24, 24, 0)
        return jnp.transpose(part.reshape(24, -1, FEATURES), (1, 0, 2))

    columns = lax.dynamic_slice_in_dim(fc, core * 2 * FEATURES, 2 * FEATURES, 1)
    columns = jnp.transpose(columns.reshape(48, 2, FEATURES), (1, 0, 2))
    across = lax.dynamic_slice_in_dim(proj, core * 96, 96, 0).reshape(2, 48, FEATURES)
    mlp = lax.all_gather(jnp.concatenate([columns, across]), BOTH)
    mlp = mlp.reshape(16, 2, 4, 48, FEATURES)
    vectors = [gain_a, shift_a, qbias, obias, gain_m, shift_m, fbias, pbias]
    sizes = tuple(vector.shape[0] for vector in vectors)
    small = jnp.stack([jnp.pad(v, (0, 256 - size)) for v, size in zip(vectors, sizes)])
    first, smalls = gather_first(jnp.concatenate([half(qkv), half(out)])[None], small[None], me)
    return (first, mlp, *place_small(me, smalls, sizes))


def gather_plain(weights):
    whole_ones = [lax.all_gather(weight, "dp", axis=0, tiled=True) for weight in weights]
    gain_a, shift_a, qkv, qbias, out, obias, gain_m, shift_m, fc, fbias, proj, pbias = whole_ones

    def blocks(weight):
        return jnp.transpose(weight.reshape(FEATURES, -1, FEATURES), (1, 0, 2))

    rows = [
        wide(v).reshape(1, -1)
        for v in (gain_a, shift_a, qbias, obias, gain_m, shift_m, fbias, pbias)
    ]
    first = jnp.concatenate([blocks(qkv), blocks(out)])
    fc = blocks(fc).reshape(2, 2, 16, 48, FEATURES)
    fc = jnp.transpose(fc, (2, 0, 1, 3, 4))
    mlp = jnp.concatenate([fc, proj.reshape(16, 2, 2, 48, FEATURES)], axis=2)
    return (first, mlp, *rows)


def reduce_plain(matrices, small):
    def joined(left, right):
        both = jnp.concatenate([left, right], axis=-1)
        if both.ndim == 4:
            both = jnp.transpose(both, (0, 2, 1, 3)).reshape(FEATURES, -1)
        return both.reshape(-1, both.shape[-1])

    qkv, out, fc, proj = [joined(*pair) for pair in matrices]
    gain_a, shift_a, qbias, obias, gain_m, shift_m, fbias, pbias = [v.reshape(-1) for v in small]
    values = (
        gain_a, shift_a, qkv, qbias, out, obias, gain_m, shift_m, fc, fbias, proj, pbias
    )
    return tuple(
        wide(lax.psum(low(lax.psum_scatter(wide(v), "dp", scatter_dimension=0, tiled=True)), "rep"))
        for v in values
    )


def forward(tokens, lengths, count, back, weights):
    weight, mlp, gain_a, shift_a, qbias, obias, gain_m, shift_m, fbias, pbias = weights
    state, kept = (tokens, [])
    for use in range(USES):
        normed_a, mixed, att, lse, hidden, normed_m = attention_forward(
            lengths, state, count, back, gain_a, shift_a, weight, qbias, obias, gain_m, shift_m
        )
        expanded, after_mlp = (None, None)
        if use < USES - 1:
            expanded, after_mlp = mlp_forward(hidden, normed_m, mlp, fbias, pbias)
        kept.append((state, normed_a, mixed, att, lse, hidden, normed_m, expanded))
        state = after_mlp
    return kept


def shards(custom, tokens, doc_lengths, cotangent, *weights):
    micro, count, width = tokens.shape
    dp, core = (lax.axis_index("dp"), lax.axis_index("rep"))
    spot = (dp // 8, dp // 4 % 2, dp // 2 % 2, dp % 2, core)
    me = (dp * 2 + core).astype(jnp.int32).reshape(1)
    places = jnp.stack(spot).astype(jnp.int32)
    side = core.astype(jnp.int32).reshape(1) if custom else jnp.zeros((1,), jnp.int32)
    back = -(-(LONGEST - 1) // BLOCK)
    lengths = doc_lengths.reshape(micro, doc_lengths.shape[-1])
    whole_ones = gather_all(weights, spot, me) if custom else gather_plain(weights)
    kept = forward(tokens.reshape(micro * count, width), lengths, count, back, whole_ones)
    weight, mlp, gain_a, gain_m = (whole_ones[0], whole_ones[1], whole_ones[2], whole_ones[6])
    grad, mlp_terms, terms, norm = (cotangent.reshape(micro * count, width), None, None, None)
    delayed = None
    for use in range(USES - 1, -1, -1):
        before, normed_a, mixed, att, lse, hidden, normed_m, expanded = kept[use]
        last = use == USES - 1
        dhid, *mlp_terms = mlp_backward(
            side, grad, hidden, normed_m, att, expanded, mlp, gain_m, mlp_terms,
            whole_ones[-2:] if last else None,
        )
        if last:
            state, (dhid, *mlp_terms) = (dhid, mlp_terms)
        sending = custom and use == 0
        if delayed is not None:
            terms = delayed()
        if sending:
            fc_mine, fc_theirs, proj_mine, proj_theirs, out_mine, out_theirs = [
                part.reshape(16, -1, part.shape[-1]) for part in mlp_terms[:6]
            ]
            sums = Reduction(
                places, (fc_mine, proj_mine, out_mine), (fc_theirs, proj_theirs, out_theirs)
            )
            sums.got, terms = lax.optimization_barrier((sums.got, terms))
            dhid = after(dhid, sums.first())
        if use:
            gmix, grad, *norm = attention_backward_all(
                lengths, dhid, count, back, att, mixed, lse, weight, before, gain_a
            )
            delayed = functools.partial(attention_terms, side, normed_a, in_hbm([gmix]))
            continue
        gmix = [
            attention_backward(index, lengths, dhid, count, back, att, mixed, lse, weight)
            for index in range(micro)
        ]
        terms = attention_terms(side, normed_a, gmix, terms)
        if sending:
            qkv_sums = Reduction(
                places, *[(part.reshape(16, -1, part.shape[-1]),) for part in terms[:2]]
            )
            sums.got, terms = lax.optimization_barrier((sums.got, terms))
            gmix = after(gmix, sums.second())
        grad, *norm = attention_input(dhid, before, gmix, weight, gain_a, jnp.bfloat16, norm)
        if sending:
            sums.got, qkv_sums.got = after((sums.got, qkv_sums.got), norm)
    small = (norm[0], norm[1], terms[2], mlp_terms[6], mlp_terms[9], mlp_terms[10])
    small += (mlp_terms[7], mlp_terms[8])
    if custom:
        packed = jax.ShapeDtypeStruct((16, 16, width // 2), jnp.bfloat16)
        qkv_sums.alone = in_vmem(pack_small_kernel, "pack_small", [packed], side, *small)
        sums.got = after(sums.got, qkv_sums.alone)
        qkv_sums.got = after(qkv_sums.got, sums.third())
        qkv_sums.first()
        qkv_sums.second()
        sums.got = after(sums.got, qkv_sums.third())
        sums.fourth()
        qkv_sums.fourth()
        fc, proj, out = sums.whole(side, ((4, 48), (1, 192), (1, 48)))
        qkv, small = qkv_sums.whole(side, ((3, 48),))
        parts = []
        for row, sizes in enumerate(SMALL_ROWS):
            start = 0
            for size in sizes:
                parts.append(small[row, start : start + size])
                start += size
        gain_a, shift_a, qbias, obias, gain_m, shift_m, fbias, pbias = parts
        final = (
            gain_a, shift_a, qkv, qbias, out, obias, gain_m, shift_m, fc, fbias, proj, pbias
        )
    else:
        matrices = (terms[:2], mlp_terms[4:6], mlp_terms[:2], mlp_terms[2:4])
        final = reduce_plain(matrices, small)
    return (state.reshape(tokens.shape), grad.reshape(tokens.shape), *final)


def solution(mesh):
    custom = mesh.shape["dp"] == 16 and mesh.shape["rep"] == 2
    placed = tuple(
        P("dp", None) if index in (2, 4, 8, 10) else P("dp") for index in range(12)
    )
    rows = P(None, BOTH, None)
    return jax.shard_map(
        functools.partial(shards, custom),
        mesh=mesh,
        in_specs=(rows, rows, rows, *placed),
        out_specs=(rows, rows, *placed),
        check_vma=False,
    )
```

```python
import functools
import math

import jax
import jax.numpy as jnp
from jax import lax
from jax.experimental import pallas as pl
from jax.experimental.pallas import tpu as pltpu
from jax.sharding import PartitionSpec as P

H = 12
HD = 64
USES = 2
LONGEST = 256
BOTH = ("dp", "rep")


NORM_EPS = 1e-05
BLOCK = 128
FEATURES = H * HD
VMEM_LIMIT = 40 << 20
COST_SCALE = 8


def dot(left, right):
    return jnp.dot(left, right, preferred_element_type=jnp.float32)


def transposed_dot(left, right):
    return lax.dot_general(
        left, right, (((0,), (0,)), ((), ())), preferred_element_type=jnp.float32
    )


def dot_transposed(left, right):
    return lax.dot_general(
        left, right, (((1,), (1,)), ((), ())), preferred_element_type=jnp.float32
    )


def norm_parts(values):
    center = values - jnp.mean(values, axis=-1, keepdims=True)
    spread = jnp.mean(center * center, axis=-1, keepdims=True)
    scale = lax.rsqrt(spread + NORM_EPS)
    return (center * scale, scale)


def norm_back(normed, scale, gain, grad):
    inner = grad * gain
    first = jnp.mean(inner, axis=-1, keepdims=True)
    second = jnp.mean(inner * normed, axis=-1, keepdims=True)
    return (inner - first - normed * second) * scale


def segment_of(places, lengths, docs):
    end = jnp.int32(0)
    segment = jnp.zeros(places.shape, jnp.int32)
    for doc in range(docs):
        end = end + lengths[doc]
        segment = segment + (places >= end).astype(jnp.int32)
    return segment


def allowed_bias(count, lengths, docs, query_axis):
    query_shape = (count, 1) if query_axis == 0 else (1, count)
    key_shape = (1, count) if query_axis == 0 else (count, 1)
    query = lax.broadcasted_iota(jnp.int32, query_shape, query_axis)
    key = lax.broadcasted_iota(jnp.int32, key_shape, 1 - query_axis)
    same = segment_of(query, lengths, docs) == segment_of(key, lengths, docs)
    return jnp.where(same & (key <= query), 0.0, -1e30).astype(jnp.float32)


GROUP = 4
LANES = GROUP * HD


def head_split(array):
    head = lax.broadcasted_iota(jnp.int32, array.shape, 1) // HD
    zero = jnp.zeros_like(array)
    return jnp.concatenate([jnp.where(head == h, array, zero) for h in range(GROUP)], axis=0)


def head_join(stacked):
    count = stacked.shape[0] // GROUP
    head = lax.broadcasted_iota(jnp.int32, (count, LANES), 1) // HD
    joined = stacked[:count]
    for h in range(1, GROUP):
        joined = jnp.where(head == h, stacked[h * count : (h + 1) * count], joined)
    return joined


def attention_forward_kernel(
    docs,
    back,
    lengths_ref,
    state_ref,
    gain_ref,
    shift_ref,
    weight_ref,
    qbias_ref,
    obias_ref,
    gain2_ref,
    shift2_ref,
    normed_ref,
    mixed_ref,
    att_ref,
    lse_ref,
    hidden_ref,
    normed2_ref,
    bias_ref,
    lse_cols,
):
    micro = pl.program_id(0)
    state = state_ref[...].astype(jnp.float32)
    count = state.shape[0]
    normed = (norm_parts(state)[0] * gain_ref[...] + shift_ref[...]).astype(jnp.bfloat16)
    normed_ref[...] = normed
    for part in range(3):
        columns = slice(part * FEATURES, (part + 1) * FEATURES)
        mixed_ref[:, columns] = (dot(normed, weight_ref[part]) + qbias_ref[:, columns]).astype(
            jnp.bfloat16
        )
    bias_ref[...] = allowed_bias(count, [lengths_ref[micro, d] for d in range(docs)], docs, 0)
    lse_cols[...] = jnp.zeros_like(lse_cols)

    def one_group(group, carry):
        lanes = pl.multiple_of(group * LANES, LANES)
        for block in range(count // BLOCK):
            rows = slice(block * BLOCK, (block + 1) * BLOCK)
            low_key = max(0, block - back) * BLOCK
            keys = slice(low_key, (block + 1) * BLOCK)
            query = head_split(mixed_ref[rows, pl.ds(lanes, LANES)])
            key = mixed_ref[keys, pl.ds(FEATURES + lanes, LANES)]
            value = mixed_ref[keys, pl.ds(2 * FEATURES + lanes, LANES)]
            scores = dot_transposed(query, key)
            bias = bias_ref[rows, keys]
            scores = scores * 0.125 + jnp.concatenate([bias] * GROUP, axis=0)
            top = jnp.max(scores, axis=-1, keepdims=True)
            expo = jnp.exp(scores - top)
            total_expo = jnp.sum(expo, axis=-1, keepdims=True)
            result = dot(expo.astype(jnp.bfloat16), value) / total_expo
            att_ref[rows, pl.ds(lanes, LANES)] = head_join(result).astype(jnp.bfloat16)
            lse = top + jnp.log(total_expo)
            lane = lax.broadcasted_iota(jnp.int32, (BLOCK, 128), 1)
            for h in range(GROUP):
                lse_cols[rows, :] += jnp.where(
                    lane == GROUP * group + h, lse[h * BLOCK : (h + 1) * BLOCK], 0.0
                )
        return carry

    lax.fori_loop(0, H // GROUP, one_group, 0, unroll=H // GROUP)
    lse = jnp.transpose(lse_cols[...])
    for index in range(H):
        lse_ref[index] = lse[index : index + 1]
    hidden = state + (dot(att_ref[...], weight_ref[3]) + obias_ref[...])
    hidden_ref[...] = hidden
    normed2_ref[...] = (norm_parts(hidden)[0] * gain2_ref[...] + shift2_ref[...]).astype(
        jnp.bfloat16
    )


def whole(array):
    dims = len(array.shape)
    return pl.BlockSpec(array.shape, lambda *unused: (0,) * dims, pipeline_mode=pl.Buffered(1))


SMEM = pl.BlockSpec(memory_space=pltpu.SMEM)


def in_hbm(arrays):
    return [pltpu.with_memory_space_constraint(array, pltpu.HBM) for array in arrays]


def rows_of(count, width):
    return pl.BlockSpec((count, width), lambda i: (i, 0))


def params(limit=VMEM_LIMIT):
    return pltpu.CompilerParams(vmem_limit_bytes=limit)


def cost(flops, transcendentals, *arrays):
    size = sum(math.prod(a.shape) * a.dtype.itemsize for a in arrays)
    return pl.CostEstimate(
        flops=int(flops) // COST_SCALE,
        transcendentals=int(transcendentals) // COST_SCALE,
        bytes_accessed=int(size) // COST_SCALE,
    )


def attention_forward(lengths, state, count, back, gain, shift, weight, qbias, obias, gain2, shift2):
    rows = state.shape[0]
    micro, docs = lengths.shape
    width = FEATURES
    shape = pltpu.HBM
    outs = (
        shape((rows, width), jnp.bfloat16),
        shape((rows, 3 * width), jnp.bfloat16),
        shape((rows, width), jnp.bfloat16),
        shape((micro * H, 1, count), jnp.float32),
        shape((rows, width), jnp.float32),
        shape((rows, width), jnp.bfloat16),
    )
    weights = (gain, shift, weight, qbias, obias, gain2, shift2)
    return pl.pallas_call(
        functools.partial(attention_forward_kernel, docs, back),
        grid=(micro,),
        out_shape=outs,
        in_specs=[SMEM, rows_of(count, width)] + [whole(w) for w in weights],
        out_specs=(
            rows_of(count, width),
            rows_of(count, 3 * width),
            rows_of(count, width),
            pl.BlockSpec((H, 1, count), lambda i: (i, 0, 0)),
            rows_of(count, width),
            rows_of(count, width),
        ),
        scratch_shapes=[
            pltpu.VMEM((count, count), jnp.float32),
            pltpu.VMEM((count, 128), jnp.float32),
        ],
        compiler_params=params(),
        cost_estimate=cost(
            8 * rows * width * width + 4 * rows * count * width, rows * count * H, state, *weights, *outs
        ),
        name="attention_forward",
    )(lengths, *in_hbm((state, *weights)))


GELU_C = 0.7978845608028654
GELU_K = 0.044715 * GELU_C


def gelu_gate(value):
    square = value * value
    gate = 0.5 * jnp.tanh(value * (GELU_C + GELU_K * square)) + 0.5
    return (gate, square)


def mlp_forward_kernel(
    hidden_ref, normed_ref, fc_ref, fbias_ref, proj_ref, pbias_ref, expanded_ref, state_ref
):
    chunk = 256

    @pl.when(pl.program_id(0) == 0)
    def _():
        state_ref[...] = hidden_ref[...] + pbias_ref[...]

    for start in range(0, normed_ref.shape[0], chunk):
        rows = slice(start, start + chunk)
        expanded = dot(normed_ref[rows, :], square_of(fc_ref)) + fbias_ref[...]
        expanded_ref[rows, :] = expanded.astype(expanded_ref.dtype)
        gate, unused = gelu_gate(expanded)
        activated = (expanded * gate).astype(jnp.bfloat16)
        state_ref[rows, :] += dot(activated, square_of(proj_ref))


DEVICE_GROUPS = 16


def square_of(ref):
    return ref[...].reshape(FEATURES, FEATURES)


def fc_at(step):
    return jnp.minimum(step, 3)


FC_BLOCK = pl.BlockSpec((16, 1, 1, 48, FEATURES), lambda i: (0, fc_at(i) // 2, fc_at(i) % 2, 0, 0))
PROJ_BLOCK = pl.BlockSpec((4, 2, 2, 48, FEATURES), lambda i: (fc_at(i), 0, 1, 0, 0))


def mlp_forward(hidden, normed, mlp, fbias, pbias):
    rows, width = hidden.shape
    block = width
    hidden_units = 4 * block
    shape = pltpu.HBM
    outs = (
        shape((rows, hidden_units), jnp.bfloat16),
        shape((rows, width), jnp.float32),
    )
    specs = (
        pl.BlockSpec((rows, block), lambda i: (0, i)),
        pl.BlockSpec((rows, width), lambda i: (0, 0)),
    )
    return pl.pallas_call(
        mlp_forward_kernel,
        grid=(hidden_units // block,),
        out_shape=outs,
        in_specs=[
            whole(hidden),
            whole(normed),
            FC_BLOCK,
            pl.BlockSpec((1, block), lambda i: (0, i)),
            PROJ_BLOCK,
            whole(pbias),
        ],
        out_specs=specs,
        compiler_params=params(),
        cost_estimate=cost(
            4 * rows * width * hidden_units, rows * hidden_units, hidden, normed, mlp, *outs
        ),
        name="mlp_forward",
    )(*in_hbm((hidden, normed, mlp, fbias, mlp, pbias)))


def transposed_dot(left, right):
    return lax.dot_general(
        left, right, (((0,), (0,)), ((), ())), preferred_element_type=jnp.float32
    )


def dot_transposed(left, right):
    return lax.dot_general(
        left, right, (((1,), (1,)), ((), ())), preferred_element_type=jnp.float32
    )


def store_halves(core, value, mine_ref, theirs_ref, earlier):
    half = value.shape[1] // 2
    left, right = (value[:, :half], value[:, half:])
    mine = jnp.where(core == 0, left, right)
    theirs = jnp.where(core == 0, right, left)
    shape = mine_ref.shape
    mine, theirs = (mine.reshape(shape), theirs.reshape(shape))
    if earlier is not None:
        mine = mine + earlier[0][...].astype(jnp.float32)
        theirs = theirs + earlier[1][...].astype(jnp.float32)
    mine_ref[...] = mine.astype(mine_ref.dtype)
    theirs_ref[...] = theirs.astype(theirs_ref.dtype)


def mlp_backward_kernel(
    more,
    forward,
    core_ref,
    grad_ref,
    hidden_ref,
    normed_ref,
    att_ref,
    *rest,
):
    if forward:
        fbias_ref, pbias_ref, fc_ref, proj_ref, gain_ref, *rest = rest
    else:
        expanded_ref, fc_ref, proj_ref, gain_ref, *rest = rest
    earlier = rest[:11] if more else (None,) * 11
    if more:
        rest = rest[11:]
    if forward:
        final_ref, *rest, state_ref = rest
    (
        dhid_ref,
        fc_mine,
        fc_theirs,
        proj_mine,
        proj_theirs,
        out_mine,
        out_theirs,
        dobias_ref,
        dfbias_ref,
        dpbias_ref,
        dgain_ref,
        dshift_ref,
        low_ref,
        normed_t,
        acc_ref,
        act_ref,
        ge_ref,
        hidden_buf,
        att_buf,
        sems,
    ) = rest
    step = pl.program_id(0)
    core = core_ref[0]
    rows = grad_ref.shape[0]
    blocks = pl.num_programs(0) - 1
    chunk = 256
    chunks = [slice(start, start + chunk) for start in range(0, rows, chunk)]
    late = [
        pltpu.make_async_copy(hidden_ref, hidden_buf, sems.at[0]),
        pltpu.make_async_copy(att_ref, att_buf, sems.at[1]),
    ]

    @pl.when(step == 0)
    def _():
        for copy in late:
            copy.start()
        low_grad = grad_ref[...].astype(jnp.bfloat16)
        low_ref[...] = low_grad
        dpbias = jnp.sum(low_grad.astype(jnp.float32), axis=0, keepdims=True)
        dpbias_ref[...] = dpbias + earlier[8][...] if more else dpbias
        normed_t[...] = jnp.transpose(normed_ref[...])
        acc_ref[...] = jnp.zeros_like(acc_ref)
        if forward:
            state_ref[...] = jnp.zeros_like(state_ref)

    @pl.when(step < blocks)
    def _():
        bias_sum = jnp.zeros(dfbias_ref.shape[1:], jnp.float32)
        for part in chunks:
            grad_act = dot_transposed(low_ref[part, :], square_of(proj_ref))
            if forward:
                value = dot(normed_ref[part, :], square_of(fc_ref)) + fbias_ref[...]
            else:
                value = expanded_ref[part, :].astype(jnp.float32)
            gate, square = gelu_gate(value)
            act = value * gate
            slope = gate + act * (1.0 - gate) * (2 * GELU_C + 6 * GELU_K * square)
            activated = act.astype(jnp.bfloat16)
            act_ref[part, :] = activated
            if forward:
                state_ref[part, :] += dot(activated, square_of(proj_ref))
            grad_exp = (grad_act * slope).astype(jnp.bfloat16)
            ge_ref[part, :] = grad_exp
            bias_sum = bias_sum + jnp.sum(grad_exp.astype(jnp.float32), axis=0, keepdims=True)
            acc_ref[part, :] += dot_transposed(grad_exp, square_of(fc_ref))
        dfbias_ref[0] = bias_sum + earlier[7][0] if more else bias_sum
        dproj = transposed_dot(act_ref[...], low_ref[...])
        store_halves(core, dproj, proj_mine, proj_theirs, earlier[2:4] if more else None)
        dfc = dot(normed_t[...], ge_ref[...])
        store_halves(core, dfc, fc_mine, fc_theirs, earlier[:2] if more else None)

    @pl.when(step == blocks)
    def _():
        for copy in late:
            copy.wait()
        dgain = jnp.zeros(dgain_ref.shape, jnp.float32)
        dshift, dobias = (dgain, dgain)
        copies = []
        for index, part in enumerate(chunks):
            hidden = hidden_buf[part, :]
            if forward:
                final = hidden + (state_ref[part, :] + pbias_ref[...])
                final_ref[part, :] = final.astype(jnp.bfloat16)
            normed, scale = norm_parts(hidden)
            grad_norm = acc_ref[part, :]
            dgain = dgain + jnp.sum(grad_norm * normed, axis=0, keepdims=True)
            dshift = dshift + jnp.sum(grad_norm, axis=0, keepdims=True)
            dhid = grad_ref[part, :].astype(jnp.float32) + norm_back(
                normed, scale, gain_ref[...], grad_norm
            )
            hidden_buf[part, :] = dhid
            copies.append(
                pltpu.make_async_copy(
                    hidden_buf.at[part, :], dhid_ref.at[part, :], sems.at[2 + index]
                )
            )
            copies[-1].start()
            low_dhid = dhid.astype(jnp.bfloat16)
            low_ref[part, :] = low_dhid
            dobias = dobias + jnp.sum(low_dhid.astype(jnp.float32), axis=0, keepdims=True)
        dgain_ref[...] = dgain + earlier[9][...] if more else dgain
        dshift_ref[...] = dshift + earlier[10][...] if more else dshift
        dobias_ref[...] = dobias + earlier[6][...] if more else dobias
        dout = transposed_dot(att_buf[...], low_ref[...])
        store_halves(core, dout, out_mine, out_theirs, earlier[4:6] if more else None)
        for copy in copies:
            copy.wait()


def mlp_backward(core, grad, hidden, normed, att, expanded, mlp, gain, earlier=None, biases=None):
    rows, width = hidden.shape
    blocks, block = (4, width)
    shape = pltpu.HBM
    groups = DEVICE_GROUPS
    each = width // groups
    fc_half = shape((groups, blocks, each, width // 2), jnp.bfloat16)
    proj_half = shape((blocks * width, width // 2), jnp.bfloat16)
    out_half = shape((groups, each, width // 2), jnp.bfloat16)
    row = shape((1, width), jnp.float32)
    outs = (
        shape((rows, width), jnp.float32),
        fc_half,
        fc_half,
        proj_half,
        proj_half,
        out_half,
        out_half,
        row,
        shape((blocks, 1, block), jnp.float32),
        row,
        row,
        row,
    )
    fc_spec = pl.BlockSpec((groups, None, each, width // 2), lambda i: (0, jnp.minimum(i, 3), 0, 0))
    proj_spec = pl.BlockSpec((width, width // 2), lambda i: (jnp.minimum(i, 3), 0))
    out_spec = pl.BlockSpec((groups, each, width // 2), lambda i: (0, 0, 0))
    bias = pl.BlockSpec((1, 1, block), lambda i: (jnp.minimum(i, 3), 0, 0))
    vector = pl.BlockSpec((1, width), lambda i: (0, 0))
    inputs = [grad, hidden, normed, att]
    raw = pl.BlockSpec(memory_space=pltpu.HBM)
    specs = [whole(grad), raw, whole(normed), raw]
    out_specs = [raw]
    scratch = []
    if biases is None:
        inputs.append(expanded)
        specs.append(pl.BlockSpec((rows, block), lambda i: (0, jnp.minimum(i, 3))))
    else:
        inputs += list(biases)
        specs += [pl.BlockSpec((1, block), lambda i: (0, jnp.minimum(i, 3))), whole(biases[1])]
        outs = (shape((rows, width), jnp.bfloat16), *outs)
        out_specs = [pl.BlockSpec((rows, width), lambda i: (0, 0)), raw]
        scratch = [pltpu.VMEM((rows, width), jnp.float32)]
    inputs += [mlp, mlp, gain]
    specs += [FC_BLOCK, PROJ_BLOCK, whole(gain)]
    summed = [fc_spec, fc_spec, proj_spec, proj_spec, out_spec, out_spec, vector, bias]
    summed += [vector, vector, vector]
    if earlier is not None:
        inputs += list(earlier)
        specs += summed
    return pl.pallas_call(
        functools.partial(mlp_backward_kernel, earlier is not None, biases is not None),
        grid=(blocks + 1,),
        out_shape=outs,
        in_specs=[SMEM] + specs,
        out_specs=out_specs + summed,
        scratch_shapes=[
            pltpu.VMEM((rows, width), jnp.bfloat16),
            pltpu.VMEM((width, rows), jnp.bfloat16),
            pltpu.VMEM((rows, width), jnp.float32),
            pltpu.VMEM((rows, block), jnp.bfloat16),
            pltpu.VMEM((rows, block), jnp.bfloat16),
            pltpu.VMEM((rows, width), jnp.float32),
            pltpu.VMEM((rows, width), jnp.bfloat16),
            pltpu.SemaphoreType.DMA((2 + rows // 256,)),
            *scratch,
        ],
        compiler_params=params(54 << 20),
        cost_estimate=cost(8 * rows * width * blocks * block, rows * blocks * block, *inputs, *outs),
        name="mlp_backward",
    )(core, *in_hbm(inputs))


def input_gradient(
    dhid_ref, state_ref, gmix_ref, weight_ref, gain_ref, earlier, grad_ref, dgain_ref, dshift_ref
):
    step = pl.program_id(0)
    grad_norm = dot_transposed(gmix_ref[:, :FEATURES], weight_ref[0])
    for part in range(1, 3):
        grad_norm = grad_norm + dot_transposed(
            gmix_ref[:, part * FEATURES : (part + 1) * FEATURES], weight_ref[part]
        )
    normed, scale = norm_parts(state_ref[...].astype(jnp.float32))
    dgain = jnp.sum(grad_norm * normed, axis=0, keepdims=True)
    dshift = jnp.sum(grad_norm, axis=0, keepdims=True)

    @pl.when(step == 0)
    def _():
        dgain_ref[...] = dgain if earlier is None else dgain + earlier[0][...]
        dshift_ref[...] = dshift if earlier is None else dshift + earlier[1][...]

    @pl.when(step > 0)
    def _():
        dgain_ref[...] += dgain
        dshift_ref[...] += dshift

    grad = dhid_ref[...] + norm_back(normed, scale, gain_ref[...], grad_norm)
    grad_ref[...] = grad.astype(grad_ref.dtype)


def attention_backward_kernel(
    docs,
    back,
    micro,
    lengths_ref,
    dhid_ref,
    att_ref,
    mixed_ref,
    lse_ref,
    out_ref,
    *rest,
):
    if micro is None:
        micro = pl.program_id(0)
        state_ref, gain_ref, gmix_ref, grad_ref, dgain_ref, dshift_ref, *rest = rest
        finish = functools.partial(
            input_gradient, dhid_ref, state_ref, gmix_ref, out_ref, gain_ref, None,
            grad_ref, dgain_ref, dshift_ref,
        )
    else:
        gmix_ref, *rest = rest
        finish = None
    datt_ref, bias_ref, delta_ref, dq_ref = rest
    count = dhid_ref.shape[0]
    low_grad = dhid_ref[...].astype(jnp.bfloat16)
    datt = dot_transposed(low_grad, out_ref[out_ref.shape[0] - 1]).astype(jnp.bfloat16)
    datt_ref[...] = datt
    product = datt.astype(jnp.float32) * att_ref[...].astype(jnp.float32)
    high = product.astype(jnp.bfloat16)
    rest_low = (product - high.astype(jnp.float32)).astype(jnp.bfloat16)
    feature = lax.broadcasted_iota(jnp.int32, (16, FEATURES), 1)
    head = lax.broadcasted_iota(jnp.int32, (16, FEATURES), 0)
    chosen = ((feature >= head * HD) & (feature < (head + 1) * HD)).astype(jnp.bfloat16)
    delta = dot_transposed(chosen, high) + dot_transposed(chosen, rest_low)
    for index in range(H):
        delta_ref[index] = delta[index : index + 1]
    bias_ref[...] = allowed_bias(count, [lengths_ref[micro, d] for d in range(docs)], docs, 1)

    def one_group(group, carry):
        lanes = pl.multiple_of(group * LANES, LANES)
        dq_ref[...] = jnp.zeros_like(dq_ref)
        for block in range(count // BLOCK):
            keys = slice(block * BLOCK, (block + 1) * BLOCK)
            rows = slice(block * BLOCK, min(count, (block + 1 + back) * BLOCK))
            key = head_split(mixed_ref[keys, pl.ds(FEATURES + lanes, LANES)])
            value = head_split(mixed_ref[keys, pl.ds(2 * FEATURES + lanes, LANES)])
            query = mixed_ref[rows, pl.ds(lanes, LANES)]
            datt_group = datt_ref[rows, pl.ds(lanes, LANES)]
            scores = dot_transposed(key, query)
            dprobs = dot_transposed(value, datt_group)
            bias = bias_ref[keys, rows]
            probs_low, dscores_low = ([], [])
            for h in range(GROUP):
                part = slice(h * BLOCK, (h + 1) * BLOCK)
                lse = lse_ref[GROUP * group + h, :, rows]
                delta = delta_ref[GROUP * group + h, :, rows]
                probs = jnp.exp((scores[part] * 0.125 + bias) - lse)
                dscores = probs * (dprobs[part] - delta)
                probs_low.append(probs.astype(jnp.bfloat16))
                dscores_low.append(dscores.astype(jnp.bfloat16))
            probs_low = jnp.concatenate(probs_low, axis=0)
            dscores_low = jnp.concatenate(dscores_low, axis=0)
            dvalue = head_join(dot(probs_low, datt_group))
            dkey = head_join(dot(dscores_low, query)) * 0.125
            dq_ref[rows, :] += transposed_dot(dscores_low, key)
            gmix_ref[keys, pl.ds(FEATURES + lanes, LANES)] = dkey.astype(jnp.bfloat16)
            gmix_ref[keys, pl.ds(2 * FEATURES + lanes, LANES)] = dvalue.astype(jnp.bfloat16)
        gmix_ref[:, pl.ds(lanes, LANES)] = (dq_ref[...] * 0.125).astype(jnp.bfloat16)
        return carry

    lax.fori_loop(0, H // GROUP, one_group, 0, unroll=H // GROUP)
    if finish is not None:
        finish()


def attention_backward(micro, lengths, dhid, count, back, att, mixed, lse, weight):
    width = dhid.shape[1]
    docs = lengths.shape[1]
    outs = jax.ShapeDtypeStruct((count, 3 * width), jnp.bfloat16)
    inputs = [dhid, att, mixed, lse, weight]
    return pl.pallas_call(
        functools.partial(attention_backward_kernel, docs, back, micro),
        grid=(1,),
        out_shape=outs,
        in_specs=[
            SMEM,
            pl.BlockSpec((count, width), lambda i: (micro, 0)),
            pl.BlockSpec((count, width), lambda i: (micro, 0)),
            pl.BlockSpec((count, 3 * width), lambda i: (micro, 0)),
            pl.BlockSpec((H, 1, count), lambda i: (micro, 0, 0)),
            pl.BlockSpec((1, width, width), lambda i: (3, 0, 0)),
        ],
        out_specs=pl.BlockSpec((count, 3 * width), lambda i: (0, 0)),
        scratch_shapes=[
            pltpu.VMEM((count, width), jnp.bfloat16),
            pltpu.VMEM((count, count), jnp.float32),
            pltpu.VMEM((H, 1, count), jnp.float32),
            pltpu.VMEM((count, LANES), jnp.float32),
        ],
        compiler_params=params(),
        cost_estimate=cost(
            2 * count * width * width + 10 * count * count * width, count * count * H, outs, outs
        ),
        name="attention_backward",
    )(lengths, *in_hbm(inputs))


def attention_backward_all(lengths, dhid, count, back, att, mixed, lse, weight, state, gain):
    rows, width = dhid.shape
    micro, docs = lengths.shape
    vector = pl.BlockSpec((1, width), lambda i: (0, 0))
    outs = (
        pltpu.HBM((rows, 3 * width), jnp.bfloat16),
        pltpu.HBM((rows, width), jnp.float32),
        jax.ShapeDtypeStruct((1, width), jnp.float32),
        jax.ShapeDtypeStruct((1, width), jnp.float32),
    )
    inputs = [dhid, att, mixed, lse, weight, state, gain]
    return pl.pallas_call(
        functools.partial(attention_backward_kernel, docs, back, None),
        grid=(micro,),
        out_shape=outs,
        in_specs=[
            SMEM,
            rows_of(count, width),
            rows_of(count, width),
            rows_of(count, 3 * width),
            pl.BlockSpec((H, 1, count), lambda i: (i, 0, 0)),
            whole(weight),
            rows_of(count, width),
            whole(gain),
        ],
        out_specs=[rows_of(count, 3 * width), rows_of(count, width), vector, vector],
        scratch_shapes=[
            pltpu.VMEM((count, width), jnp.bfloat16),
            pltpu.VMEM((count, count), jnp.float32),
            pltpu.VMEM((H, 1, count), jnp.float32),
            pltpu.VMEM((count, LANES), jnp.float32),
        ],
        compiler_params=params(44 << 20),
        cost_estimate=cost(
            8 * rows * width * width + 10 * rows * count * width, rows * count * H, *inputs, *outs
        ),
        name="attention_backward_all",
    )(lengths, *in_hbm(inputs))


def attention_terms_kernel(more, micro, core_ref, normed_ref, *rest):
    gmix_refs, rest = (rest[:micro], rest[micro:])
    earlier = rest[:3] if more else (None,) * 3
    if more:
        rest = rest[3:]
    mine_ref, theirs_ref, dbias_ref = rest
    core = core_ref[0]
    terms, dbias, start = (0.0, 0.0, 0)
    for gmix_ref in gmix_refs:
        right = gmix_ref[...]
        stop = start + right.shape[0]
        terms = terms + transposed_dot(normed_ref[start:stop], right)
        dbias = dbias + jnp.sum(right.astype(jnp.float32), axis=0, keepdims=True)
        start = stop
    dbias_ref[0] = dbias + earlier[2][0] if more else dbias
    store_halves(core, terms, mine_ref, theirs_ref, earlier[:2] if more else None)


def attention_terms(core, normed, gmix, earlier=None):
    rows, width = normed.shape
    groups = DEVICE_GROUPS
    each = width // groups
    shape = pltpu.HBM
    half = shape((groups, 3, each, width // 2), jnp.bfloat16)
    outs = (half, half, shape((3, 1, width), jnp.float32))
    halves = pl.BlockSpec((groups, None, each, width // 2), lambda i: (0, i, 0, 0))
    summed = [halves, halves, pl.BlockSpec((1, 1, width), lambda i: (i, 0, 0))]
    inputs = [normed, *gmix]
    specs = [whole(normed)] + [
        pl.BlockSpec((part.shape[0], width), lambda i: (0, i)) for part in gmix
    ]
    if earlier is not None:
        inputs += list(earlier)
        specs += summed
    return pl.pallas_call(
        functools.partial(attention_terms_kernel, earlier is not None, len(gmix)),
        grid=(3,),
        out_shape=outs,
        in_specs=[SMEM] + specs,
        out_specs=summed,
        compiler_params=params(),
        cost_estimate=cost(6 * rows * width * width, 0, *inputs, *outs),
        name="attention_terms",
    )(core, *in_hbm(inputs[:1]), *gmix, *in_hbm(inputs[1 + len(gmix) :]))


def attention_input_kernel(more, micro, dhid_ref, state_ref, weight_ref, gain_ref, *rest):
    gmix_refs, rest = (rest[:micro], rest[micro:])
    earlier = rest[:2] if more else None
    if more:
        rest = rest[2:]
    grad_ref, dgain_ref, dshift_ref, gmix_ref = rest
    each = pl.num_programs(0) // micro
    for index, part_ref in enumerate(gmix_refs):

        @pl.when(pl.program_id(0) // each == index)
        def _(part_ref=part_ref):
            gmix_ref[...] = part_ref[...]

    input_gradient(
        dhid_ref, state_ref, gmix_ref, weight_ref, gain_ref, earlier, grad_ref, dgain_ref, dshift_ref
    )


def attention_input(dhid, state, gmix, weight, gain, kind, earlier=None, chunk=256):
    rows, width = dhid.shape
    shape = jax.ShapeDtypeStruct
    vector = pl.BlockSpec((1, width), lambda i: (0, 0))
    outs = (shape((rows, width), kind), shape((1, width), jnp.float32), shape((1, width), jnp.float32))
    inputs = [dhid, state, weight, gain, *gmix]
    each = rows // chunk // len(gmix)
    specs = [
        rows_of(chunk, width),
        rows_of(chunk, width),
        pl.BlockSpec((3, width, width), lambda i: (0, 0, 0), pipeline_mode=pl.Buffered(1)),
        whole(gain),
    ]
    for index in range(len(gmix)):
        specs.append(
            pl.BlockSpec(
                (chunk, 3 * width),
                lambda i, index=index: (jnp.clip(i - index * each, 0, each - 1), 0),
            )
        )
    if earlier is not None:
        inputs += list(earlier)
        specs += [vector, vector]
    return pl.pallas_call(
        functools.partial(attention_input_kernel, earlier is not None, len(gmix)),
        grid=(rows // chunk,),
        out_shape=outs,
        in_specs=specs,
        out_specs=[rows_of(chunk, width), vector, vector],
        scratch_shapes=[pltpu.VMEM((chunk, 3 * width), jnp.bfloat16)],
        compiler_params=params(),
        cost_estimate=cost(6 * rows * width * width, 0, *inputs, *outs),
        name="attention_input",
    )(*in_hbm(inputs[:4]), *gmix, *in_hbm(inputs[4 + len(gmix) :]))


def place_small_kernel(sizes, me_ref, *refs):
    smalls, outs = (refs[:4], refs[4:])
    dp = me_ref[0] // 2
    slot = lax.broadcasted_iota(jnp.int32, (16, 1), 0)
    owner = ((slot % 4) * 4 + (slot // 8) * 2 + slot // 4 % 2) ^ dp
    for index, (size, out_ref) in enumerate(zip(sizes, outs)):
        width = 16 * size
        lane = lax.broadcasted_iota(jnp.int32, (256, width), 0)
        column = lax.broadcasted_iota(jnp.int32, (256, width), 1)
        spread = (column % size == lane).astype(jnp.bfloat16)
        rows = jnp.concatenate([ref[z, index : index + 1] for ref in smalls for z in range(4)], axis=0)
        spread_rows = dot(rows, spread)
        column = lax.broadcasted_iota(jnp.int32, (1, width), 1)
        out_ref[...] = jnp.sum(
            jnp.where(column // size == owner, spread_rows, 0.0), axis=0, keepdims=True
        )


def place_small(me, smalls, sizes):
    return pl.pallas_call(
        functools.partial(place_small_kernel, sizes),
        out_shape=[jax.ShapeDtypeStruct((1, 16 * size), jnp.float32) for size in sizes],
        in_specs=[SMEM] + [pl.BlockSpec(memory_space=pltpu.VMEM)] * len(smalls),
        out_specs=[pl.BlockSpec(memory_space=pltpu.VMEM)] * len(sizes),
        name="place_small",
    )(me, *smalls)


def swap(value, bits):
    return lax.ppermute(value, BOTH, [(i, i ^ bits) for i in range(32)])


CORE, X, Y, Z1, Z2, Z3 = (1, 2, 4, 8, 16, 24)


def place_kernel(slots, me_ref, *refs):
    sources, (out, sems) = (refs[: len(slots)], refs[len(slots) :])
    me = me_ref[0]
    copies = []
    for source, rels in zip(sources, slots):
        for inner, rel in enumerate(rels):
            copies.append(
                pltpu.make_async_copy(
                    source.at[inner], out.at[:, rel ^ me], sems.at[len(copies)]
                )
            )
    for copy in copies:
        copy.start()
    for copy in copies:
        copy.wait()


def place(me, sources, slots):
    placed = pl.pallas_call(
        functools.partial(place_kernel, slots),
        out_shape=jax.ShapeDtypeStruct((4, 32, 24, FEATURES), jnp.bfloat16),
        in_specs=[SMEM] + [pl.BlockSpec(memory_space=pl.ANY)] * len(sources),
        out_specs=pl.BlockSpec(memory_space=pltpu.VMEM),
        scratch_shapes=[pltpu.SemaphoreType.DMA((32,))],
        name="place",
    )(me, *sources)
    return placed.reshape(4, FEATURES, FEATURES)


def after(values, *others):
    return lax.optimization_barrier((values, others))[0]


def gather_first(piece, small, me):
    base = (0, Z1, Z2, Z3)
    pieces = lax.optimization_barrier(
        [piece] + [swap(piece, bits) for bits in base[1:]]
        + [small] + [swap(small, bits) for bits in base[1:]]
    )
    four, small = (jnp.concatenate(pieces[:4]), jnp.concatenate(pieces[4:]))
    four_x, four_y, four_core, small_x, small_y = lax.optimization_barrier(
        (swap(four, X), swap(four, Y), swap(four, CORE), swap(small, X), swap(small, Y))
    )
    near_xy, far_xy, x_core, y_core, small_xy = lax.optimization_barrier(
        (
            swap(four_y[:2], X), swap(four_x[2:], Y), swap(four_x, CORE), swap(four_y, CORE),
            swap(small_y, X),
        )
    )
    parts = [four, four_x, four_y, near_xy, far_xy]
    parts += [four_core, x_core, y_core, swap(near_xy, CORE), swap(far_xy, CORE)]
    slots = [base] + [tuple(rel ^ bits for rel in base) for bits in (X, Y)]
    slots += [(X ^ Y, X ^ Y ^ Z1), (X ^ Y ^ Z2, X ^ Y ^ Z3)]
    slots += [tuple(rel ^ CORE for rel in rels) for rels in slots]
    return (place(me, parts, slots), (small, small_x, small_y, small_xy))


def pick(array, axis, index):
    return lax.dynamic_index_in_dim(array, index, axis, keepdims=False)


def low(value):
    return value.astype(jnp.bfloat16)


def wide(value):
    return value.astype(jnp.float32)


def add(*terms):
    total = wide(terms[0])
    for term in terms[1:]:
        total = total + wide(term)
    return total


def device_at(z_pair, z_low, y, x):
    return z_pair * 8 + z_low * 4 + y * 2 + x


def total(*terms):
    result = terms[0].astype(jnp.float32)
    for term in terms[1:]:
        result = result + term.astype(jnp.float32)
    return result


def first_sums_kernel(views, spot_ref, *refs):
    mine, got, alone = (refs[:views], refs[views : 2 * views], refs[2 * views : -4])
    near_sent, far_sent, near_kept, far_kept = refs[-4:]
    z_pair, y, x = (spot_ref[0], spot_ref[2], spot_ref[3])
    for low_z in range(2):
        for other in range(2):
            for out, device in (
                (near_sent, device_at(z_pair, low_z, other, 1 - x)),
                (far_sent, device_at(1 - z_pair, low_z, 1 - y, other)),
                (near_kept, device_at(z_pair, low_z, other, x)),
                (far_kept, device_at(1 - z_pair, low_z, y, other)),
            ):
                start = 0
                for left, right in zip(mine, got):
                    count = left.shape[1]
                    out[low_z, other, start : start + count] = total(
                        left[device], right[device]
                    ).astype(jnp.bfloat16)
                    start += count
                for only in alone:
                    out[low_z, other, start:] = only[device]


def second_sums_kernel(spot_ref, near, far, near_in, far_in, *outs):
    near_sent, far_sent, near_kept, far_kept = outs
    y, x = (spot_ref[2], spot_ref[3])
    for low_z in range(2):
        for out, kept, got, index in (
            (near_sent, near, near_in, 1 - y),
            (far_sent, far, far_in, 1 - x),
            (near_kept, near, near_in, y),
            (far_kept, far, far_in, x),
        ):
            out[low_z] = total(kept[low_z, index], got[low_z, index]).astype(jnp.bfloat16)


def third_sums_kernel(spot_ref, near, far, near_in, far_in, sent, kept):
    low_z = spot_ref[1]
    for index, (left, right) in enumerate(((near, near_in), (far, far_in))):
        sent[index] = total(left[1 - low_z], right[1 - low_z]).astype(jnp.bfloat16)
        kept[index] = total(left[low_z], right[low_z])


def assemble_kernel(layouts, core_ref, half_ref, other_ref, *outs):
    if len(outs) > len(layouts):
        outs[-1][...] = half_ref[-16:] + other_ref[-16:]
    core = core_ref[0]
    half, other = (half_ref[...], other_ref[...])
    left = jnp.where(core == 0, half, other)
    right = jnp.where(core == 0, other, half)
    start, wide_half = (0, half.shape[1])
    for (blocks, rows), out in zip(layouts, outs):
        for block in range(blocks):
            part = slice(start, start + rows)
            column = 2 * block * wide_half
            out[:, column : column + wide_half] = left[part]
            out[:, column + wide_half : column + 2 * wide_half] = right[part]
            start += rows


SMALL_ROWS = ((48, 48, 144, 48, 48, 48), (192, 48))


def pack_small_kernel(unused_ref, *refs):
    *vectors, out = refs
    width = out.shape[2]
    device = lax.broadcasted_iota(jnp.int32, (16, 1), 0)
    rows, vectors = ([], iter(vectors))
    for sizes in SMALL_ROWS:
        row, start = (jnp.zeros((16, width), jnp.float32), 0)
        for size, ref in zip(sizes, vectors):
            if len(ref.shape) == 2:
                vector = ref[...]
            else:
                vector = jnp.concatenate([ref[i] for i in range(ref.shape[0])], axis=1)
            column = lax.broadcasted_iota(jnp.int32, (1, 16 * size), 1)
            parts = jnp.where(column // size == device, vector, 0.0).astype(jnp.bfloat16)
            place_in = lax.broadcasted_iota(jnp.int32, (16 * size, width), 0) % size + start
            lane = lax.broadcasted_iota(jnp.int32, (16 * size, width), 1)
            row = row + dot(parts, (place_in == lane).astype(jnp.bfloat16))
            start += size
        rows.append(row)
    line = lax.broadcasted_iota(jnp.int32, out.shape[1:], 0)
    for d in range(16):
        first, second = (rows[0][d : d + 1], rows[1][d : d + 1])
        value = jnp.where(line == 0, first, jnp.where(line == 1, second, 0.0))
        out[d] = value.astype(jnp.bfloat16)


def in_vmem(kernel, name, outs, *args):
    vmem = pl.BlockSpec(memory_space=pltpu.VMEM)
    return pl.pallas_call(
        kernel,
        out_shape=outs,
        in_specs=[SMEM] + [vmem] * (len(args) - 1),
        out_specs=[vmem] * len(outs),
        compiler_params=params(),
        cost_estimate=cost(0, 0, *args, *outs),
        name=name,
    )(*args)


class Reduction:
    def __init__(self, spot, mine, theirs):
        self.spot = spot
        self.mine = list(mine)
        self.got = [swap(part, CORE) for part in theirs]
        self.alone = []
        self.width = self.mine[0].shape[2]

    def like(self, *lead, kind=jnp.bfloat16):
        count = sum(part.shape[1] for part in (*self.mine, *self.alone))
        return jax.ShapeDtypeStruct((*lead, count, self.width), kind)

    def first(self):
        near_sent, far_sent, *self.kept = in_vmem(
            functools.partial(first_sums_kernel, len(self.mine)),
            "first_sums",
            [self.like(2, 2)] * 4,
            self.spot,
            *self.mine,
            *self.got,
            *self.alone,
        )
        self.got = [swap(near_sent, X), swap(far_sent, Y)]
        return self.kept

    def second(self):
        near_sent, far_sent, *self.kept = in_vmem(
            second_sums_kernel, "second_sums", [self.like(2)] * 4, self.spot, *self.kept, *self.got
        )
        self.got = [swap(near_sent, Y), swap(far_sent, X)]
        return self.kept

    def third(self):
        sent, kept = in_vmem(
            third_sums_kernel,
            "third_sums",
            [self.like(2), self.like(2, kind=jnp.float32)],
            self.spot,
            *self.kept,
            *self.got,
        )
        self.kept, self.got = ([kept], [swap(sent, Z1)])
        return self.kept

    def fourth(self):
        (kept,), (got,) = (self.kept, self.got)
        far = low(kept[1] + wide(got[1]))
        self.kept, self.got = ([kept[0], got[0]], [swap(far, Z2)])
        return far

    def fifth(self):
        half = total(*self.kept, *self.got)
        self.kept, self.got = ([half], [swap(half, CORE)])

    def whole(self, core, layouts):
        outs = [
            jax.ShapeDtypeStruct((rows, 2 * self.width * blocks), jnp.float32)
            for blocks, rows in layouts
        ]
        if self.alone:
            outs.append(jax.ShapeDtypeStruct((16, self.width), jnp.float32))
        return in_vmem(
            functools.partial(assemble_kernel, layouts), "assemble", outs, core, *self.kept, *self.got
        )


def gather_all(weights, spot, me):
    gain_a, shift_a, qkv, qbias, out, obias, gain_m, shift_m, fc, fbias, proj, pbias = weights
    core = spot[4]

    def half(weight):
        part = lax.dynamic_slice_in_dim(weight, core * 24, 24, 0)
        return jnp.transpose(part.reshape(24, -1, FEATURES), (1, 0, 2))

    columns = lax.dynamic_slice_in_dim(fc, core * 2 * FEATURES, 2 * FEATURES, 1)
    columns = jnp.transpose(columns.reshape(48, 2, FEATURES), (1, 0, 2))
    across = lax.dynamic_slice_in_dim(proj, core * 96, 96, 0).reshape(2, 48, FEATURES)
    mlp = lax.all_gather(jnp.concatenate([columns, across]), BOTH)
    mlp = mlp.reshape(16, 2, 4, 48, FEATURES)
    vectors = [gain_a, shift_a, qbias, obias, gain_m, shift_m, fbias, pbias]
    sizes = tuple(vector.shape[0] for vector in vectors)
    small = jnp.stack([jnp.pad(v, (0, 256 - size)) for v, size in zip(vectors, sizes)])
    first, smalls = gather_first(jnp.concatenate([half(qkv), half(out)])[None], small[None], me)
    return (first, mlp, *place_small(me, smalls, sizes))


def gather_plain(weights):
    whole_ones = [lax.all_gather(weight, "dp", axis=0, tiled=True) for weight in weights]
    gain_a, shift_a, qkv, qbias, out, obias, gain_m, shift_m, fc, fbias, proj, pbias = whole_ones

    def blocks(weight):
        return jnp.transpose(weight.reshape(FEATURES, -1, FEATURES), (1, 0, 2))

    rows = [
        wide(v).reshape(1, -1)
        for v in (gain_a, shift_a, qbias, obias, gain_m, shift_m, fbias, pbias)
    ]
    first = jnp.concatenate([blocks(qkv), blocks(out)])
    fc = blocks(fc).reshape(2, 2, 16, 48, FEATURES)
    fc = jnp.transpose(fc, (2, 0, 1, 3, 4))
    mlp = jnp.concatenate([fc, proj.reshape(16, 2, 2, 48, FEATURES)], axis=2)
    return (first, mlp, *rows)


def reduce_plain(matrices, small):
    def joined(left, right):
        both = jnp.concatenate([left, right], axis=-1)
        if both.ndim == 4:
            both = jnp.transpose(both, (0, 2, 1, 3)).reshape(FEATURES, -1)
        return both.reshape(-1, both.shape[-1])

    qkv, out, fc, proj = [joined(*pair) for pair in matrices]
    gain_a, shift_a, qbias, obias, gain_m, shift_m, fbias, pbias = [v.reshape(-1) for v in small]
    values = (
        gain_a, shift_a, qkv, qbias, out, obias, gain_m, shift_m, fc, fbias, proj, pbias
    )
    return tuple(
        wide(lax.psum(low(lax.psum_scatter(wide(v), "dp", scatter_dimension=0, tiled=True)), "rep"))
        for v in values
    )


def forward(tokens, lengths, count, back, weights):
    weight, mlp, gain_a, shift_a, qbias, obias, gain_m, shift_m, fbias, pbias = weights
    state, kept = (tokens, [])
    for use in range(USES):
        normed_a, mixed, att, lse, hidden, normed_m = attention_forward(
            lengths, state, count, back, gain_a, shift_a, weight, qbias, obias, gain_m, shift_m
        )
        expanded, after_mlp = (None, None)
        if use < USES - 1:
            expanded, after_mlp = mlp_forward(hidden, normed_m, mlp, fbias, pbias)
        kept.append((state, normed_a, mixed, att, lse, hidden, normed_m, expanded))
        state = after_mlp
    return kept


def shards(custom, tokens, doc_lengths, cotangent, *weights):
    micro, count, width = tokens.shape
    dp, core = (lax.axis_index("dp"), lax.axis_index("rep"))
    spot = (dp // 8, dp // 4 % 2, dp // 2 % 2, dp % 2, core)
    me = (dp * 2 + core).astype(jnp.int32).reshape(1)
    places = jnp.stack(spot).astype(jnp.int32)
    side = core.astype(jnp.int32).reshape(1) if custom else jnp.zeros((1,), jnp.int32)
    back = -(-(LONGEST - 1) // BLOCK)
    lengths = doc_lengths.reshape(micro, doc_lengths.shape[-1])
    whole_ones = gather_all(weights, spot, me) if custom else gather_plain(weights)
    kept = forward(tokens.reshape(micro * count, width), lengths, count, back, whole_ones)
    weight, mlp, gain_a, gain_m = (whole_ones[0], whole_ones[1], whole_ones[2], whole_ones[6])
    grad, mlp_terms, terms, norm = (cotangent.reshape(micro * count, width), None, None, None)
    delayed = None
    for use in range(USES - 1, -1, -1):
        before, normed_a, mixed, att, lse, hidden, normed_m, expanded = kept[use]
        last = use == USES - 1
        dhid, *mlp_terms = mlp_backward(
            side, grad, hidden, normed_m, att, expanded, mlp, gain_m, mlp_terms,
            whole_ones[-2:] if last else None,
        )
        if last:
            state, (dhid, *mlp_terms) = (dhid, mlp_terms)
        sending = custom and use == 0
        if delayed is not None:
            terms = delayed()
        if sending:
            fc_mine, fc_theirs, proj_mine, proj_theirs, out_mine, out_theirs = [
                part.reshape(16, -1, part.shape[-1]) for part in mlp_terms[:6]
            ]
            sums = Reduction(
                places, (fc_mine, proj_mine, out_mine), (fc_theirs, proj_theirs, out_theirs)
            )
            sums.got, terms = lax.optimization_barrier((sums.got, terms))
            dhid = after(dhid, sums.first())
        if use:
            gmix, grad, *norm = attention_backward_all(
                lengths, dhid, count, back, att, mixed, lse, weight, before, gain_a
            )
            delayed = functools.partial(attention_terms, side, normed_a, in_hbm([gmix]))
            continue
        gmix = [
            attention_backward(index, lengths, dhid, count, back, att, mixed, lse, weight)
            for index in range(micro)
        ]
        terms = attention_terms(side, normed_a, gmix, terms)
        if sending:
            qkv_sums = Reduction(
                places, *[(part.reshape(16, -1, part.shape[-1]),) for part in terms[:2]]
            )
            sums.got, terms = lax.optimization_barrier((sums.got, terms))
            gmix = after(gmix, sums.second())
        grad, *norm = attention_input(dhid, before, gmix, weight, gain_a, jnp.bfloat16, norm)
        if sending:
            sums.got, qkv_sums.got = after((sums.got, qkv_sums.got), norm)
    small = (norm[0], norm[1], terms[2], mlp_terms[6], mlp_terms[9], mlp_terms[10])
    small += (mlp_terms[7], mlp_terms[8])
    if custom:
        packed = jax.ShapeDtypeStruct((16, 16, width // 2), jnp.bfloat16)
        qkv_sums.alone = in_vmem(pack_small_kernel, "pack_small", [packed], side, *small)
        sums.got = after(sums.got, qkv_sums.alone)
        qkv_sums.got = after(qkv_sums.got, sums.third())
        qkv_sums.first()
        qkv_sums.second()
        qkv_sums.got = after(qkv_sums.got, sums.fourth())
        qkv_sums.third()
        qkv_sums.fourth()
        sums.fifth()
        qkv_sums.fifth()
        fc, proj, out = sums.whole(side, ((4, 48), (1, 192), (1, 48)))
        qkv, small = qkv_sums.whole(side, ((3, 48),))
        parts = []
        for row, sizes in enumerate(SMALL_ROWS):
            start = 0
            for size in sizes:
                parts.append(small[row, start : start + size])
                start += size
        gain_a, shift_a, qbias, obias, gain_m, shift_m, fbias, pbias = parts
        final = (
            gain_a, shift_a, qkv, qbias, out, obias, gain_m, shift_m, fc, fbias, proj, pbias
        )
    else:
        matrices = (terms[:2], mlp_terms[4:6], mlp_terms[:2], mlp_terms[2:4])
        final = reduce_plain(matrices, small)
    return (state.reshape(tokens.shape), grad.reshape(tokens.shape), *final)


def solution(mesh):
    custom = mesh.shape["dp"] == 16 and mesh.shape["rep"] == 2
    placed = tuple(
        P("dp", None) if index in (2, 4, 8, 10) else P("dp") for index in range(12)
    )
    rows = P(None, BOTH, None)
    return jax.shard_map(
        functools.partial(shards, custom),
        mesh=mesh,
        in_specs=(rows, rows, rows, *placed),
        out_specs=(rows, rows, *placed),
        check_vma=False,
    )
```

```python
import functools
import math

import jax
import jax.numpy as jnp
from jax import lax
from jax.experimental import pallas as pl
from jax.experimental.pallas import tpu as pltpu
from jax.sharding import PartitionSpec as P

H = 12
HD = 64
USES = 2
LONGEST = 256
BOTH = ("dp", "rep")


NORM_EPS = 1e-05
BLOCK = 128
FEATURES = H * HD
VMEM_LIMIT = 40 << 20
COST_SCALE = 8


def dot(left, right):
    return jnp.dot(left, right, preferred_element_type=jnp.float32)


def transposed_dot(left, right):
    return lax.dot_general(
        left, right, (((0,), (0,)), ((), ())), preferred_element_type=jnp.float32
    )


def dot_transposed(left, right):
    return lax.dot_general(
        left, right, (((1,), (1,)), ((), ())), preferred_element_type=jnp.float32
    )


def norm_parts(values):
    center = values - jnp.mean(values, axis=-1, keepdims=True)
    spread = jnp.mean(center * center, axis=-1, keepdims=True)
    scale = lax.rsqrt(spread + NORM_EPS)
    return (center * scale, scale)


def norm_back(normed, scale, gain, grad):
    inner = grad * gain
    first = jnp.mean(inner, axis=-1, keepdims=True)
    second = jnp.mean(inner * normed, axis=-1, keepdims=True)
    return (inner - first - normed * second) * scale


def segment_of(places, lengths, docs):
    end = jnp.int32(0)
    segment = jnp.zeros(places.shape, jnp.int32)
    for doc in range(docs):
        end = end + lengths[doc]
        segment = segment + (places >= end).astype(jnp.int32)
    return segment


def allowed_bias(count, lengths, docs, query_axis):
    query_shape = (count, 1) if query_axis == 0 else (1, count)
    key_shape = (1, count) if query_axis == 0 else (count, 1)
    query = lax.broadcasted_iota(jnp.int32, query_shape, query_axis)
    key = lax.broadcasted_iota(jnp.int32, key_shape, 1 - query_axis)
    same = segment_of(query, lengths, docs) == segment_of(key, lengths, docs)
    return jnp.where(same & (key <= query), 0.0, -1e30).astype(jnp.float32)


GROUP = 4
LANES = GROUP * HD


def head_split(array):
    head = lax.broadcasted_iota(jnp.int32, array.shape, 1) // HD
    zero = jnp.zeros_like(array)
    return jnp.concatenate([jnp.where(head == h, array, zero) for h in range(GROUP)], axis=0)


def head_join(stacked):
    count = stacked.shape[0] // GROUP
    head = lax.broadcasted_iota(jnp.int32, (count, LANES), 1) // HD
    joined = stacked[:count]
    for h in range(1, GROUP):
        joined = jnp.where(head == h, stacked[h * count : (h + 1) * count], joined)
    return joined


def attention_forward_kernel(
    docs,
    back,
    lengths_ref,
    state_ref,
    gain_ref,
    shift_ref,
    weight_ref,
    qbias_ref,
    obias_ref,
    gain2_ref,
    shift2_ref,
    normed_ref,
    mixed_ref,
    att_ref,
    lse_ref,
    hidden_ref,
    normed2_ref,
    bias_ref,
    lse_cols,
):
    micro = pl.program_id(0)
    state = state_ref[...].astype(jnp.float32)
    count = state.shape[0]
    normed = (norm_parts(state)[0] * gain_ref[...] + shift_ref[...]).astype(jnp.bfloat16)
    normed_ref[...] = normed
    for part in range(3):
        columns = slice(part * FEATURES, (part + 1) * FEATURES)
        mixed_ref[:, columns] = (dot(normed, weight_ref[part]) + qbias_ref[:, columns]).astype(
            jnp.bfloat16
        )
    bias_ref[...] = allowed_bias(count, [lengths_ref[micro, d] for d in range(docs)], docs, 0)
    lse_cols[...] = jnp.zeros_like(lse_cols)

    def one_group(group, carry):
        lanes = pl.multiple_of(group * LANES, LANES)
        for block in range(count // BLOCK):
            rows = slice(block * BLOCK, (block + 1) * BLOCK)
            low_key = max(0, block - back) * BLOCK
            keys = slice(low_key, (block + 1) * BLOCK)
            query = head_split(mixed_ref[rows, pl.ds(lanes, LANES)])
            key = mixed_ref[keys, pl.ds(FEATURES + lanes, LANES)]
            value = mixed_ref[keys, pl.ds(2 * FEATURES + lanes, LANES)]
            scores = dot_transposed(query, key)
            bias = bias_ref[rows, keys]
            scores = scores * 0.125 + jnp.concatenate([bias] * GROUP, axis=0)
            top = jnp.max(scores, axis=-1, keepdims=True)
            expo = jnp.exp(scores - top)
            total_expo = jnp.sum(expo, axis=-1, keepdims=True)
            result = dot(expo.astype(jnp.bfloat16), value) / total_expo
            att_ref[rows, pl.ds(lanes, LANES)] = head_join(result).astype(jnp.bfloat16)
            lse = top + jnp.log(total_expo)
            lane = lax.broadcasted_iota(jnp.int32, (BLOCK, 128), 1)
            for h in range(GROUP):
                lse_cols[rows, :] += jnp.where(
                    lane == GROUP * group + h, lse[h * BLOCK : (h + 1) * BLOCK], 0.0
                )
        return carry

    lax.fori_loop(0, H // GROUP, one_group, 0, unroll=H // GROUP)
    lse = jnp.transpose(lse_cols[...])
    for index in range(H):
        lse_ref[index] = lse[index : index + 1]
    hidden = state + (dot(att_ref[...], weight_ref[3]) + obias_ref[...])
    hidden_ref[...] = hidden
    normed2_ref[...] = (norm_parts(hidden)[0] * gain2_ref[...] + shift2_ref[...]).astype(
        jnp.bfloat16
    )


def whole(array):
    dims = len(array.shape)
    return pl.BlockSpec(array.shape, lambda *unused: (0,) * dims, pipeline_mode=pl.Buffered(1))


SMEM = pl.BlockSpec(memory_space=pltpu.SMEM)


def in_hbm(arrays):
    return [pltpu.with_memory_space_constraint(array, pltpu.HBM) for array in arrays]


def rows_of(count, width):
    return pl.BlockSpec((count, width), lambda i: (i, 0))


def params(limit=VMEM_LIMIT):
    return pltpu.CompilerParams(vmem_limit_bytes=limit)


def cost(flops, transcendentals, *arrays):
    size = sum(math.prod(a.shape) * a.dtype.itemsize for a in arrays)
    return pl.CostEstimate(
        flops=int(flops) // COST_SCALE,
        transcendentals=int(transcendentals) // COST_SCALE,
        bytes_accessed=int(size) // COST_SCALE,
    )


def attention_forward(lengths, state, count, back, gain, shift, weight, qbias, obias, gain2, shift2):
    rows = state.shape[0]
    micro, docs = lengths.shape
    width = FEATURES
    shape = pltpu.HBM
    outs = (
        shape((rows, width), jnp.bfloat16),
        shape((rows, 3 * width), jnp.bfloat16),
        shape((rows, width), jnp.bfloat16),
        shape((micro * H, 1, count), jnp.float32),
        shape((rows, width), jnp.float32),
        shape((rows, width), jnp.bfloat16),
    )
    weights = (gain, shift, weight, qbias, obias, gain2, shift2)
    return pl.pallas_call(
        functools.partial(attention_forward_kernel, docs, back),
        grid=(micro,),
        out_shape=outs,
        in_specs=[SMEM, rows_of(count, width)] + [whole(w) for w in weights],
        out_specs=(
            rows_of(count, width),
            rows_of(count, 3 * width),
            rows_of(count, width),
            pl.BlockSpec((H, 1, count), lambda i: (i, 0, 0)),
            rows_of(count, width),
            rows_of(count, width),
        ),
        scratch_shapes=[
            pltpu.VMEM((count, count), jnp.float32),
            pltpu.VMEM((count, 128), jnp.float32),
        ],
        compiler_params=params(),
        cost_estimate=cost(
            8 * rows * width * width + 4 * rows * count * width, rows * count * H, state, *weights, *outs
        ),
        name="attention_forward",
    )(lengths, *in_hbm((state, *weights)))


GELU_C = 0.7978845608028654
GELU_K = 0.044715 * GELU_C


def gelu_gate(value):
    square = value * value
    gate = 0.5 * jnp.tanh(value * (GELU_C + GELU_K * square)) + 0.5
    return (gate, square)


def mlp_forward_kernel(
    hidden_ref, normed_ref, fc_ref, fbias_ref, proj_ref, pbias_ref, expanded_ref, state_ref
):
    chunk = 256

    @pl.when(pl.program_id(0) == 0)
    def _():
        state_ref[...] = hidden_ref[...] + pbias_ref[...]

    for start in range(0, normed_ref.shape[0], chunk):
        rows = slice(start, start + chunk)
        expanded = dot(normed_ref[rows, :], square_of(fc_ref)) + fbias_ref[...]
        expanded_ref[rows, :] = expanded.astype(expanded_ref.dtype)
        gate, unused = gelu_gate(expanded)
        activated = (expanded * gate).astype(jnp.bfloat16)
        state_ref[rows, :] += dot(activated, square_of(proj_ref))


DEVICE_GROUPS = 16


def square_of(ref):
    return ref[...].reshape(FEATURES, FEATURES)


def fc_at(step):
    return jnp.minimum(step, 3)


FC_BLOCK = pl.BlockSpec((16, 1, 1, 48, FEATURES), lambda i: (0, fc_at(i) // 2, fc_at(i) % 2, 0, 0))
PROJ_BLOCK = pl.BlockSpec((4, 2, 2, 48, FEATURES), lambda i: (fc_at(i), 0, 1, 0, 0))


def mlp_forward(hidden, normed, mlp, fbias, pbias):
    rows, width = hidden.shape
    block = width
    hidden_units = 4 * block
    shape = pltpu.HBM
    outs = (
        shape((rows, hidden_units), jnp.bfloat16),
        shape((rows, width), jnp.float32),
    )
    specs = (
        pl.BlockSpec((rows, block), lambda i: (0, i)),
        pl.BlockSpec((rows, width), lambda i: (0, 0)),
    )
    return pl.pallas_call(
        mlp_forward_kernel,
        grid=(hidden_units // block,),
        out_shape=outs,
        in_specs=[
            whole(hidden),
            whole(normed),
            FC_BLOCK,
            pl.BlockSpec((1, block), lambda i: (0, i)),
            PROJ_BLOCK,
            whole(pbias),
        ],
        out_specs=specs,
        compiler_params=params(),
        cost_estimate=cost(
            4 * rows * width * hidden_units, rows * hidden_units, hidden, normed, mlp, *outs
        ),
        name="mlp_forward",
    )(*in_hbm((hidden, normed, mlp, fbias, mlp, pbias)))


def transposed_dot(left, right):
    return lax.dot_general(
        left, right, (((0,), (0,)), ((), ())), preferred_element_type=jnp.float32
    )


def dot_transposed(left, right):
    return lax.dot_general(
        left, right, (((1,), (1,)), ((), ())), preferred_element_type=jnp.float32
    )


def store_halves(core, value, mine_ref, theirs_ref, earlier):
    half = value.shape[1] // 2
    left, right = (value[:, :half], value[:, half:])
    mine = jnp.where(core == 0, left, right)
    theirs = jnp.where(core == 0, right, left)
    shape = mine_ref.shape
    mine, theirs = (mine.reshape(shape), theirs.reshape(shape))
    if earlier is not None:
        mine = mine + earlier[0][...].astype(jnp.float32)
        theirs = theirs + earlier[1][...].astype(jnp.float32)
    mine_ref[...] = mine.astype(mine_ref.dtype)
    theirs_ref[...] = theirs.astype(theirs_ref.dtype)


def mlp_backward_kernel(
    more,
    forward,
    core_ref,
    grad_ref,
    hidden_ref,
    normed_ref,
    att_ref,
    *rest,
):
    if forward:
        fbias_ref, pbias_ref, fc_ref, proj_ref, gain_ref, *rest = rest
    else:
        expanded_ref, fc_ref, proj_ref, gain_ref, *rest = rest
    earlier = rest[:11] if more else (None,) * 11
    if more:
        rest = rest[11:]
    if forward:
        final_ref, *rest, state_ref = rest
    (
        dhid_ref,
        fc_mine,
        fc_theirs,
        proj_mine,
        proj_theirs,
        out_mine,
        out_theirs,
        dobias_ref,
        dfbias_ref,
        dpbias_ref,
        dgain_ref,
        dshift_ref,
        low_ref,
        normed_t,
        acc_ref,
        act_ref,
        ge_ref,
        hidden_buf,
        att_buf,
        sems,
    ) = rest
    step = pl.program_id(0)
    core = core_ref[0]
    rows = grad_ref.shape[0]
    blocks = pl.num_programs(0) - 1
    chunk = 256
    chunks = [slice(start, start + chunk) for start in range(0, rows, chunk)]
    late = [
        pltpu.make_async_copy(hidden_ref, hidden_buf, sems.at[0]),
        pltpu.make_async_copy(att_ref, att_buf, sems.at[1]),
    ]

    @pl.when(step == 0)
    def _():
        for copy in late:
            copy.start()
        low_grad = grad_ref[...].astype(jnp.bfloat16)
        low_ref[...] = low_grad
        dpbias = jnp.sum(low_grad.astype(jnp.float32), axis=0, keepdims=True)
        dpbias_ref[...] = dpbias + earlier[8][...] if more else dpbias
        normed_t[...] = jnp.transpose(normed_ref[...])
        acc_ref[...] = jnp.zeros_like(acc_ref)
        if forward:
            state_ref[...] = jnp.zeros_like(state_ref)

    @pl.when(step < blocks)
    def _():
        bias_sum = jnp.zeros(dfbias_ref.shape[1:], jnp.float32)
        for part in chunks:
            grad_act = dot_transposed(low_ref[part, :], square_of(proj_ref))
            if forward:
                value = dot(normed_ref[part, :], square_of(fc_ref)) + fbias_ref[...]
            else:
                value = expanded_ref[part, :].astype(jnp.float32)
            gate, square = gelu_gate(value)
            act = value * gate
            slope = gate + act * (1.0 - gate) * (2 * GELU_C + 6 * GELU_K * square)
            activated = act.astype(jnp.bfloat16)
            act_ref[part, :] = activated
            if forward:
                state_ref[part, :] += dot(activated, square_of(proj_ref))
            grad_exp = (grad_act * slope).astype(jnp.bfloat16)
            ge_ref[part, :] = grad_exp
            bias_sum = bias_sum + jnp.sum(grad_exp.astype(jnp.float32), axis=0, keepdims=True)
            acc_ref[part, :] += dot_transposed(grad_exp, square_of(fc_ref))
        dfbias_ref[0] = bias_sum + earlier[7][0] if more else bias_sum
        dproj = transposed_dot(act_ref[...], low_ref[...])
        store_halves(core, dproj, proj_mine, proj_theirs, earlier[2:4] if more else None)
        dfc = dot(normed_t[...], ge_ref[...])
        store_halves(core, dfc, fc_mine, fc_theirs, earlier[:2] if more else None)

    @pl.when(step == blocks)
    def _():
        for copy in late:
            copy.wait()
        dgain = jnp.zeros(dgain_ref.shape, jnp.float32)
        dshift, dobias = (dgain, dgain)
        copies = []
        for index, part in enumerate(chunks):
            hidden = hidden_buf[part, :]
            if forward:
                final = hidden + (state_ref[part, :] + pbias_ref[...])
                final_ref[part, :] = final.astype(jnp.bfloat16)
            normed, scale = norm_parts(hidden)
            grad_norm = acc_ref[part, :]
            dgain = dgain + jnp.sum(grad_norm * normed, axis=0, keepdims=True)
            dshift = dshift + jnp.sum(grad_norm, axis=0, keepdims=True)
            dhid = grad_ref[part, :].astype(jnp.float32) + norm_back(
                normed, scale, gain_ref[...], grad_norm
            )
            hidden_buf[part, :] = dhid
            copies.append(
                pltpu.make_async_copy(
                    hidden_buf.at[part, :], dhid_ref.at[part, :], sems.at[2 + index]
                )
            )
            copies[-1].start()
            low_dhid = dhid.astype(jnp.bfloat16)
            low_ref[part, :] = low_dhid
            dobias = dobias + jnp.sum(low_dhid.astype(jnp.float32), axis=0, keepdims=True)
        dgain_ref[...] = dgain + earlier[9][...] if more else dgain
        dshift_ref[...] = dshift + earlier[10][...] if more else dshift
        dobias_ref[...] = dobias + earlier[6][...] if more else dobias
        dout = transposed_dot(att_buf[...], low_ref[...])
        store_halves(core, dout, out_mine, out_theirs, earlier[4:6] if more else None)
        for copy in copies:
            copy.wait()


def mlp_backward(core, grad, hidden, normed, att, expanded, mlp, gain, earlier=None, biases=None):
    rows, width = hidden.shape
    blocks, block = (4, width)
    shape = pltpu.HBM
    groups = DEVICE_GROUPS
    each = width // groups
    fc_half = shape((groups, blocks, each, width // 2), jnp.bfloat16)
    proj_half = shape((blocks * width, width // 2), jnp.bfloat16)
    out_half = shape((groups, each, width // 2), jnp.bfloat16)
    row = shape((1, width), jnp.float32)
    outs = (
        shape((rows, width), jnp.float32),
        fc_half,
        fc_half,
        proj_half,
        proj_half,
        out_half,
        out_half,
        row,
        shape((blocks, 1, block), jnp.float32),
        row,
        row,
        row,
    )
    fc_spec = pl.BlockSpec((groups, None, each, width // 2), lambda i: (0, jnp.minimum(i, 3), 0, 0))
    proj_spec = pl.BlockSpec((width, width // 2), lambda i: (jnp.minimum(i, 3), 0))
    out_spec = pl.BlockSpec((groups, each, width // 2), lambda i: (0, 0, 0))
    bias = pl.BlockSpec((1, 1, block), lambda i: (jnp.minimum(i, 3), 0, 0))
    vector = pl.BlockSpec((1, width), lambda i: (0, 0))
    inputs = [grad, hidden, normed, att]
    raw = pl.BlockSpec(memory_space=pltpu.HBM)
    specs = [whole(grad), raw, whole(normed), raw]
    out_specs = [raw]
    scratch = []
    if biases is None:
        inputs.append(expanded)
        specs.append(pl.BlockSpec((rows, block), lambda i: (0, jnp.minimum(i, 3))))
    else:
        inputs += list(biases)
        specs += [pl.BlockSpec((1, block), lambda i: (0, jnp.minimum(i, 3))), whole(biases[1])]
        outs = (shape((rows, width), jnp.bfloat16), *outs)
        out_specs = [pl.BlockSpec((rows, width), lambda i: (0, 0)), raw]
        scratch = [pltpu.VMEM((rows, width), jnp.float32)]
    inputs += [mlp, mlp, gain]
    specs += [FC_BLOCK, PROJ_BLOCK, whole(gain)]
    summed = [fc_spec, fc_spec, proj_spec, proj_spec, out_spec, out_spec, vector, bias]
    summed += [vector, vector, vector]
    if earlier is not None:
        inputs += list(earlier)
        specs += summed
    return pl.pallas_call(
        functools.partial(mlp_backward_kernel, earlier is not None, biases is not None),
        grid=(blocks + 1,),
        out_shape=outs,
        in_specs=[SMEM] + specs,
        out_specs=out_specs + summed,
        scratch_shapes=[
            pltpu.VMEM((rows, width), jnp.bfloat16),
            pltpu.VMEM((width, rows), jnp.bfloat16),
            pltpu.VMEM((rows, width), jnp.float32),
            pltpu.VMEM((rows, block), jnp.bfloat16),
            pltpu.VMEM((rows, block), jnp.bfloat16),
            pltpu.VMEM((rows, width), jnp.float32),
            pltpu.VMEM((rows, width), jnp.bfloat16),
            pltpu.SemaphoreType.DMA((2 + rows // 256,)),
            *scratch,
        ],
        compiler_params=params(54 << 20),
        cost_estimate=cost(8 * rows * width * blocks * block, rows * blocks * block, *inputs, *outs),
        name="mlp_backward",
    )(core, *in_hbm(inputs))


def input_gradient(
    dhid_ref, state_ref, gmix_ref, weight_ref, gain_ref, earlier, grad_ref, dgain_ref, dshift_ref
):
    step = pl.program_id(0)
    grad_norm = dot_transposed(gmix_ref[:, :FEATURES], weight_ref[0])
    for part in range(1, 3):
        grad_norm = grad_norm + dot_transposed(
            gmix_ref[:, part * FEATURES : (part + 1) * FEATURES], weight_ref[part]
        )
    normed, scale = norm_parts(state_ref[...].astype(jnp.float32))
    dgain = jnp.sum(grad_norm * normed, axis=0, keepdims=True)
    dshift = jnp.sum(grad_norm, axis=0, keepdims=True)

    @pl.when(step == 0)
    def _():
        dgain_ref[...] = dgain if earlier is None else dgain + earlier[0][...]
        dshift_ref[...] = dshift if earlier is None else dshift + earlier[1][...]

    @pl.when(step > 0)
    def _():
        dgain_ref[...] += dgain
        dshift_ref[...] += dshift

    grad = dhid_ref[...] + norm_back(normed, scale, gain_ref[...], grad_norm)
    grad_ref[...] = grad.astype(grad_ref.dtype)


def attention_backward_kernel(
    docs,
    back,
    micro,
    lengths_ref,
    dhid_ref,
    att_ref,
    mixed_ref,
    lse_ref,
    out_ref,
    *rest,
):
    if micro is None:
        micro = pl.program_id(0)
        weight_ref, state_ref, gain_ref, gmix_ref, grad_ref, dgain_ref, dshift_ref, *rest = rest
        *rest, weight_buf, sem = rest
        late = pltpu.make_async_copy(weight_ref.at[pl.ds(0, 3)], weight_buf, sem.at[0])

        @pl.when(micro == 0)
        def _():
            late.start()

        def finish():
            @pl.when(micro == 0)
            def _():
                late.wait()

            input_gradient(
                dhid_ref, state_ref, gmix_ref, weight_buf, gain_ref, None,
                grad_ref, dgain_ref, dshift_ref,
            )

    else:
        gmix_ref, *rest = rest
        finish = None
    datt_ref, bias_ref, delta_ref, dq_ref = rest
    count = dhid_ref.shape[0]
    low_grad = dhid_ref[...].astype(jnp.bfloat16)
    datt = dot_transposed(low_grad, out_ref[0]).astype(jnp.bfloat16)
    datt_ref[...] = datt
    product = datt.astype(jnp.float32) * att_ref[...].astype(jnp.float32)
    high = product.astype(jnp.bfloat16)
    rest_low = (product - high.astype(jnp.float32)).astype(jnp.bfloat16)
    feature = lax.broadcasted_iota(jnp.int32, (16, FEATURES), 1)
    head = lax.broadcasted_iota(jnp.int32, (16, FEATURES), 0)
    chosen = ((feature >= head * HD) & (feature < (head + 1) * HD)).astype(jnp.bfloat16)
    delta = dot_transposed(chosen, high) + dot_transposed(chosen, rest_low)
    for index in range(H):
        delta_ref[index] = delta[index : index + 1]
    bias_ref[...] = allowed_bias(count, [lengths_ref[micro, d] for d in range(docs)], docs, 1)

    def one_group(group, carry):
        lanes = pl.multiple_of(group * LANES, LANES)
        dq_ref[...] = jnp.zeros_like(dq_ref)
        for block in range(count // BLOCK):
            keys = slice(block * BLOCK, (block + 1) * BLOCK)
            rows = slice(block * BLOCK, min(count, (block + 1 + back) * BLOCK))
            key = head_split(mixed_ref[keys, pl.ds(FEATURES + lanes, LANES)])
            value = head_split(mixed_ref[keys, pl.ds(2 * FEATURES + lanes, LANES)])
            query = mixed_ref[rows, pl.ds(lanes, LANES)]
            datt_group = datt_ref[rows, pl.ds(lanes, LANES)]
            scores = dot_transposed(key, query)
            dprobs = dot_transposed(value, datt_group)
            bias = bias_ref[keys, rows]
            probs_low, dscores_low = ([], [])
            for h in range(GROUP):
                part = slice(h * BLOCK, (h + 1) * BLOCK)
                lse = lse_ref[GROUP * group + h, :, rows]
                delta = delta_ref[GROUP * group + h, :, rows]
                probs = jnp.exp((scores[part] * 0.125 + bias) - lse)
                dscores = probs * (dprobs[part] - delta)
                probs_low.append(probs.astype(jnp.bfloat16))
                dscores_low.append(dscores.astype(jnp.bfloat16))
            probs_low = jnp.concatenate(probs_low, axis=0)
            dscores_low = jnp.concatenate(dscores_low, axis=0)
            dvalue = head_join(dot(probs_low, datt_group))
            dkey = head_join(dot(dscores_low, query)) * 0.125
            dq_ref[rows, :] += transposed_dot(dscores_low, key)
            gmix_ref[keys, pl.ds(FEATURES + lanes, LANES)] = dkey.astype(jnp.bfloat16)
            gmix_ref[keys, pl.ds(2 * FEATURES + lanes, LANES)] = dvalue.astype(jnp.bfloat16)
        gmix_ref[:, pl.ds(lanes, LANES)] = (dq_ref[...] * 0.125).astype(jnp.bfloat16)
        return carry

    lax.fori_loop(0, H // GROUP, one_group, 0, unroll=H // GROUP)
    if finish is not None:
        finish()


def attention_backward(micro, lengths, dhid, count, back, att, mixed, lse, weight):
    width = dhid.shape[1]
    docs = lengths.shape[1]
    outs = jax.ShapeDtypeStruct((count, 3 * width), jnp.bfloat16)
    inputs = [dhid, att, mixed, lse, weight]
    return pl.pallas_call(
        functools.partial(attention_backward_kernel, docs, back, micro),
        grid=(1,),
        out_shape=outs,
        in_specs=[
            SMEM,
            pl.BlockSpec((count, width), lambda i: (micro, 0)),
            pl.BlockSpec((count, width), lambda i: (micro, 0)),
            pl.BlockSpec((count, 3 * width), lambda i: (micro, 0)),
            pl.BlockSpec((H, 1, count), lambda i: (micro, 0, 0)),
            pl.BlockSpec((1, width, width), lambda i: (3, 0, 0)),
        ],
        out_specs=pl.BlockSpec((count, 3 * width), lambda i: (0, 0)),
        scratch_shapes=[
            pltpu.VMEM((count, width), jnp.bfloat16),
            pltpu.VMEM((count, count), jnp.float32),
            pltpu.VMEM((H, 1, count), jnp.float32),
            pltpu.VMEM((count, LANES), jnp.float32),
        ],
        compiler_params=params(),
        cost_estimate=cost(
            2 * count * width * width + 10 * count * count * width, count * count * H, outs, outs
        ),
        name="attention_backward",
    )(lengths, *in_hbm(inputs))


def attention_backward_all(lengths, dhid, count, back, att, mixed, lse, weight, state, gain):
    rows, width = dhid.shape
    micro, docs = lengths.shape
    vector = pl.BlockSpec((1, width), lambda i: (0, 0))
    outs = (
        pltpu.HBM((rows, 3 * width), jnp.bfloat16),
        pltpu.HBM((rows, width), jnp.float32),
        jax.ShapeDtypeStruct((1, width), jnp.float32),
        jax.ShapeDtypeStruct((1, width), jnp.float32),
    )
    inputs = [dhid, att, mixed, lse, weight, weight, state, gain]
    return pl.pallas_call(
        functools.partial(attention_backward_kernel, docs, back, None),
        grid=(micro,),
        out_shape=outs,
        in_specs=[
            SMEM,
            rows_of(count, width),
            rows_of(count, width),
            rows_of(count, 3 * width),
            pl.BlockSpec((H, 1, count), lambda i: (i, 0, 0)),
            pl.BlockSpec((1, width, width), lambda i: (3, 0, 0), pipeline_mode=pl.Buffered(1)),
            pl.BlockSpec(memory_space=pltpu.HBM),
            rows_of(count, width),
            whole(gain),
        ],
        out_specs=[rows_of(count, 3 * width), rows_of(count, width), vector, vector],
        scratch_shapes=[
            pltpu.VMEM((count, width), jnp.bfloat16),
            pltpu.VMEM((count, count), jnp.float32),
            pltpu.VMEM((H, 1, count), jnp.float32),
            pltpu.VMEM((count, LANES), jnp.float32),
            pltpu.VMEM((3, width, width), jnp.bfloat16),
            pltpu.SemaphoreType.DMA((1,)),
        ],
        compiler_params=params(44 << 20),
        cost_estimate=cost(
            8 * rows * width * width + 10 * rows * count * width, rows * count * H, *inputs, *outs
        ),
        name="attention_backward_all",
    )(lengths, *in_hbm(inputs))


def attention_terms_kernel(more, micro, core_ref, normed_ref, *rest):
    gmix_refs, rest = (rest[:micro], rest[micro:])
    earlier = rest[:3] if more else (None,) * 3
    if more:
        rest = rest[3:]
    mine_ref, theirs_ref, dbias_ref = rest
    core = core_ref[0]
    terms, dbias, start = (0.0, 0.0, 0)
    for gmix_ref in gmix_refs:
        right = gmix_ref[...]
        stop = start + right.shape[0]
        terms = terms + transposed_dot(normed_ref[start:stop], right)
        dbias = dbias + jnp.sum(right.astype(jnp.float32), axis=0, keepdims=True)
        start = stop
    dbias_ref[0] = dbias + earlier[2][0] if more else dbias
    store_halves(core, terms, mine_ref, theirs_ref, earlier[:2] if more else None)


def attention_terms(core, normed, gmix, earlier=None):
    rows, width = normed.shape
    groups = DEVICE_GROUPS
    each = width // groups
    shape = pltpu.HBM
    half = shape((groups, 3, each, width // 2), jnp.bfloat16)
    outs = (half, half, shape((3, 1, width), jnp.float32))
    halves = pl.BlockSpec((groups, None, each, width // 2), lambda i: (0, i, 0, 0))
    summed = [halves, halves, pl.BlockSpec((1, 1, width), lambda i: (i, 0, 0))]
    inputs = [normed, *gmix]
    specs = [whole(normed)] + [
        pl.BlockSpec((part.shape[0], width), lambda i: (0, i)) for part in gmix
    ]
    if earlier is not None:
        inputs += list(earlier)
        specs += summed
    return pl.pallas_call(
        functools.partial(attention_terms_kernel, earlier is not None, len(gmix)),
        grid=(3,),
        out_shape=outs,
        in_specs=[SMEM] + specs,
        out_specs=summed,
        compiler_params=params(),
        cost_estimate=cost(6 * rows * width * width, 0, *inputs, *outs),
        name="attention_terms",
    )(core, *in_hbm(inputs[:1]), *gmix, *in_hbm(inputs[1 + len(gmix) :]))


def attention_input_kernel(more, micro, dhid_ref, state_ref, weight_ref, gain_ref, *rest):
    gmix_refs, rest = (rest[:micro], rest[micro:])
    earlier = rest[:2] if more else None
    if more:
        rest = rest[2:]
    grad_ref, dgain_ref, dshift_ref, gmix_ref = rest
    each = pl.num_programs(0) // micro
    for index, part_ref in enumerate(gmix_refs):

        @pl.when(pl.program_id(0) // each == index)
        def _(part_ref=part_ref):
            gmix_ref[...] = part_ref[...]

    input_gradient(
        dhid_ref, state_ref, gmix_ref, weight_ref, gain_ref, earlier, grad_ref, dgain_ref, dshift_ref
    )


def attention_input(dhid, state, gmix, weight, gain, kind, earlier=None, chunk=256):
    rows, width = dhid.shape
    shape = jax.ShapeDtypeStruct
    vector = pl.BlockSpec((1, width), lambda i: (0, 0))
    outs = (shape((rows, width), kind), shape((1, width), jnp.float32), shape((1, width), jnp.float32))
    inputs = [dhid, state, weight, gain, *gmix]
    each = rows // chunk // len(gmix)
    specs = [
        rows_of(chunk, width),
        rows_of(chunk, width),
        pl.BlockSpec((3, width, width), lambda i: (0, 0, 0), pipeline_mode=pl.Buffered(1)),
        whole(gain),
    ]
    for index in range(len(gmix)):
        specs.append(
            pl.BlockSpec(
                (chunk, 3 * width),
                lambda i, index=index: (jnp.clip(i - index * each, 0, each - 1), 0),
            )
        )
    if earlier is not None:
        inputs += list(earlier)
        specs += [vector, vector]
    return pl.pallas_call(
        functools.partial(attention_input_kernel, earlier is not None, len(gmix)),
        grid=(rows // chunk,),
        out_shape=outs,
        in_specs=specs,
        out_specs=[rows_of(chunk, width), vector, vector],
        scratch_shapes=[pltpu.VMEM((chunk, 3 * width), jnp.bfloat16)],
        compiler_params=params(),
        cost_estimate=cost(6 * rows * width * width, 0, *inputs, *outs),
        name="attention_input",
    )(*in_hbm(inputs[:4]), *gmix, *in_hbm(inputs[4 + len(gmix) :]))


def place_small_kernel(sizes, me_ref, *refs):
    smalls, outs = (refs[:4], refs[4:])
    dp = me_ref[0] // 2
    slot = lax.broadcasted_iota(jnp.int32, (16, 1), 0)
    owner = ((slot % 4) * 4 + (slot // 8) * 2 + slot // 4 % 2) ^ dp
    for index, (size, out_ref) in enumerate(zip(sizes, outs)):
        width = 16 * size
        lane = lax.broadcasted_iota(jnp.int32, (256, width), 0)
        column = lax.broadcasted_iota(jnp.int32, (256, width), 1)
        spread = (column % size == lane).astype(jnp.bfloat16)
        rows = jnp.concatenate([ref[z, index : index + 1] for ref in smalls for z in range(4)], axis=0)
        spread_rows = dot(rows, spread)
        column = lax.broadcasted_iota(jnp.int32, (1, width), 1)
        out_ref[...] = jnp.sum(
            jnp.where(column // size == owner, spread_rows, 0.0), axis=0, keepdims=True
        )


def place_small(me, smalls, sizes):
    return pl.pallas_call(
        functools.partial(place_small_kernel, sizes),
        out_shape=[jax.ShapeDtypeStruct((1, 16 * size), jnp.float32) for size in sizes],
        in_specs=[SMEM] + [pl.BlockSpec(memory_space=pltpu.VMEM)] * len(smalls),
        out_specs=[pl.BlockSpec(memory_space=pltpu.VMEM)] * len(sizes),
        name="place_small",
    )(me, *smalls)


def swap(value, bits):
    return lax.ppermute(value, BOTH, [(i, i ^ bits) for i in range(32)])


CORE, X, Y, Z1, Z2, Z3 = (1, 2, 4, 8, 16, 24)


def place_kernel(slots, me_ref, *refs):
    sources, (out, sems) = (refs[: len(slots)], refs[len(slots) :])
    me = me_ref[0]
    copies = []
    for source, rels in zip(sources, slots):
        for inner, rel in enumerate(rels):
            copies.append(
                pltpu.make_async_copy(
                    source.at[inner], out.at[:, rel ^ me], sems.at[len(copies)]
                )
            )
    for copy in copies:
        copy.start()
    for copy in copies:
        copy.wait()


def place(me, sources, slots):
    placed = pl.pallas_call(
        functools.partial(place_kernel, slots),
        out_shape=jax.ShapeDtypeStruct((4, 32, 24, FEATURES), jnp.bfloat16),
        in_specs=[SMEM] + [pl.BlockSpec(memory_space=pl.ANY)] * len(sources),
        out_specs=pl.BlockSpec(memory_space=pltpu.VMEM),
        scratch_shapes=[pltpu.SemaphoreType.DMA((32,))],
        name="place",
    )(me, *sources)
    return placed.reshape(4, FEATURES, FEATURES)


def after(values, *others):
    return lax.optimization_barrier((values, others))[0]


def gather_first(piece, small, me):
    base = (0, Z1, Z2, Z3)
    pieces = lax.optimization_barrier(
        [piece] + [swap(piece, bits) for bits in base[1:]]
        + [small] + [swap(small, bits) for bits in base[1:]]
    )
    four, small = (jnp.concatenate(pieces[:4]), jnp.concatenate(pieces[4:]))
    four_x, four_y, four_core, small_x, small_y = lax.optimization_barrier(
        (swap(four, X), swap(four, Y), swap(four, CORE), swap(small, X), swap(small, Y))
    )
    near_xy, far_xy, x_core, y_core, small_xy = lax.optimization_barrier(
        (
            swap(four_y[:2], X), swap(four_x[2:], Y), swap(four_x, CORE), swap(four_y, CORE),
            swap(small_y, X),
        )
    )
    parts = [four, four_x, four_y, near_xy, far_xy]
    parts += [four_core, x_core, y_core, swap(near_xy, CORE), swap(far_xy, CORE)]
    slots = [base] + [tuple(rel ^ bits for rel in base) for bits in (X, Y)]
    slots += [(X ^ Y, X ^ Y ^ Z1), (X ^ Y ^ Z2, X ^ Y ^ Z3)]
    slots += [tuple(rel ^ CORE for rel in rels) for rels in slots]
    return (place(me, parts, slots), (small, small_x, small_y, small_xy))


def pick(array, axis, index):
    return lax.dynamic_index_in_dim(array, index, axis, keepdims=False)


def low(value):
    return value.astype(jnp.bfloat16)


def wide(value):
    return value.astype(jnp.float32)


def add(*terms):
    total = wide(terms[0])
    for term in terms[1:]:
        total = total + wide(term)
    return total


def device_at(z_pair, z_low, y, x):
    return z_pair * 8 + z_low * 4 + y * 2 + x


def total(*terms):
    result = terms[0].astype(jnp.float32)
    for term in terms[1:]:
        result = result + term.astype(jnp.float32)
    return result


def first_sums_kernel(views, spot_ref, *refs):
    mine, got, alone = (refs[:views], refs[views : 2 * views], refs[2 * views : -4])
    near_sent, far_sent, near_kept, far_kept = refs[-4:]
    z_pair, y, x = (spot_ref[0], spot_ref[2], spot_ref[3])
    for low_z in range(2):
        for other in range(2):
            for out, device in (
                (near_sent, device_at(z_pair, low_z, other, 1 - x)),
                (far_sent, device_at(1 - z_pair, low_z, 1 - y, other)),
                (near_kept, device_at(z_pair, low_z, other, x)),
                (far_kept, device_at(1 - z_pair, low_z, y, other)),
            ):
                start = 0
                for left, right in zip(mine, got):
                    count = left.shape[1]
                    out[low_z, other, start : start + count] = total(
                        left[device], right[device]
                    ).astype(jnp.bfloat16)
                    start += count
                for only in alone:
                    out[low_z, other, start:] = only[device]


def second_sums_kernel(spot_ref, near, far, near_in, far_in, *outs):
    near_sent, far_sent, near_kept, far_kept = outs
    y, x = (spot_ref[2], spot_ref[3])
    for low_z in range(2):
        for out, kept, got, index in (
            (near_sent, near, near_in, 1 - y),
            (far_sent, far, far_in, 1 - x),
            (near_kept, near, near_in, y),
            (far_kept, far, far_in, x),
        ):
            out[low_z] = total(kept[low_z, index], got[low_z, index]).astype(jnp.bfloat16)


def third_sums_kernel(spot_ref, near, far, near_in, far_in, sent, kept):
    low_z = spot_ref[1]
    for index, (left, right) in enumerate(((near, near_in), (far, far_in))):
        sent[index] = total(left[1 - low_z], right[1 - low_z]).astype(jnp.bfloat16)
        kept[index] = total(left[low_z], right[low_z])


def assemble_kernel(layouts, core_ref, half_ref, other_ref, *outs):
    if len(outs) > len(layouts):
        outs[-1][...] = half_ref[-16:] + other_ref[-16:]
    core = core_ref[0]
    half, other = (half_ref[...], other_ref[...])
    left = jnp.where(core == 0, half, other)
    right = jnp.where(core == 0, other, half)
    start, wide_half = (0, half.shape[1])
    for (blocks, rows), out in zip(layouts, outs):
        for block in range(blocks):
            part = slice(start, start + rows)
            column = 2 * block * wide_half
            out[:, column : column + wide_half] = left[part]
            out[:, column + wide_half : column + 2 * wide_half] = right[part]
            start += rows


SMALL_ROWS = ((48, 48, 144, 48, 48, 48), (192, 48))


def pack_small_kernel(unused_ref, *refs):
    *vectors, out = refs
    width = out.shape[2]
    device = lax.broadcasted_iota(jnp.int32, (16, 1), 0)
    rows, vectors = ([], iter(vectors))
    for sizes in SMALL_ROWS:
        row, start = (jnp.zeros((16, width), jnp.float32), 0)
        for size, ref in zip(sizes, vectors):
            if len(ref.shape) == 2:
                vector = ref[...]
            else:
                vector = jnp.concatenate([ref[i] for i in range(ref.shape[0])], axis=1)
            column = lax.broadcasted_iota(jnp.int32, (1, 16 * size), 1)
            parts = jnp.where(column // size == device, vector, 0.0).astype(jnp.bfloat16)
            place_in = lax.broadcasted_iota(jnp.int32, (16 * size, width), 0) % size + start
            lane = lax.broadcasted_iota(jnp.int32, (16 * size, width), 1)
            row = row + dot(parts, (place_in == lane).astype(jnp.bfloat16))
            start += size
        rows.append(row)
    line = lax.broadcasted_iota(jnp.int32, out.shape[1:], 0)
    for d in range(16):
        first, second = (rows[0][d : d + 1], rows[1][d : d + 1])
        value = jnp.where(line == 0, first, jnp.where(line == 1, second, 0.0))
        out[d] = value.astype(jnp.bfloat16)


def in_vmem(kernel, name, outs, *args):
    vmem = pl.BlockSpec(memory_space=pltpu.VMEM)
    return pl.pallas_call(
        kernel,
        out_shape=outs,
        in_specs=[SMEM] + [vmem] * (len(args) - 1),
        out_specs=[vmem] * len(outs),
        compiler_params=params(),
        cost_estimate=cost(0, 0, *args, *outs),
        name=name,
    )(*args)


class Reduction:
    def __init__(self, spot, mine, theirs):
        self.spot = spot
        self.mine = list(mine)
        self.got = [swap(part, CORE) for part in theirs]
        self.alone = []
        self.width = self.mine[0].shape[2]

    def like(self, *lead, kind=jnp.bfloat16):
        count = sum(part.shape[1] for part in (*self.mine, *self.alone))
        return jax.ShapeDtypeStruct((*lead, count, self.width), kind)

    def first(self):
        near_sent, far_sent, *self.kept = in_vmem(
            functools.partial(first_sums_kernel, len(self.mine)),
            "first_sums",
            [self.like(2, 2)] * 4,
            self.spot,
            *self.mine,
            *self.got,
            *self.alone,
        )
        self.got = [swap(near_sent, X), swap(far_sent, Y)]
        return self.kept

    def second(self):
        near_sent, far_sent, *self.kept = in_vmem(
            second_sums_kernel, "second_sums", [self.like(2)] * 4, self.spot, *self.kept, *self.got
        )
        self.got = [swap(near_sent, Y), swap(far_sent, X)]
        return self.kept

    def third(self):
        sent, kept = in_vmem(
            third_sums_kernel,
            "third_sums",
            [self.like(2), self.like(2, kind=jnp.float32)],
            self.spot,
            *self.kept,
            *self.got,
        )
        self.kept, self.got = ([kept], [swap(sent, Z1)])
        return self.kept

    def fourth(self):
        (kept,), (got,) = (self.kept, self.got)
        far = low(kept[1] + wide(got[1]))
        self.kept, self.got = ([kept[0], got[0]], [swap(far, Z2)])
        return far

    def fifth(self):
        half = total(*self.kept, *self.got)
        self.kept, self.got = ([half], [swap(half, CORE)])

    def whole(self, core, layouts):
        outs = [
            jax.ShapeDtypeStruct((rows, 2 * self.width * blocks), jnp.float32)
            for blocks, rows in layouts
        ]
        if self.alone:
            outs.append(jax.ShapeDtypeStruct((16, self.width), jnp.float32))
        return in_vmem(
            functools.partial(assemble_kernel, layouts), "assemble", outs, core, *self.kept, *self.got
        )


def gather_all(weights, spot, me):
    gain_a, shift_a, qkv, qbias, out, obias, gain_m, shift_m, fc, fbias, proj, pbias = weights
    core = spot[4]

    def half(weight):
        part = lax.dynamic_slice_in_dim(weight, core * 24, 24, 0)
        return jnp.transpose(part.reshape(24, -1, FEATURES), (1, 0, 2))

    columns = [
        lax.dynamic_slice_in_dim(fc, core * 2 * FEATURES + part * FEATURES, FEATURES, 1)
        for part in range(2)
    ]
    across = lax.dynamic_slice_in_dim(proj, core * 96, 96, 0).reshape(2, 48, FEATURES)
    mlp = lax.all_gather(jnp.stack([*columns, across[0], across[1]]), BOTH)
    mlp = mlp.reshape(16, 2, 4, 48, FEATURES)
    vectors = [gain_a, shift_a, qbias, obias, gain_m, shift_m, fbias, pbias]
    sizes = tuple(vector.shape[0] for vector in vectors)
    small = jnp.stack([jnp.pad(v, (0, 256 - size)) for v, size in zip(vectors, sizes)])
    first, smalls = gather_first(jnp.concatenate([half(qkv), half(out)])[None], small[None], me)
    return (first, mlp, *place_small(me, smalls, sizes))


def gather_plain(weights):
    whole_ones = [lax.all_gather(weight, "dp", axis=0, tiled=True) for weight in weights]
    gain_a, shift_a, qkv, qbias, out, obias, gain_m, shift_m, fc, fbias, proj, pbias = whole_ones

    def blocks(weight):
        return jnp.transpose(weight.reshape(FEATURES, -1, FEATURES), (1, 0, 2))

    rows = [
        wide(v).reshape(1, -1)
        for v in (gain_a, shift_a, qbias, obias, gain_m, shift_m, fbias, pbias)
    ]
    first = jnp.concatenate([blocks(qkv), blocks(out)])
    fc = blocks(fc).reshape(2, 2, 16, 48, FEATURES)
    fc = jnp.transpose(fc, (2, 0, 1, 3, 4))
    mlp = jnp.concatenate([fc, proj.reshape(16, 2, 2, 48, FEATURES)], axis=2)
    return (first, mlp, *rows)


def reduce_plain(matrices, small):
    def joined(left, right):
        both = jnp.concatenate([left, right], axis=-1)
        if both.ndim == 4:
            both = jnp.transpose(both, (0, 2, 1, 3)).reshape(FEATURES, -1)
        return both.reshape(-1, both.shape[-1])

    qkv, out, fc, proj = [joined(*pair) for pair in matrices]
    gain_a, shift_a, qbias, obias, gain_m, shift_m, fbias, pbias = [v.reshape(-1) for v in small]
    values = (
        gain_a, shift_a, qkv, qbias, out, obias, gain_m, shift_m, fc, fbias, proj, pbias
    )
    return tuple(
        wide(lax.psum(low(lax.psum_scatter(wide(v), "dp", scatter_dimension=0, tiled=True)), "rep"))
        for v in values
    )


def forward(tokens, lengths, count, back, weights):
    weight, mlp, gain_a, shift_a, qbias, obias, gain_m, shift_m, fbias, pbias = weights
    state, kept = (tokens, [])
    for use in range(USES):
        normed_a, mixed, att, lse, hidden, normed_m = attention_forward(
            lengths, state, count, back, gain_a, shift_a, weight, qbias, obias, gain_m, shift_m
        )
        expanded, after_mlp = (None, None)
        if use < USES - 1:
            expanded, after_mlp = mlp_forward(hidden, normed_m, mlp, fbias, pbias)
        kept.append((state, normed_a, mixed, att, lse, hidden, normed_m, expanded))
        state = after_mlp
    return kept


def shards(custom, tokens, doc_lengths, cotangent, *weights):
    micro, count, width = tokens.shape
    dp, core = (lax.axis_index("dp"), lax.axis_index("rep"))
    spot = (dp // 8, dp // 4 % 2, dp // 2 % 2, dp % 2, core)
    me = (dp * 2 + core).astype(jnp.int32).reshape(1)
    places = jnp.stack(spot).astype(jnp.int32)
    side = core.astype(jnp.int32).reshape(1) if custom else jnp.zeros((1,), jnp.int32)
    back = -(-(LONGEST - 1) // BLOCK)
    lengths = doc_lengths.reshape(micro, doc_lengths.shape[-1])
    whole_ones = gather_all(weights, spot, me) if custom else gather_plain(weights)
    kept = forward(tokens.reshape(micro * count, width), lengths, count, back, whole_ones)
    weight, mlp, gain_a, gain_m = (whole_ones[0], whole_ones[1], whole_ones[2], whole_ones[6])
    grad, mlp_terms, terms, norm = (cotangent.reshape(micro * count, width), None, None, None)
    delayed = None
    for use in range(USES - 1, -1, -1):
        before, normed_a, mixed, att, lse, hidden, normed_m, expanded = kept[use]
        last = use == USES - 1
        dhid, *mlp_terms = mlp_backward(
            side, grad, hidden, normed_m, att, expanded, mlp, gain_m, mlp_terms,
            whole_ones[-2:] if last else None,
        )
        if last:
            state, (dhid, *mlp_terms) = (dhid, mlp_terms)
        sending = custom and use == 0
        if delayed is not None:
            terms = delayed()
        if sending:
            fc_mine, fc_theirs, proj_mine, proj_theirs, out_mine, out_theirs = [
                part.reshape(16, -1, part.shape[-1]) for part in mlp_terms[:6]
            ]
            sums = Reduction(
                places, (fc_mine, proj_mine, out_mine), (fc_theirs, proj_theirs, out_theirs)
            )
            sums.got, terms = lax.optimization_barrier((sums.got, terms))
            dhid = after(dhid, sums.first())
        if use:
            gmix, grad, *norm = attention_backward_all(
                lengths, dhid, count, back, att, mixed, lse, weight, before, gain_a
            )
            delayed = functools.partial(attention_terms, side, normed_a, in_hbm([gmix]))
            continue
        gmix = [
            attention_backward(index, lengths, dhid, count, back, att, mixed, lse, weight)
            for index in range(micro)
        ]
        terms = attention_terms(side, normed_a, gmix, terms)
        if sending:
            qkv_sums = Reduction(
                places, *[(part.reshape(16, -1, part.shape[-1]),) for part in terms[:2]]
            )
            sums.got, terms = lax.optimization_barrier((sums.got, terms))
            gmix = after(gmix, sums.second())
        grad, *norm = attention_input(dhid, before, gmix, weight, gain_a, jnp.bfloat16, norm)
        if sending:
            sums.got, qkv_sums.got = after((sums.got, qkv_sums.got), norm)
    small = (norm[0], norm[1], terms[2], mlp_terms[6], mlp_terms[9], mlp_terms[10])
    small += (mlp_terms[7], mlp_terms[8])
    if custom:
        packed = jax.ShapeDtypeStruct((16, 16, width // 2), jnp.bfloat16)
        qkv_sums.alone = in_vmem(pack_small_kernel, "pack_small", [packed], side, *small)
        sums.got = after(sums.got, qkv_sums.alone)
        qkv_sums.got = after(qkv_sums.got, sums.third())
        qkv_sums.first()
        qkv_sums.second()
        qkv_sums.got = after(qkv_sums.got, sums.fourth())
        qkv_sums.third()
        qkv_sums.fourth()
        sums.fifth()
        qkv_sums.fifth()
        fc, proj, out = sums.whole(side, ((4, 48), (1, 192), (1, 48)))
        qkv, small = qkv_sums.whole(side, ((3, 48),))
        parts = []
        for row, sizes in enumerate(SMALL_ROWS):
            start = 0
            for size in sizes:
                parts.append(small[row, start : start + size])
                start += size
        gain_a, shift_a, qbias, obias, gain_m, shift_m, fbias, pbias = parts
        final = (
            gain_a, shift_a, qkv, qbias, out, obias, gain_m, shift_m, fc, fbias, proj, pbias
        )
    else:
        matrices = (terms[:2], mlp_terms[4:6], mlp_terms[:2], mlp_terms[2:4])
        final = reduce_plain(matrices, small)
    return (state.reshape(tokens.shape), grad.reshape(tokens.shape), *final)


def solution(mesh):
    custom = mesh.shape["dp"] == 16 and mesh.shape["rep"] == 2
    placed = tuple(
        P("dp", None) if index in (2, 4, 8, 10) else P("dp") for index in range(12)
    )
    rows = P(None, BOTH, None)
    return jax.shard_map(
        functools.partial(shards, custom),
        mesh=mesh,
        in_specs=(rows, rows, rows, *placed),
        out_specs=(rows, rows, *placed),
        check_vma=False,
    )
```
